32 devices in a mesh: ctx: 16 (over z, y, core), tp: 2 (over x).
Axes of the slice: x: 2, y: 2, z: 4, core: 2. Of those that a mesh axis runs over, the one named last changes fastest.
Arguments:
- tokens: bfloat16 [4096, 1024], P('ctx'), may hold values from -6 to 6
- seq_ids: int32 [4096], P('ctx'), may hold values from 0 to 3, never falling along the last dimension, each value on 1 to 2048 neighbouring positions
- attention_norm_gain: float32 [1024], replicated, may hold values from 0.5 to 1.5
- qkv_weight: bfloat16 [1024, 3, 1024], P(None, None, 'tp'), may hold values from -1 to 1, as said below
- out_weight: bfloat16 [1024, 1024], P('tp'), may hold values from -1.5 to 1.5
- feedforward_norm_gain: float32 [1024], replicated, may hold values from 0.5 to 1.5
- mlp_in_weight: bfloat16 [1024, 2, 2624], P(None, None, 'tp'), may hold values from -0.1875 to 0.1875
- mlp_out_weight: bfloat16 [2624, 1024], P('tp'), may hold values from -0.125 to 0.125
- grad_out: bfloat16 [4096, 1024], P('ctx'), may hold values from -6 to 6
Outputs:
- output: bfloat16 [4096, 1024], P('ctx')
- grad_tokens: float32 [4096, 1024], P('ctx')
- grad_norm1_gain: float32 [1024], replicated
- grad_qkv_weight: float32 [1024, 3, 1024], P(None, None, 'tp')
- grad_out_weight: float32 [1024, 1024], P('tp')
- grad_norm2_gain: float32 [1024], replicated
- grad_mlp_in_weight: float32 [1024, 2, 2624], P(None, None, 'tp')
- grad_mlp_out_weight: float32 [2624, 1024], P('tp')
The draws below stay inside these ranges and needn't reach their ends.
Inputs may be any that keep to these rules, and one draw needn't show every extreme that they name: `seq_ids`: never falling along the tokens; every one of the 4 sequences has at least one token and one has exactly 2048. `qkv_weight`: A projection matrix with entries of order 1024^(-1/2).
All inputs are finite; a program needn't handle non-finite values.
Results may differ from the reference program's by a relative error of at most 0.025.
Values may be sent and summed in bfloat16 or wider, within the bound.
No kernel may reach another device: no remote copies, remote signals or barrier semaphores. Data moves between devices by JAX's collectives and lax.ppermute only.
A program may use at most 256 MiB of HBM per device.

```python
import math
import jax
import jax.numpy as jnp
import numpy as np
from jax import lax

D = 1024
HEADS = 16
HD = 64
FF = 2624
SEQS = 4
TOKENS = 4096


def draw_qkv_weight(key, part):
    first_key = jax.random.fold_in(key, 0)
    shape = (D, 3, HEADS * HD)
    spread = D ** (-0.5)
    return jnp.clip(jax.random.normal(first_key, shape, jnp.float32) * spread, -0.9, 0.9).astype(jnp.bfloat16)


def level_of(key, shape, pieces, least, top_value):
    gain = 1.0
    for axis_at, blocks in pieces:
        heights = jax.random.uniform(jax.random.fold_in(jax.random.fold_in(key, 6), axis_at), (blocks,), jnp.float32, least / len(pieces), top_value / len(pieces))
        gain = gain * jnp.repeat(jnp.exp(heights), shape[axis_at] // blocks).reshape((-1,) + (1,) * (len(shape) - 1 - axis_at))
    return gain


def profile(count, total, limit, slope):
    portions = [(1 << 20) // math.isqrt(standing ** slope) + 1 for standing in range(2, count + 1)]
    rest, given = total - limit - (count - 1), [1] * (count - 1)
    while rest > 0:
        candidates = [i for i in range(count - 1) if given[i] < limit]
        pool, left = sum([portions[i] for i in candidates]), rest
        for i in candidates:
            addition = min(limit - given[i], max(1, left * portions[i] // pool), rest)
            given[i] = given[i] + addition
            rest = rest - addition
    return np.array([limit] + given)


def uneven(rng, number_of, total, limit, lean):
    if number_of == 2:
        one = jax.random.randint(rng, (), max(1, total - limit), min(limit, total - 1) + 1)
        return jnp.stack([one, total - one])
    tallies = jnp.asarray(profile(number_of, total, limit, lean), jnp.int32)
    twos = (number_of - 1) // 2
    source_of, receiver = tallies[1:1 + 2 * twos:2], tallies[2:2 + 2 * twos:2]
    room = jnp.minimum(source_of - 1, limit - receiver)
    moved = jax.random.randint(jax.random.fold_in(rng, 1), (twos,), 0, 1 << 20) % (room + 1)
    tallies = tallies.at[1:1 + 2 * twos:2].set(source_of - moved).at[2:2 + 2 * twos:2].set(receiver + moved)
    return tallies[jax.random.permutation(jax.random.fold_in(rng, 2), number_of)]


def normal_values(rng, extent, scale, bound, cuts=(), kind=jnp.bfloat16):
    values = jax.random.normal(rng, extent, jnp.float32) * scale
    if len(cuts) > 0:
        values = level_of(rng, extent, cuts, -0.22, 0.18) * values
    return jnp.clip(values, min=-bound, max=bound).astype(kind)


def setup_inputs(seed: int = 0) -> dict:
    streams_of = jax.random.split(jax.random.key(seed), 10)
    tokens = normal_values(streams_of[0], (TOKENS, D), 1.0, 6.0, ((0, 16),))
    seq_ids = jnp.searchsorted(jnp.cumsum(uneven(streams_of[1], SEQS, TOKENS, TOKENS // 2, 1)), jnp.arange(TOKENS), side="right").astype(jnp.int32)
    attention_norm_gain = jnp.clip(1.0 + 0.1 * jax.random.normal(streams_of[2], (D,), jnp.float32), 0.5, 1.5)
    qkv_weight = draw_qkv_weight(jax.random.fold_in(streams_of[9], 71), 0)
    out_weight = normal_values(streams_of[4], (HEADS * HD, D), 16 ** -0.5, 1.5, ((0, 2),))
    feedforward_norm_gain = jnp.clip(1.0 + 0.1 * jax.random.normal(streams_of[5], (D,), jnp.float32), 0.5, 1.5)
    mlp_in_weight = normal_values(streams_of[6], (D, 2, FF), D ** -0.5, 0.1875, ((2, 2),))
    mlp_out_weight = normal_values(streams_of[7], (FF, D), FF ** -0.5, 0.125, ((0, 2),))
    grad_out = normal_values(streams_of[8], (TOKENS, D), 1.0, 6.0, ((0, 16),))
    return dict(tokens=tokens, seq_ids=seq_ids, attention_norm_gain=attention_norm_gain, qkv_weight=qkv_weight, out_weight=out_weight, feedforward_norm_gain=feedforward_norm_gain, mlp_in_weight=mlp_in_weight, mlp_out_weight=mlp_out_weight, grad_out=grad_out)


EPS = 1e-05
BASE = 160000.0
MASKED = -1e+30
ROOT_HALF = 0.7071067811865476
INV_ROOT_TWO_PI = 0.3989422804014327

def layer_normalize(values_in, norm_gain_vector):
    token_average = lax.optimization_barrier(jnp.mean(values_in, axis=-1, keepdims=True))
    centered_input = values_in - token_average
    inverse_deviation = lax.rsqrt(lax.optimization_barrier(jnp.mean(centered_input * centered_input, axis=-1, keepdims=True)) + EPS)
    standardized_input = centered_input * inverse_deviation
    return (standardized_input, inverse_deviation, standardized_input * norm_gain_vector)

def layer_normalize_backward(output_gradient, standardized_input, inverse_deviation, norm_gain_vector):
    normalized_gradient = output_gradient * norm_gain_vector
    correction_term = lax.optimization_barrier(jnp.mean(normalized_gradient, axis=-1, keepdims=True)) + standardized_input * lax.optimization_barrier(jnp.mean(normalized_gradient * standardized_input, axis=-1, keepdims=True))
    return (inverse_deviation * (normalized_gradient - correction_term), lax.optimization_barrier(jnp.sum(output_gradient * standardized_input, axis=0)))

def gelu_value(v):
    return v * 0.5 * (1.0 + lax.erf(v * ROOT_HALF))

def gelu_slope(v):
    return 0.5 * (1.0 + lax.erf(v * ROOT_HALF)) + v * jnp.exp(-0.5 * v * v) * INV_ROOT_TWO_PI

def rope_tables(positions, head_size):
    half = head_size // 2
    inverse = BASE ** (-(jnp.arange(half, dtype=jnp.float32) * (2.0 / head_size)))
    angle = positions.astype(jnp.float32)[:, None] * inverse[None, :]
    angle = jnp.concatenate([angle, angle], axis=-1)
    return (jnp.cos(angle), jnp.sin(angle))

def rotate(field, cosine, sine):
    half = field.shape[-1] // 2
    turned = jnp.concatenate([-field[..., half:], field[..., :half]], axis=-1)
    return field * cosine[:, None, :] + turned * sine[:, None, :]

def unrotate(grad, cosine, sine):
    half = grad.shape[-1] // 2
    lifted = grad * sine[:, None, :]
    back = jnp.concatenate([lifted[..., half:], -lifted[..., :half]], axis=-1)
    return grad * cosine[:, None, :] + back

def block_grads(q_rows, do_rows, lse_rows, delta_rows, seq_rows, k_rows, v_rows, seq_cols, scale):
    f32 = jnp.float32
    scores = jnp.einsum('qhd,khd->hqk', q_rows.astype(f32), k_rows.astype(f32)) * scale
    same = (seq_rows[:, None] == seq_cols[None, :])[None]
    probs = jnp.where(same, jnp.exp(scores - lse_rows.T[:, :, None]), 0.0)
    grad_v = jnp.einsum('hqk,qhd->khd', probs.astype(jnp.bfloat16).astype(f32), do_rows.astype(f32))
    grad_p = jnp.einsum('qhd,khd->hqk', do_rows.astype(f32), v_rows.astype(f32))
    grad_s = (probs * (grad_p - delta_rows.T[:, :, None])).astype(jnp.bfloat16).astype(f32)
    grad_q = jnp.einsum('hqk,khd->qhd', grad_s, k_rows.astype(f32)) * scale
    grad_k = jnp.einsum('hqk,qhd->khd', grad_s, q_rows.astype(f32)) * scale
    return (grad_q, grad_k, grad_v)

def reference(tokens, seq_ids, attention_norm_gain, qkv_weight, out_weight, feedforward_norm_gain, mlp_in_weight, mlp_out_weight, grad_out):
    f32 = jnp.float32
    bf16 = jnp.bfloat16
    ntok, width = tokens.shape
    cols = qkv_weight.shape[2]
    nheads = cols // HD
    hidden_units = mlp_in_weight.shape[2]
    scale = 1.0 / math.sqrt(HD)
    block = math.gcd(ntok, 512)
    nblocks = ntok // block
    input_tokens = tokens.astype(f32)
    attention_standardized, attention_inverse_deviation, attention_normed_input = layer_normalize(input_tokens, attention_norm_gain)
    first = attention_normed_input.astype(bf16)
    qkv_flat = qkv_weight.reshape(width, 3 * cols)
    proj = jnp.dot(first, qkv_flat, preferred_element_type=f32).reshape(ntok, 3, nheads, HD)
    positions = jnp.arange(ntok, dtype=jnp.int32)
    cosine, sine = rope_tables(positions, HD)
    query = rotate(proj[:, 0], cosine, sine).astype(bf16)
    keys = rotate(proj[:, 1], cosine, sine).astype(bf16)
    values = proj[:, 2].astype(bf16)

    def forward_block(index):
        start = (index * block).astype(jnp.int32)
        q_rows = lax.dynamic_slice_in_dim(query, start, block, 0)
        s_rows = lax.dynamic_slice_in_dim(seq_ids, start, block, 0)
        scores = jnp.einsum('qhd,khd->hqk', q_rows.astype(f32), keys.astype(f32)) * scale
        same = (s_rows[:, None] == seq_ids[None, :])[None]
        top = lax.optimization_barrier(jnp.max(jnp.where(same, scores, MASKED), axis=-1))
        probs = jnp.where(same, jnp.exp(scores - top[..., None]), 0.0)
        den = lax.optimization_barrier(jnp.sum(probs, axis=-1))
        acc = jnp.einsum('hqk,khd->hqd', probs.astype(bf16).astype(f32), values.astype(f32))
        result = (acc / den[..., None]).transpose(1, 0, 2).astype(bf16)
        return (result, (top + jnp.log(den)).T)
    attended, lse = lax.map(forward_block, jnp.arange(nblocks, dtype=jnp.int32))
    attended = attended.reshape(ntok, nheads, HD)
    lse = lse.reshape(ntok, nheads)
    attended_flat = attended.reshape(ntok, cols)
    residual_middle = input_tokens + jnp.dot(attended_flat, out_weight, preferred_element_type=f32)
    feedforward_standardized, feedforward_inverse_deviation, feedforward_normed_input = layer_normalize(residual_middle, feedforward_norm_gain)
    second = feedforward_normed_input.astype(bf16)
    in_flat = mlp_in_weight.reshape(width, 2 * hidden_units)
    mixed = jnp.dot(second, in_flat, preferred_element_type=f32).reshape(ntok, 2, hidden_units)
    act_in = mixed[:, 0]
    gate = mixed[:, 1]
    hidden = (gelu_value(act_in) * gate).astype(bf16)
    output = (residual_middle + jnp.dot(hidden, mlp_out_weight, preferred_element_type=f32)).astype(bf16)
    upstream = grad_out.astype(f32)
    grad_w_out = jnp.dot(hidden.T, grad_out, preferred_element_type=f32)
    grad_hidden = jnp.dot(grad_out, mlp_out_weight.T, preferred_element_type=f32)
    grad_mixed = jnp.stack([grad_hidden * gate * gelu_slope(act_in), grad_hidden * gelu_value(act_in)], axis=1).astype(bf16)
    grad_mixed_flat = grad_mixed.reshape(ntok, 2 * hidden_units)
    grad_w_in = jnp.dot(second.T, grad_mixed_flat, preferred_element_type=f32).reshape(width, 2, hidden_units)
    feedforward_norm_gradient = jnp.dot(grad_mixed_flat, in_flat.T, preferred_element_type=f32)
    feedforward_normed_gradient, feedforward_gain_gradient = layer_normalize_backward(feedforward_norm_gradient, feedforward_standardized, feedforward_inverse_deviation, feedforward_norm_gain)
    grad_mid = upstream + feedforward_normed_gradient
    grad_mid_b = grad_mid.astype(bf16)
    grad_w_attn = jnp.dot(attended_flat.T, grad_mid_b, preferred_element_type=f32)
    grad_att = jnp.dot(grad_mid_b, out_weight.T, preferred_element_type=f32).astype(bf16).reshape(ntok, nheads, HD)
    delta = lax.optimization_barrier(jnp.sum(grad_att.astype(f32) * attended.astype(f32), axis=-1))

    def backward_block(carry, index):
        grad_key, grad_value = carry
        start = (index * block).astype(jnp.int32)
        q_rows = lax.dynamic_slice_in_dim(query, start, block, 0)
        do_rows = lax.dynamic_slice_in_dim(grad_att, start, block, 0)
        l_rows = lax.dynamic_slice_in_dim(lse, start, block, 0)
        d_rows = lax.dynamic_slice_in_dim(delta, start, block, 0)
        s_rows = lax.dynamic_slice_in_dim(seq_ids, start, block, 0)
        gq, gk, gv = block_grads(q_rows, do_rows, l_rows, d_rows, s_rows, keys, values, seq_ids, scale)
        return ((grad_key + gk, grad_value + gv), gq)
    zero = jnp.zeros((ntok, nheads, HD), f32)
    (grad_key, grad_value), grad_query = lax.scan(backward_block, (zero, zero), jnp.arange(nblocks, dtype=jnp.int32))
    grad_query = grad_query.reshape(ntok, nheads, HD)
    grad_proj = jnp.stack([unrotate(grad_query, cosine, sine), unrotate(grad_key, cosine, sine), grad_value], axis=1)
    grad_proj = grad_proj.astype(bf16).reshape(ntok, 3 * cols)
    grad_w_qkv = jnp.dot(first.T, grad_proj, preferred_element_type=f32).reshape(width, 3, cols)
    attention_norm_gradient = jnp.dot(grad_proj, qkv_flat.T, preferred_element_type=f32)
    attention_normed_gradient, attention_gain_gradient = layer_normalize_backward(attention_norm_gradient, attention_standardized, attention_inverse_deviation, attention_norm_gain)
    grad_tokens = grad_mid + attention_normed_gradient
    return (output, grad_tokens, attention_gain_gradient, grad_w_qkv, grad_w_attn, feedforward_gain_gradient, grad_w_in, grad_w_out)
```

```python
import functools
import math

import jax
import jax.numpy as jnp
from jax import lax
from jax.experimental import pallas as pl
from jax.experimental.pallas import tpu as pltpu
from jax.sharding import PartitionSpec as P

HD = 64
EPS = 1e-05
BASE = 160000.0
MASKED = -1e30
ROOT_HALF = 0.7071067811865476
INV_ROOT_TWO_PI = 0.3989422804014327
SEQS = 4
F32 = jnp.float32
BF16 = jnp.bfloat16
PAD = 16


def layer_normalize(values_in, norm_gain_vector):
    token_average = jnp.mean(values_in, axis=-1, keepdims=True)
    centered_input = values_in - token_average
    inverse_deviation = lax.rsqrt(
        jnp.mean(centered_input * centered_input, axis=-1, keepdims=True) + EPS
    )
    standardized_input = centered_input * inverse_deviation
    return (standardized_input, inverse_deviation, standardized_input * norm_gain_vector)


def layer_normalize_backward(
    output_gradient, standardized_input, inverse_deviation, norm_gain_vector
):
    normalized_gradient = output_gradient * norm_gain_vector
    correction_term = jnp.mean(
        normalized_gradient, axis=-1, keepdims=True
    ) + standardized_input * jnp.mean(
        normalized_gradient * standardized_input, axis=-1, keepdims=True
    )
    return (
        inverse_deviation * (normalized_gradient - correction_term),
        jnp.sum(output_gradient * standardized_input, axis=0),
    )


def gelu_value(v):
    return v * 0.5 * (1.0 + lax.erf(v * ROOT_HALF))


def gelu_slope(v):
    return 0.5 * (1.0 + lax.erf(v * ROOT_HALF)) + v * jnp.exp(-0.5 * v * v) * INV_ROOT_TWO_PI


def rope_tables_t(positions, head_size):
    half = head_size // 2
    inverse = BASE ** (-(jnp.arange(half, dtype=F32) * (2.0 / head_size)))
    angle = inverse[:, None] * positions.astype(F32)[None, :]
    return (jnp.cos(angle), jnp.sin(angle))


def rotate_t(field, cosine, sine):
    half = field.shape[1] // 2
    one, two = field[:, :half], field[:, half:]
    return jnp.concatenate([one * cosine - two * sine, two * cosine + one * sine], axis=1)


def unrotate_t(grad, cosine, sine):
    half = grad.shape[1] // 2
    one, two = grad[:, :half], grad[:, half:]
    return jnp.concatenate([one * cosine + two * sine, two * cosine - one * sine], axis=1)


def fill_natural(kvn, own, oth, groups, count, chunk):
    for r in range(groups):
        for c in range(count // chunk):
            at = slice(c * chunk, (c + 1) * chunk)
            if r == 0:
                piece = own[HD : 3 * HD, at]
            else:
                piece = oth[r - 1, 0 : 2 * HD, at]
            kvn[r * count + c * chunk : r * count + (c + 1) * chunk, :] = (
                piece.astype(F32).T.astype(BF16)
            )


def forward_kernel(lo, hi, q_ref, own, oth, rows, out, lse, kvn, *, groups, count, kb):
    i = pl.program_id(0)

    @pl.when(i == 0)
    def _():
        fill_natural(kvn, own, oth, groups, count, min(count, 256))

    qb = q_ref.shape[1]
    q = (q_ref[...].astype(F32) * (1.0 / math.sqrt(HD))).astype(BF16)
    q = jnp.concatenate([q, jnp.zeros_like(q)], axis=0)
    spot = lax.broadcasted_iota(jnp.int32, (kb, qb), 0)
    carry = (
        jnp.full((1, qb), MASKED, F32),
        jnp.zeros((1, qb), F32),
        jnp.zeros((HD, qb), F32),
    )
    for r in range(groups):
        first = rows[r : r + 1, :]
        end = rows[groups + r : groups + r + 1, :]

        def step(j, carry, r=r, first=first, end=end):
            top, den, acc = carry
            k0 = pl.multiple_of(j * kb, kb)
            s = jnp.dot(kvn[pl.ds(r * count + k0, kb), :], q, preferred_element_type=F32)
            s = jnp.where((spot >= first - k0) & (spot < end - k0), s, MASKED)
            new = jnp.maximum(top, jnp.max(s, axis=0, keepdims=True))
            p = jnp.exp(s - new)
            fade = jnp.exp(top - new)
            den = den * fade + jnp.sum(p, axis=0, keepdims=True)
            if r == 0:
                v = own[2 * HD : 3 * HD, pl.ds(k0, kb)]
            else:
                v = oth[r - 1, HD : 2 * HD, pl.ds(k0, kb)]
            acc = acc * fade + jnp.dot(v, p.astype(BF16), preferred_element_type=F32)
            return (new, den, acc)

        carry = lax.fori_loop(
            lo[i * groups + r] // kb, (hi[i * groups + r] + kb - 1) // kb, step, carry
        )
    top, den, acc = carry
    out[...] = (acc / den).astype(BF16)
    lse[...] = top + jnp.log(den)


def backward_kernel(
    lo, hi, q_ref, own, oth, rows, out, do_ref, lse, dq, dkv, dkv_oth, kvn, acc,
    *, groups, count, kb
):
    i = pl.program_id(0)

    @pl.when(i == 0)
    def _():
        fill_natural(kvn, own, oth, groups, count, min(count, 256))
        acc[...] = jnp.zeros_like(acc)

    qb = q_ref.shape[1]
    scale = 1.0 / math.sqrt(HD)
    qf = q_ref[...].astype(F32) * scale
    q = qf.astype(BF16)
    do = do_ref[...]
    dof = do.astype(F32)
    delta = jnp.sum(dof * out[...].astype(F32), axis=0, keepdims=True)
    none = jnp.zeros_like(q)
    q_pad = jnp.concatenate([q, none], axis=0)
    do_pad = jnp.concatenate([none, do], axis=0)
    q_nat = jnp.concatenate([qf, jnp.zeros_like(qf)], axis=0).T.astype(BF16)
    do_nat = jnp.concatenate([jnp.zeros_like(dof), dof], axis=0).T.astype(BF16)
    spot = lax.broadcasted_iota(jnp.int32, (kb, qb), 0)
    level = lse[...]
    grad = jnp.zeros((HD, qb), F32)
    for r in range(groups):
        first = rows[r : r + 1, :]
        end = rows[groups + r : groups + r + 1, :]

        def step(j, grad, r=r, first=first, end=end):
            k0 = pl.multiple_of(j * kb, kb)
            at = pl.ds(r * count + k0, kb)
            kv = kvn[at, :]
            s = jnp.dot(kv, q_pad, preferred_element_type=F32)
            dp = jnp.dot(kv, do_pad, preferred_element_type=F32)
            p = jnp.where((spot >= first - k0) & (spot < end - k0), jnp.exp(s - level), 0.0)
            ds = (p * (dp - delta)).astype(BF16)
            acc[at, :] += jnp.dot(ds, q_nat, preferred_element_type=F32) + jnp.dot(
                p.astype(BF16), do_nat, preferred_element_type=F32
            )
            if r == 0:
                k = own[HD : 2 * HD, pl.ds(k0, kb)]
            else:
                k = oth[r - 1, 0:HD, pl.ds(k0, kb)]
            return grad + jnp.dot(k, ds, preferred_element_type=F32)

        grad = lax.fori_loop(
            lo[i * groups + r] // kb, (hi[i * groups + r] + kb - 1) // kb, step, grad
        )
    dq[...] = (grad * scale).astype(BF16)

    @pl.when(i == pl.num_programs(0) - 1)
    def _():
        chunk = min(count, 256)
        for r in range(groups):
            for c in range(count // chunk):
                at = slice(c * chunk, (c + 1) * chunk)
                piece = acc[r * count + c * chunk : r * count + (c + 1) * chunk, :].T
                if r == 0:
                    dkv[:, at] = piece
                else:
                    dkv_oth[r - 1, :, at] = piece.astype(BF16)


def blocks_of(count):
    return math.gcd(count, 256), math.gcd(count, 512)


def whole(shape):
    return pl.BlockSpec(shape, lambda i, *_: (0,) * len(shape))


def attention_forward(lo, hi, own, oth, rows, groups):
    count = own.shape[1]
    qb, kb = blocks_of(count)
    col = lambda height: pl.BlockSpec((height, qb), lambda i, *_: (0, i))
    return pl.pallas_call(
        functools.partial(forward_kernel, groups=groups, count=count, kb=kb),
        grid_spec=pltpu.PrefetchScalarGridSpec(
            num_scalar_prefetch=2,
            grid=(count // qb,),
            in_specs=[col(HD), whole(own.shape), whole(oth.shape), col(rows.shape[0])],
            out_specs=[col(HD), col(1)],
            scratch_shapes=[pltpu.VMEM((groups * count, 2 * HD), BF16)],
        ),
        out_shape=[
            jax.ShapeDtypeStruct((HD, count), BF16),
            jax.ShapeDtypeStruct((1, count), F32),
        ],
        name="attention_forward",
    )(lo, hi, own, own, oth, rows)


def attention_backward(lo, hi, own, oth, rows, out, do, lse, groups):
    count = own.shape[1]
    qb, kb = blocks_of(count)
    col = lambda height: pl.BlockSpec((height, qb), lambda i, *_: (0, i))
    others = (max(groups - 1, 1), 2 * HD, count)
    return pl.pallas_call(
        functools.partial(backward_kernel, groups=groups, count=count, kb=kb),
        grid_spec=pltpu.PrefetchScalarGridSpec(
            num_scalar_prefetch=2,
            grid=(count // qb,),
            in_specs=[
                col(HD), whole(own.shape), whole(oth.shape), col(rows.shape[0]),
                col(HD), col(HD), col(1),
            ],
            out_specs=[col(HD), whole((2 * HD, count)), whole(others)],
            scratch_shapes=[
                pltpu.VMEM((groups * count, 2 * HD), BF16),
                pltpu.VMEM((groups * count, 2 * HD), F32),
            ],
        ),
        out_shape=[
            jax.ShapeDtypeStruct((HD, count), BF16),
            jax.ShapeDtypeStruct((2 * HD, count), F32),
            jax.ShapeDtypeStruct(others, BF16),
        ],
        name="attention_backward",
    )(lo, hi, own, own, oth, rows, out, do, lse)


def layer(
    tokens,
    seq_ids,
    attention_norm_gain,
    qkv_weight,
    out_weight,
    feedforward_norm_gain,
    mlp_in_weight,
    mlp_out_weight,
    grad_out,
    *,
    ctx,
    tp,
):
    tok_rows, width = tokens.shape
    local_cols = qkv_weight.shape[2]
    heads_here = local_cols // HD
    hidden_here = mlp_in_weight.shape[2]
    groups = ctx // heads_here
    part = tok_rows // groups
    count = ctx * part
    me = lax.axis_index("ctx")

    def tp_sum(value):
        value = value.astype(BF16)
        if tp == 2:
            other = lax.ppermute(value, "tp", [(0, 1), (1, 0)])
            return value.astype(F32) + other.astype(F32)
        return lax.psum(value, "tp").astype(F32)

    def to_group(value, r):
        pairs = [(i, i // groups * groups + (i + r) % groups) for i in range(ctx)]
        return lax.ppermute(value, "ctx", pairs)

    def to_heads(value):
        rows = value.shape[1]
        value = value.reshape(heads_here, rows, groups, part).transpose(0, 2, 1, 3)
        value = lax.all_to_all(value.reshape(ctx, rows, part), "ctx", 0, 0)
        return value.transpose(1, 0, 2).reshape(rows, count)

    def to_tokens(value):
        rows = value.shape[0]
        value = value.reshape(rows, ctx, part).transpose(1, 0, 2)
        value = lax.all_to_all(value, "ctx", 0, 0)
        value = value.reshape(heads_here, groups, rows, part).transpose(0, 2, 1, 3)
        return value.reshape(heads_here, rows, tok_rows)

    def swap(value, bit):
        return lax.ppermute(value, "ctx", [(i, i ^ (1 << bit)) for i in range(ctx)])

    def ctx_sum(value, order):
        for bit in order:
            side = (me >> bit) & 1
            halves = value.reshape(2, value.shape[0] // 2, value.shape[1])
            send = lax.dynamic_index_in_dim(halves, 1 - side, 0, keepdims=False)
            keep = lax.dynamic_index_in_dim(halves, side, 0, keepdims=False)
            value = (keep.astype(F32) + swap(send, bit).astype(F32)).astype(BF16)
        for bit in reversed(order):
            side = (me >> bit) & 1
            other = swap(value, bit)
            value = jnp.concatenate(
                [jnp.where(side == 0, value, other), jnp.where(side == 0, other, value)], axis=0
            )
        return value

    bits = list(range(ctx.bit_length() - 1))
    order_a = bits
    order_b = bits[:1] + bits[2:3] + bits[1:2] + bits[3:]

    input_tokens = tokens.astype(F32)
    attention_standardized, attention_inverse_deviation, attention_normed_input = layer_normalize(
        input_tokens, attention_norm_gain
    )
    first = attention_normed_input.astype(BF16)
    qkv_flat = qkv_weight.reshape(width, 3 * local_cols)
    proj = lax.dot_general(
        qkv_flat, first, (((0,), (1,)), ((), ())), preferred_element_type=F32
    ).reshape(3, heads_here, HD, tok_rows)
    positions = me * tok_rows + jnp.arange(tok_rows, dtype=jnp.int32)
    cosine, sine = rope_tables_t(positions, HD)
    ids = jnp.broadcast_to(seq_ids.astype(BF16)[None, None, :], (heads_here, PAD, tok_rows))
    packed = jnp.concatenate(
        [
            rotate_t(proj[0], cosine, sine).astype(BF16),
            rotate_t(proj[1], cosine, sine).astype(BF16),
            proj[2].astype(BF16),
            ids,
        ],
        axis=1,
    )
    own = to_heads(packed)
    if groups > 1:
        oth = jnp.stack([to_group(own[HD:], groups - r) for r in range(1, groups)])
    else:
        oth = own[None, HD:]
    id_own = own[3 * HD]
    id_all = jnp.concatenate([id_own[None], oth[: groups - 1, 2 * HD]], axis=0)
    marks = jnp.arange(SEQS + 1, dtype=F32)
    below = jnp.sum((id_all.astype(F32)[:, None, :] < marks[None, :, None]).astype(jnp.int32), -1)
    first_key = jnp.zeros((groups, count), jnp.int32)
    end_key = jnp.zeros((groups, count), jnp.int32)
    for s in range(SEQS):
        hit = (id_own == s)[None, :]
        first_key = jnp.where(hit, below[:, s : s + 1], first_key)
        end_key = jnp.where(hit, below[:, s + 1 : s + 2], end_key)
    rows = jnp.concatenate([first_key, end_key], axis=0)
    qb, _ = blocks_of(count)
    lo = first_key[:, ::qb].T.reshape(-1)
    hi = end_key[:, qb - 1 :: qb].T.reshape(-1)
    att_head, lse = attention_forward(lo, hi, own, oth, rows, groups)
    attended = to_tokens(att_head).reshape(local_cols, tok_rows)
    attn_part = lax.dot_general(
        attended, out_weight, (((0,), (0,)), ((), ())), preferred_element_type=F32
    )
    residual_middle = input_tokens + tp_sum(attn_part)
    feedforward_standardized, feedforward_inverse_deviation, feedforward_normed_input = (
        layer_normalize(residual_middle, feedforward_norm_gain)
    )
    second = feedforward_normed_input.astype(BF16)
    in_act = mlp_in_weight[:, 0]
    in_gate = mlp_in_weight[:, 1]
    act_in = jnp.dot(second, in_act, preferred_element_type=F32)
    gate = jnp.dot(second, in_gate, preferred_element_type=F32)
    hidden = (gelu_value(act_in) * gate).astype(BF16)
    upstream = grad_out.astype(F32)
    grad_hidden = lax.dot_general(
        grad_out, mlp_out_weight, (((1,), (1,)), ((), ())), preferred_element_type=F32
    )
    grad_act = (grad_hidden * gate * gelu_slope(act_in)).astype(BF16)
    grad_gate = (grad_hidden * gelu_value(act_in)).astype(BF16)
    over_cols = (((1,), (1,)), ((), ()))
    over_rows = (((0,), (0,)), ((), ()))
    second_part = lax.dot_general(
        grad_act, in_act, over_cols, preferred_element_type=F32
    ) + lax.dot_general(grad_gate, in_gate, over_cols, preferred_element_type=F32)
    feedforward_norm_gradient = tp_sum(second_part)
    grad_w_act = lax.dot_general(second, grad_act, over_rows, preferred_element_type=F32)
    grad_w_gate = lax.dot_general(second, grad_gate, over_rows, preferred_element_type=F32)
    grad_w_out = lax.dot_general(hidden, grad_out, over_rows, preferred_element_type=F32)
    sum_act, sum_gate, sum_w_out = (
        lax.psum(value.astype(BF16), "ctx").astype(F32)
        for value in (grad_w_act, grad_w_gate, grad_w_out)
    )
    ffn_part = jnp.dot(hidden, mlp_out_weight, preferred_element_type=F32)
    output = (residual_middle + tp_sum(ffn_part)).astype(BF16)
    feedforward_normed_gradient, feedforward_gain_gradient = layer_normalize_backward(
        feedforward_norm_gradient,
        feedforward_standardized,
        feedforward_inverse_deviation,
        feedforward_norm_gain,
    )
    grad_mid = upstream + feedforward_normed_gradient
    grad_mid_b = grad_mid.astype(BF16)
    grad_att = (
        lax.dot_general(out_weight, grad_mid_b, over_cols, preferred_element_type=F32)
        .astype(BF16)
        .reshape(heads_here, HD, tok_rows)
    )
    do_head = to_heads(grad_att)
    dq, dkv, dkv_oth = attention_backward(
        lo, hi, own, oth, rows, att_head, do_head, lse, groups
    )
    for r in range(1, groups):
        dkv = dkv + to_group(dkv_oth[r - 1], r).astype(F32)
    grads = to_tokens(jnp.concatenate([dq, dkv.astype(BF16)], axis=0)).astype(F32)
    grad_proj = (
        jnp.stack(
            [
                unrotate_t(grads[:, :HD], cosine, sine),
                unrotate_t(grads[:, HD : 2 * HD], cosine, sine),
                grads[:, 2 * HD :],
            ]
        )
        .astype(BF16)
        .reshape(3 * local_cols, tok_rows)
    )
    first_part = lax.dot_general(
        grad_proj, qkv_flat, (((0,), (1,)), ((), ())), preferred_element_type=F32
    )
    attention_norm_gradient = tp_sum(first_part)
    grad_w_qkv = jnp.concatenate(
        [
            lax.dot_general(
                first,
                grad_proj[c * local_cols : (c + 1) * local_cols],
                (((0,), (1,)), ((), ())),
                preferred_element_type=F32,
            ).astype(BF16)
            for c in range(3)
        ],
        axis=0,
    )
    grad_w_attn = jnp.dot(attended, grad_mid_b, preferred_element_type=F32).astype(BF16)
    sum_attn = ctx_sum(grad_w_attn, order_a)
    middle = 3 * width // 2
    sum_qkv = (
        jnp.concatenate(
            [ctx_sum(grad_w_qkv[:middle], order_a), ctx_sum(grad_w_qkv[middle:], order_b)], axis=0
        )
        .reshape(3, width, local_cols)
        .transpose(1, 0, 2)
        .astype(F32)
    )
    attention_normed_gradient, attention_gain_gradient = layer_normalize_backward(
        attention_norm_gradient,
        attention_standardized,
        attention_inverse_deviation,
        attention_norm_gain,
    )
    grad_tokens = grad_mid + attention_normed_gradient
    gains = jnp.stack([attention_gain_gradient, feedforward_gain_gradient])
    for bit in bits:
        gains = gains + swap(gains, bit)
    return (
        output,
        grad_tokens,
        gains[0],
        sum_qkv,
        sum_attn.astype(F32),
        gains[1],
        jnp.stack([sum_act, sum_gate], axis=1),
        sum_w_out,
    )


def solution(mesh):
    return jax.shard_map(
        functools.partial(layer, ctx=mesh.shape["ctx"], tp=mesh.shape["tp"]),
        mesh=mesh,
        in_specs=(
            P("ctx", None),
            P("ctx"),
            P(),
            P(None, None, "tp"),
            P("tp", None),
            P(),
            P(None, None, "tp"),
            P("tp", None),
            P("ctx", None),
        ),
        out_specs=(
            P("ctx", None),
            P("ctx", None),
            P(),
            P(None, None, "tp"),
            P("tp", None),
            P(),
            P(None, None, "tp"),
            P("tp", None),
        ),
        check_vma=False,
    )
```

```python
import functools
import math

import jax
import jax.numpy as jnp
from jax import lax
from jax.experimental import pallas as pl
from jax.experimental.pallas import tpu as pltpu
from jax.sharding import PartitionSpec as P

HD = 64
EPS = 1e-05
BASE = 160000.0
MASKED = -1e30
ROOT_HALF = 0.7071067811865476
INV_ROOT_TWO_PI = 0.3989422804014327
SEQS = 4
F32 = jnp.float32
BF16 = jnp.bfloat16
PAD = 16


def layer_normalize(values_in, norm_gain_vector):
    token_average = jnp.mean(values_in, axis=-1, keepdims=True)
    centered_input = values_in - token_average
    inverse_deviation = lax.rsqrt(
        jnp.mean(centered_input * centered_input, axis=-1, keepdims=True) + EPS
    )
    standardized_input = centered_input * inverse_deviation
    return (standardized_input, inverse_deviation, standardized_input * norm_gain_vector)


def layer_normalize_backward(
    output_gradient, standardized_input, inverse_deviation, norm_gain_vector
):
    normalized_gradient = output_gradient * norm_gain_vector
    correction_term = jnp.mean(
        normalized_gradient, axis=-1, keepdims=True
    ) + standardized_input * jnp.mean(
        normalized_gradient * standardized_input, axis=-1, keepdims=True
    )
    return (
        inverse_deviation * (normalized_gradient - correction_term),
        jnp.sum(output_gradient * standardized_input, axis=0),
    )


def gelu_value(v):
    return v * 0.5 * (1.0 + lax.erf(v * ROOT_HALF))


def gelu_slope(v):
    return 0.5 * (1.0 + lax.erf(v * ROOT_HALF)) + v * jnp.exp(-0.5 * v * v) * INV_ROOT_TWO_PI


def rope_tables_t(positions, head_size):
    half = head_size // 2
    inverse = BASE ** (-(jnp.arange(half, dtype=F32) * (2.0 / head_size)))
    angle = inverse[:, None] * positions.astype(F32)[None, :]
    return (jnp.cos(angle), jnp.sin(angle))


def rotate_t(field, cosine, sine):
    half = field.shape[1] // 2
    one, two = field[:, :half], field[:, half:]
    return jnp.concatenate([one * cosine - two * sine, two * cosine + one * sine], axis=1)


def unrotate_t(grad, cosine, sine):
    half = grad.shape[1] // 2
    one, two = grad[:, :half], grad[:, half:]
    return jnp.concatenate([one * cosine + two * sine, two * cosine - one * sine], axis=1)


def fill_natural(kvn, own, oth, groups, count, chunk):
    for r in range(groups):
        for c in range(count // chunk):
            at = slice(c * chunk, (c + 1) * chunk)
            if r == 0:
                piece = own[HD : 3 * HD, at]
            else:
                piece = oth[r - 1, 0 : 2 * HD, at]
            kvn[r * count + c * chunk : r * count + (c + 1) * chunk, :] = (
                piece.astype(F32).T.astype(BF16)
            )


def forward_kernel(lo, hi, q_ref, own, oth, rows, out, lse, kvn, *, groups, count, kb):
    i = pl.program_id(0)

    @pl.when(i == 0)
    def _():
        fill_natural(kvn, own, oth, groups, count, min(count, 256))

    qb = q_ref.shape[1]
    q = (q_ref[...].astype(F32) * (1.0 / math.sqrt(HD))).astype(BF16)
    q = jnp.concatenate([q, jnp.zeros_like(q)], axis=0)
    spot = lax.broadcasted_iota(jnp.int32, (kb, qb), 0)
    carry = (
        jnp.full((1, qb), MASKED, F32),
        jnp.zeros((1, qb), F32),
        jnp.zeros((HD, qb), F32),
    )
    for r in range(groups):
        first = rows[r : r + 1, :]
        end = rows[groups + r : groups + r + 1, :]

        def step(j, carry, r=r, first=first, end=end):
            top, den, acc = carry
            k0 = pl.multiple_of(j * kb, kb)
            s = jnp.dot(kvn[pl.ds(r * count + k0, kb), :], q, preferred_element_type=F32)
            s = jnp.where((spot >= first - k0) & (spot < end - k0), s, MASKED)
            new = jnp.maximum(top, jnp.max(s, axis=0, keepdims=True))
            p = jnp.exp(s - new)
            fade = jnp.exp(top - new)
            den = den * fade + jnp.sum(p, axis=0, keepdims=True)
            if r == 0:
                v = own[2 * HD : 3 * HD, pl.ds(k0, kb)]
            else:
                v = oth[r - 1, HD : 2 * HD, pl.ds(k0, kb)]
            acc = acc * fade + jnp.dot(v, p.astype(BF16), preferred_element_type=F32)
            return (new, den, acc)

        carry = lax.fori_loop(
            lo[i * groups + r] // kb, (hi[i * groups + r] + kb - 1) // kb, step, carry
        )
    top, den, acc = carry
    out[...] = (acc / den).astype(BF16)
    lse[...] = top + jnp.log(den)


def backward_kernel(
    lo, hi, q_ref, own, oth, rows, out, do_ref, lse, dq, dkv, dkv_oth, kvn, acc,
    *, groups, count, kb
):
    i = pl.program_id(0)

    @pl.when(i == 0)
    def _():
        fill_natural(kvn, own, oth, groups, count, min(count, 256))
        acc[...] = jnp.zeros_like(acc)

    qb = q_ref.shape[1]
    scale = 1.0 / math.sqrt(HD)
    qf = q_ref[...].astype(F32) * scale
    q = qf.astype(BF16)
    do = do_ref[...]
    dof = do.astype(F32)
    delta = jnp.sum(dof * out[...].astype(F32), axis=0, keepdims=True)
    none = jnp.zeros_like(q)
    q_pad = jnp.concatenate([q, none], axis=0)
    do_pad = jnp.concatenate([none, do], axis=0)
    q_nat = jnp.concatenate([qf, jnp.zeros_like(qf)], axis=0).T.astype(BF16)
    do_nat = jnp.concatenate([jnp.zeros_like(dof), dof], axis=0).T.astype(BF16)
    spot = lax.broadcasted_iota(jnp.int32, (kb, qb), 0)
    level = lse[...]
    grad = jnp.zeros((HD, qb), F32)
    for r in range(groups):
        first = rows[r : r + 1, :]
        end = rows[groups + r : groups + r + 1, :]

        def step(j, grad, r=r, first=first, end=end):
            k0 = pl.multiple_of(j * kb, kb)
            at = pl.ds(r * count + k0, kb)
            kv = kvn[at, :]
            s = jnp.dot(kv, q_pad, preferred_element_type=F32)
            dp = jnp.dot(kv, do_pad, preferred_element_type=F32)
            p = jnp.where((spot >= first - k0) & (spot < end - k0), jnp.exp(s - level), 0.0)
            ds = (p * (dp - delta)).astype(BF16)
            acc[at, :] += jnp.dot(ds, q_nat, preferred_element_type=F32) + jnp.dot(
                p.astype(BF16), do_nat, preferred_element_type=F32
            )
            if r == 0:
                k = own[HD : 2 * HD, pl.ds(k0, kb)]
            else:
                k = oth[r - 1, 0:HD, pl.ds(k0, kb)]
            return grad + jnp.dot(k, ds, preferred_element_type=F32)

        grad = lax.fori_loop(
            lo[i * groups + r] // kb, (hi[i * groups + r] + kb - 1) // kb, step, grad
        )
    dq[...] = grad * scale

    @pl.when(i == pl.num_programs(0) - 1)
    def _():
        chunk = min(count, 256)
        for r in range(groups):
            for c in range(count // chunk):
                at = slice(c * chunk, (c + 1) * chunk)
                piece = acc[r * count + c * chunk : r * count + (c + 1) * chunk, :].T
                if r == 0:
                    dkv[:, at] = piece
                else:
                    dkv_oth[r - 1, :, at] = piece.astype(BF16)


def blocks_of(count):
    return math.gcd(count, 256), math.gcd(count, 512)


def whole(shape):
    return pl.BlockSpec(shape, lambda i, *_: (0,) * len(shape))


def attention_forward(lo, hi, own, oth, rows, groups):
    count = own.shape[1]
    qb, kb = blocks_of(count)
    col = lambda height: pl.BlockSpec((height, qb), lambda i, *_: (0, i))
    return pl.pallas_call(
        functools.partial(forward_kernel, groups=groups, count=count, kb=kb),
        grid_spec=pltpu.PrefetchScalarGridSpec(
            num_scalar_prefetch=2,
            grid=(count // qb,),
            in_specs=[col(HD), whole(own.shape), whole(oth.shape), col(rows.shape[0])],
            out_specs=[col(HD), col(1)],
            scratch_shapes=[pltpu.VMEM((groups * count, 2 * HD), BF16)],
        ),
        out_shape=[
            jax.ShapeDtypeStruct((HD, count), BF16),
            jax.ShapeDtypeStruct((1, count), F32),
        ],
        name="attention_forward",
    )(lo, hi, own, own, oth, rows)


def attention_backward(lo, hi, own, oth, rows, out, do, lse, groups):
    count = own.shape[1]
    qb, kb = blocks_of(count)
    col = lambda height: pl.BlockSpec((height, qb), lambda i, *_: (0, i))
    others = (max(groups - 1, 1), 2 * HD, count)
    return pl.pallas_call(
        functools.partial(backward_kernel, groups=groups, count=count, kb=kb),
        grid_spec=pltpu.PrefetchScalarGridSpec(
            num_scalar_prefetch=2,
            grid=(count // qb,),
            in_specs=[
                col(HD), whole(own.shape), whole(oth.shape), col(rows.shape[0]),
                col(HD), col(HD), col(1),
            ],
            out_specs=[col(HD), whole((2 * HD, count)), whole(others)],
            scratch_shapes=[
                pltpu.VMEM((groups * count, 2 * HD), BF16),
                pltpu.VMEM((groups * count, 2 * HD), F32),
            ],
        ),
        out_shape=[
            jax.ShapeDtypeStruct((HD, count), F32),
            jax.ShapeDtypeStruct((2 * HD, count), F32),
            jax.ShapeDtypeStruct(others, BF16),
        ],
        name="attention_backward",
    )(lo, hi, own, own, oth, rows, out, do, lse)


def layer(
    tokens,
    seq_ids,
    attention_norm_gain,
    qkv_weight,
    out_weight,
    feedforward_norm_gain,
    mlp_in_weight,
    mlp_out_weight,
    grad_out,
    *,
    ctx,
    tp,
):
    tok_rows, width = tokens.shape
    local_cols = qkv_weight.shape[2]
    heads_here = local_cols // HD
    hidden_here = mlp_in_weight.shape[2]
    groups = ctx // heads_here
    part = tok_rows // groups
    count = ctx * part
    me = lax.axis_index("ctx")

    def tp_sum(value):
        value = value.astype(BF16)
        if tp == 2:
            other = lax.ppermute(value, "tp", [(0, 1), (1, 0)])
            return value.astype(F32) + other.astype(F32)
        return lax.psum(value, "tp").astype(F32)

    def to_group(value, r):
        pairs = [(i, i // groups * groups + (i + r) % groups) for i in range(ctx)]
        return lax.ppermute(value, "ctx", pairs)

    def to_heads(value):
        rows = value.shape[1]
        value = value.reshape(heads_here, rows, groups, part).transpose(0, 2, 1, 3)
        value = lax.all_to_all(value.reshape(ctx, rows, part), "ctx", 0, 0)
        return value.transpose(1, 0, 2).reshape(rows, count)

    def to_tokens(value):
        rows = value.shape[0]
        value = value.reshape(rows, ctx, part).transpose(1, 0, 2)
        value = lax.all_to_all(value, "ctx", 0, 0)
        value = value.reshape(heads_here, groups, rows, part).transpose(0, 2, 1, 3)
        return value.reshape(heads_here, rows, tok_rows)

    def swap(value, bit):
        return lax.ppermute(value, "ctx", [(i, i ^ (1 << bit)) for i in range(ctx)])

    def after(value, *needed):
        return lax.optimization_barrier((value,) + needed)[0]

    def split(value, bit, axis):
        low, high = jnp.split(value, 2, axis=axis)
        side = (me >> bit) & 1
        return jnp.where(side == 0, low, high), jnp.where(side == 0, high, low)

    def add(keep, other):
        return (keep.astype(F32) + other.astype(F32)).astype(BF16)

    def join(mine, other, bit, axis):
        side = (me >> bit) & 1
        return jnp.concatenate(
            [jnp.where(side == 0, mine, other), jnp.where(side == 0, other, mine)], axis=axis
        )

    bits = list(range(ctx.bit_length() - 1))
    group_bits = list(range(groups.bit_length() - 1))
    head_bits = bits[len(group_bits) :]
    over_cols = (((1,), (1,)), ((), ()))
    over_rows = (((0,), (0,)), ((), ()))
    across = (((0,), (1,)), ((), ()))

    def dot(left, right, dims=(((1,), (0,)), ((), ()))):
        return lax.dot_general(left, right, dims, preferred_element_type=F32)

    input_tokens = tokens.astype(F32)
    attention_standardized, attention_inverse_deviation, attention_normed_input = layer_normalize(
        input_tokens, attention_norm_gain
    )
    first = attention_normed_input.astype(BF16)
    planes = [qkv_weight[:, c] for c in range(3)]
    proj = [dot(plane, first, across).reshape(heads_here, HD, tok_rows) for plane in planes]
    positions = me * tok_rows + jnp.arange(tok_rows, dtype=jnp.int32)
    cosine, sine = rope_tables_t(positions, HD)
    ids = jnp.broadcast_to(seq_ids.astype(BF16)[None, None, :], (heads_here, PAD, tok_rows))
    packed = jnp.concatenate(
        [
            rotate_t(proj[0], cosine, sine).astype(BF16),
            rotate_t(proj[1], cosine, sine).astype(BF16),
            proj[2].astype(BF16),
            ids,
        ],
        axis=1,
    )
    own = to_heads(packed)
    if groups > 1:
        oth = jnp.stack([to_group(own[HD:], groups - r) for r in range(1, groups)])
    else:
        oth = own[None, HD:]
    id_own = own[3 * HD]
    id_all = jnp.concatenate([id_own[None], oth[: groups - 1, 2 * HD]], axis=0)
    marks = jnp.arange(SEQS + 1, dtype=F32)
    below = jnp.sum((id_all.astype(F32)[:, None, :] < marks[None, :, None]).astype(jnp.int32), -1)
    first_key = jnp.zeros((groups, count), jnp.int32)
    end_key = jnp.zeros((groups, count), jnp.int32)
    for s in range(SEQS):
        hit = (id_own == s)[None, :]
        first_key = jnp.where(hit, below[:, s : s + 1], first_key)
        end_key = jnp.where(hit, below[:, s + 1 : s + 2], end_key)
    rows = jnp.concatenate([first_key, end_key], axis=0)
    qb, _ = blocks_of(count)
    lo = first_key[:, ::qb].T.reshape(-1)
    hi = end_key[:, qb - 1 :: qb].T.reshape(-1)

    place = me % groups
    parts = after(first, own).reshape(groups, part, width)
    held = [lax.dynamic_index_in_dim(parts, place, 0, keepdims=False)]
    for r in range(1, groups):
        held.append(
            to_group(
                lax.dynamic_index_in_dim(parts, (place + r) % groups, 0, keepdims=False), r
            )
        )
    held = jnp.stack(held)
    held = jnp.concatenate(
        [
            lax.dynamic_index_in_dim(held, (place - c) % groups, 0, keepdims=False)
            for c in range(groups)
        ],
        axis=0,
    )
    first_all = lax.all_gather(
        held,
        "ctx",
        axis=0,
        tiled=True,
        axis_index_groups=[[h * groups + g for h in range(heads_here)] for g in range(groups)],
    )

    att_head, lse = attention_forward(lo, hi, own, oth, rows, groups)
    attended = to_tokens(att_head).reshape(local_cols, tok_rows)
    attn_part = dot(attended, out_weight, over_rows)
    residual_middle = input_tokens + tp_sum(attn_part)
    feedforward_standardized, feedforward_inverse_deviation, feedforward_normed_input = (
        layer_normalize(residual_middle, feedforward_norm_gain)
    )
    second, first_all = lax.optimization_barrier(
        (feedforward_normed_input.astype(BF16), first_all)
    )
    in_act = mlp_in_weight[:, 0]
    in_gate = mlp_in_weight[:, 1]
    act_in = dot(second, in_act)
    gate = dot(second, in_gate)
    hidden = (gelu_value(act_in) * gate).astype(BF16)
    upstream = grad_out.astype(F32)
    grad_hidden = dot(grad_out, mlp_out_weight, over_cols)
    grad_act = (grad_hidden * gate * gelu_slope(act_in)).astype(BF16)
    grad_gate = (grad_hidden * gelu_value(act_in)).astype(BF16)
    second_part = dot(grad_act, in_act, over_cols) + dot(grad_gate, in_gate, over_cols)
    feedforward_norm_gradient = tp_sum(second_part)
    grad_w_in = jnp.concatenate(
        [dot(grad_act, second, over_rows), dot(grad_gate, second, over_rows)], axis=0
    ).astype(BF16)
    grad_w_out = dot(hidden, grad_out, over_rows).astype(BF16)
    feedforward_norm_gradient, grad_w_in, grad_w_out = lax.optimization_barrier(
        (feedforward_norm_gradient, grad_w_in, grad_w_out)
    )
    sum_in = lax.psum(grad_w_in, "ctx")
    feedforward_normed_gradient, feedforward_gain_gradient = layer_normalize_backward(
        feedforward_norm_gradient,
        feedforward_standardized,
        feedforward_inverse_deviation,
        feedforward_norm_gain,
    )
    grad_mid = upstream + feedforward_normed_gradient
    grad_mid_b = grad_mid.astype(BF16)
    grad_att = dot(out_weight, grad_mid_b, over_cols).astype(BF16)
    do_head = to_heads(grad_att.reshape(heads_here, HD, tok_rows))

    late_mid = after(grad_mid_b, grad_att)
    grad_w_attn = dot(attended, late_mid).astype(BF16)
    pair = jnp.concatenate([grad_w_out, grad_w_attn], axis=0)
    keep, send = split(pair, 0, 0)
    keep, came = lax.optimization_barrier((keep, swap(send, 0)))
    pair = add(keep, came)
    keep, send = split(pair, 1, 1)
    send, do_head = lax.optimization_barrier((send, do_head))
    came = swap(send, 1)
    ffn_part = dot(after(hidden, grad_att), mlp_out_weight)
    output_sum = tp_sum(after(ffn_part.astype(BF16), do_head))
    dq, dkv, dkv_oth = attention_backward(
        lo, hi, own, oth, rows, att_head, do_head, lse, groups
    )
    output_sum, keep, came, dq, dkv, dkv_oth = lax.optimization_barrier(
        (output_sum, keep, came, dq, dkv, dkv_oth)
    )
    output = (residual_middle + output_sum).astype(BF16)
    for r in range(1, groups):
        dkv = dkv + to_group(dkv_oth[r - 1], r).astype(F32)
    spots = (
        jnp.arange(ctx, dtype=jnp.int32)[:, None] * tok_rows
        + place * part
        + jnp.arange(part, dtype=jnp.int32)[None, :]
    ).reshape(-1)
    cosine_head, sine_head = rope_tables_t(spots, HD)
    grads = jnp.concatenate(
        [
            unrotate_t(dq[None], cosine_head, sine_head)[0].astype(BF16),
            unrotate_t(dkv[None, :HD], cosine_head, sine_head)[0].astype(BF16),
            dkv[HD:].astype(BF16),
        ],
        axis=0,
    )
    grad_proj = to_tokens(grads)

    share = dot(grads, first_all).astype(BF16)
    for bit in group_bits:
        mine, send = split(share, bit, 1)
        share = add(mine, swap(send, bit))
    share = share[None]
    for at, bit in enumerate(reversed(head_bits)):
        share = join(share, swap(share, bit), bit, 0)
        if at == 0:
            grad_proj, share = lax.optimization_barrier((grad_proj, share))
    for bit in reversed(group_bits):
        share = join(share, swap(share, bit), bit, 2)

    pair = add(keep, came)
    for bit in bits[2:]:
        keep, send = split(pair, bit, 1)
        pair = add(keep, swap(send, bit))
    for bit in reversed(bits):
        pair = join(pair, swap(pair, bit), bit, 1 if bit else 0)
    sum_w_out, sum_attn = pair[:hidden_here], pair[hidden_here:]

    first_part = sum(
        dot(grad_proj[:, c * HD : (c + 1) * HD].reshape(local_cols, tok_rows), planes[c], across)
        for c in range(3)
    )
    attention_norm_gradient = tp_sum(first_part)
    attention_normed_gradient, attention_gain_gradient = layer_normalize_backward(
        attention_norm_gradient,
        attention_standardized,
        attention_inverse_deviation,
        attention_norm_gain,
    )
    grad_tokens = grad_mid + attention_normed_gradient
    gains = jnp.stack([attention_gain_gradient, feedforward_gain_gradient])
    for bit in bits:
        gains = gains + swap(gains, bit)
    sum_in = after(sum_in, share, pair, grad_tokens, gains)
    k = len(head_bits)
    sum_qkv = share.reshape((2,) * k + (3, HD, width)).transpose(
        (k + 2, k) + tuple(reversed(range(k))) + (k + 1,)
    )
    return (
        output,
        grad_tokens,
        gains[0],
        sum_qkv.reshape(width, 3, local_cols).astype(F32),
        sum_attn.astype(F32),
        gains[1],
        sum_in.reshape(2, hidden_here, width).transpose(2, 0, 1).astype(F32),
        sum_w_out.astype(F32),
    )


def solution(mesh):
    return jax.shard_map(
        functools.partial(layer, ctx=mesh.shape["ctx"], tp=mesh.shape["tp"]),
        mesh=mesh,
        in_specs=(
            P("ctx", None),
            P("ctx"),
            P(),
            P(None, None, "tp"),
            P("tp", None),
            P(),
            P(None, None, "tp"),
            P("tp", None),
            P("ctx", None),
        ),
        out_specs=(
            P("ctx", None),
            P("ctx", None),
            P(),
            P(None, None, "tp"),
            P("tp", None),
            P(),
            P(None, None, "tp"),
            P("tp", None),
        ),
        check_vma=False,
    )
```

```python
import functools
import math

import jax
import jax.numpy as jnp
from jax import lax
from jax.experimental import pallas as pl
from jax.experimental.pallas import tpu as pltpu
from jax.sharding import PartitionSpec as P

HD = 64
EPS = 1e-05
BASE = 160000.0
MASKED = -1e30
ROOT_HALF = 0.7071067811865476
INV_ROOT_TWO_PI = 0.3989422804014327
SEQS = 4
F32 = jnp.float32
BF16 = jnp.bfloat16
PAD = 16


def layer_normalize(values_in, norm_gain_vector):
    token_average = jnp.mean(values_in, axis=-1, keepdims=True)
    centered_input = values_in - token_average
    inverse_deviation = lax.rsqrt(
        jnp.mean(centered_input * centered_input, axis=-1, keepdims=True) + EPS
    )
    standardized_input = centered_input * inverse_deviation
    return (standardized_input, inverse_deviation, standardized_input * norm_gain_vector)


def layer_normalize_backward(
    output_gradient, standardized_input, inverse_deviation, norm_gain_vector
):
    normalized_gradient = output_gradient * norm_gain_vector
    correction_term = jnp.mean(
        normalized_gradient, axis=-1, keepdims=True
    ) + standardized_input * jnp.mean(
        normalized_gradient * standardized_input, axis=-1, keepdims=True
    )
    return (
        inverse_deviation * (normalized_gradient - correction_term),
        jnp.sum(output_gradient * standardized_input, axis=0),
    )


def gelu_value(v):
    return v * 0.5 * (1.0 + lax.erf(v * ROOT_HALF))


def gelu_slope(v):
    return 0.5 * (1.0 + lax.erf(v * ROOT_HALF)) + v * jnp.exp(-0.5 * v * v) * INV_ROOT_TWO_PI


def rope_tables_t(positions, head_size):
    half = head_size // 2
    inverse = BASE ** (-(jnp.arange(half, dtype=F32) * (2.0 / head_size)))
    angle = inverse[:, None] * positions.astype(F32)[None, :]
    return (jnp.cos(angle), jnp.sin(angle))


def rotate_t(field, cosine, sine):
    half = field.shape[1] // 2
    one, two = field[:, :half], field[:, half:]
    return jnp.concatenate([one * cosine - two * sine, two * cosine + one * sine], axis=1)


def unrotate_t(grad, cosine, sine):
    half = grad.shape[1] // 2
    one, two = grad[:, :half], grad[:, half:]
    return jnp.concatenate([one * cosine + two * sine, two * cosine - one * sine], axis=1)


def fill_natural(kvn, own, oth, groups, count, chunk):
    for r in range(groups):
        for c in range(count // chunk):
            at = slice(c * chunk, (c + 1) * chunk)
            if r == 0:
                piece = own[HD : 3 * HD, at]
            else:
                piece = oth[r - 1, 0 : 2 * HD, at]
            kvn[r * count + c * chunk : r * count + (c + 1) * chunk, :] = (
                piece.astype(F32).T.astype(BF16)
            )


def forward_kernel(lo, hi, q_ref, own, oth, rows, out, lse, kvn, *, groups, count, kb):
    i = pl.program_id(0)

    @pl.when(i == 0)
    def _():
        fill_natural(kvn, own, oth, groups, count, min(count, 256))

    qb = q_ref.shape[1]
    q = (q_ref[...].astype(F32) * (1.0 / math.sqrt(HD))).astype(BF16)
    q = jnp.concatenate([q, jnp.zeros_like(q)], axis=0)
    spot = lax.broadcasted_iota(jnp.int32, (kb, qb), 0)
    carry = (
        jnp.full((1, qb), MASKED, F32),
        jnp.zeros((1, qb), F32),
        jnp.zeros((HD, qb), F32),
    )
    for r in range(groups):
        first = rows[r : r + 1, :]
        end = rows[groups + r : groups + r + 1, :]

        def step(j, carry, r=r, first=first, end=end):
            top, den, acc = carry
            k0 = pl.multiple_of(j * kb, kb)
            s = jnp.dot(kvn[pl.ds(r * count + k0, kb), :], q, preferred_element_type=F32)
            s = jnp.where((spot >= first - k0) & (spot < end - k0), s, MASKED)
            new = jnp.maximum(top, jnp.max(s, axis=0, keepdims=True))
            p = jnp.exp(s - new)
            fade = jnp.exp(top - new)
            den = den * fade + jnp.sum(p, axis=0, keepdims=True)
            if r == 0:
                v = own[2 * HD : 3 * HD, pl.ds(k0, kb)]
            else:
                v = oth[r - 1, HD : 2 * HD, pl.ds(k0, kb)]
            acc = acc * fade + jnp.dot(v, p.astype(BF16), preferred_element_type=F32)
            return (new, den, acc)

        carry = lax.fori_loop(
            lo[i * groups + r] // kb, (hi[i * groups + r] + kb - 1) // kb, step, carry
        )
    top, den, acc = carry
    out[...] = (acc / den).astype(BF16)
    lse[...] = top + jnp.log(den)


def backward_kernel(
    lo, hi, q_ref, own, oth, rows, out, do_ref, lse, dq, dkv, dkv_oth, kvn, acc,
    *, groups, count, kb
):
    i = pl.program_id(0)

    @pl.when(i == 0)
    def _():
        fill_natural(kvn, own, oth, groups, count, min(count, 256))
        acc[...] = jnp.zeros_like(acc)

    qb = q_ref.shape[1]
    scale = 1.0 / math.sqrt(HD)
    qf = q_ref[...].astype(F32) * scale
    q = qf.astype(BF16)
    do = do_ref[...]
    dof = do.astype(F32)
    delta = jnp.sum(dof * out[...].astype(F32), axis=0, keepdims=True)
    none = jnp.zeros_like(q)
    q_pad = jnp.concatenate([q, none], axis=0)
    do_pad = jnp.concatenate([none, do], axis=0)
    q_nat = jnp.concatenate([qf, jnp.zeros_like(qf)], axis=0).T.astype(BF16)
    do_nat = jnp.concatenate([jnp.zeros_like(dof), dof], axis=0).T.astype(BF16)
    spot = lax.broadcasted_iota(jnp.int32, (kb, qb), 0)
    level = lse[...]
    grad = jnp.zeros((HD, qb), F32)
    for r in range(groups):
        first = rows[r : r + 1, :]
        end = rows[groups + r : groups + r + 1, :]

        def step(j, grad, r=r, first=first, end=end):
            k0 = pl.multiple_of(j * kb, kb)
            at = pl.ds(r * count + k0, kb)
            kv = kvn[at, :]
            s = jnp.dot(kv, q_pad, preferred_element_type=F32)
            dp = jnp.dot(kv, do_pad, preferred_element_type=F32)
            p = jnp.where((spot >= first - k0) & (spot < end - k0), jnp.exp(s - level), 0.0)
            ds = (p * (dp - delta)).astype(BF16)
            acc[at, :] += jnp.dot(ds, q_nat, preferred_element_type=F32) + jnp.dot(
                p.astype(BF16), do_nat, preferred_element_type=F32
            )
            if r == 0:
                k = own[HD : 2 * HD, pl.ds(k0, kb)]
            else:
                k = oth[r - 1, 0:HD, pl.ds(k0, kb)]
            return grad + jnp.dot(k, ds, preferred_element_type=F32)

        grad = lax.fori_loop(
            lo[i * groups + r] // kb, (hi[i * groups + r] + kb - 1) // kb, step, grad
        )
    dq[...] = grad * scale

    @pl.when(i == pl.num_programs(0) - 1)
    def _():
        chunk = min(count, 256)
        for r in range(groups):
            for c in range(count // chunk):
                at = slice(c * chunk, (c + 1) * chunk)
                piece = acc[r * count + c * chunk : r * count + (c + 1) * chunk, :].T
                if r == 0:
                    dkv[:, at] = piece
                else:
                    dkv_oth[r - 1, :, at] = piece.astype(BF16)


def blocks_of(count):
    return math.gcd(count, 256), math.gcd(count, 512)


def whole(shape):
    return pl.BlockSpec(shape, lambda i, *_: (0,) * len(shape))


def attention_forward(lo, hi, own, oth, rows, groups):
    count = own.shape[1]
    qb, kb = blocks_of(count)
    col = lambda height: pl.BlockSpec((height, qb), lambda i, *_: (0, i))
    return pl.pallas_call(
        functools.partial(forward_kernel, groups=groups, count=count, kb=kb),
        grid_spec=pltpu.PrefetchScalarGridSpec(
            num_scalar_prefetch=2,
            grid=(count // qb,),
            in_specs=[col(HD), whole(own.shape), whole(oth.shape), col(rows.shape[0])],
            out_specs=[col(HD), col(1)],
            scratch_shapes=[pltpu.VMEM((groups * count, 2 * HD), BF16)],
        ),
        out_shape=[
            jax.ShapeDtypeStruct((HD, count), BF16),
            jax.ShapeDtypeStruct((1, count), F32),
        ],
        name="attention_forward",
    )(lo, hi, own, own, oth, rows)


def attention_backward(lo, hi, own, oth, rows, out, do, lse, groups):
    count = own.shape[1]
    qb, kb = blocks_of(count)
    col = lambda height: pl.BlockSpec((height, qb), lambda i, *_: (0, i))
    others = (max(groups - 1, 1), 2 * HD, count)
    return pl.pallas_call(
        functools.partial(backward_kernel, groups=groups, count=count, kb=kb),
        grid_spec=pltpu.PrefetchScalarGridSpec(
            num_scalar_prefetch=2,
            grid=(count // qb,),
            in_specs=[
                col(HD), whole(own.shape), whole(oth.shape), col(rows.shape[0]),
                col(HD), col(HD), col(1),
            ],
            out_specs=[col(HD), whole((2 * HD, count)), whole(others)],
            scratch_shapes=[
                pltpu.VMEM((groups * count, 2 * HD), BF16),
                pltpu.VMEM((groups * count, 2 * HD), F32),
            ],
        ),
        out_shape=[
            jax.ShapeDtypeStruct((HD, count), F32),
            jax.ShapeDtypeStruct((2 * HD, count), F32),
            jax.ShapeDtypeStruct(others, BF16),
        ],
        name="attention_backward",
    )(lo, hi, own, own, oth, rows, out, do, lse)


def layer(
    tokens,
    seq_ids,
    attention_norm_gain,
    qkv_weight,
    out_weight,
    feedforward_norm_gain,
    mlp_in_weight,
    mlp_out_weight,
    grad_out,
    *,
    ctx,
    tp,
):
    tok_rows, width = tokens.shape
    local_cols = qkv_weight.shape[2]
    heads_here = local_cols // HD
    hidden_here = mlp_in_weight.shape[2]
    groups = ctx // heads_here
    part = tok_rows // groups
    count = ctx * part
    me = lax.axis_index("ctx")

    def tp_sum(value):
        value = value.astype(BF16)
        if tp == 2:
            other = lax.ppermute(value, "tp", [(0, 1), (1, 0)])
            return value.astype(F32) + other.astype(F32)
        return lax.psum(value, "tp").astype(F32)

    def to_group(value, r):
        pairs = [(i, i // groups * groups + (i + r) % groups) for i in range(ctx)]
        return lax.ppermute(value, "ctx", pairs)

    def for_heads(value):
        rows = value.shape[1]
        value = value.reshape(heads_here, rows, groups, part).transpose(0, 2, 1, 3)
        return value.reshape(ctx, rows, part)

    def to_heads(chunks):
        value = lax.all_to_all(chunks, "ctx", 0, 0)
        return value.transpose(1, 0, 2).reshape(chunks.shape[1], count)

    def for_tokens(value):
        return value.reshape(value.shape[0], ctx, part).transpose(1, 0, 2)

    def to_tokens(chunks):
        rows = chunks.shape[1]
        value = lax.all_to_all(chunks, "ctx", 0, 0)
        value = value.reshape(heads_here, groups, rows, part).transpose(0, 2, 1, 3)
        return value.reshape(heads_here, rows, tok_rows)

    def after(value, *needed):
        return lax.optimization_barrier((value,) + needed)[0]

    bits = list(range(ctx.bit_length() - 1))
    group_bits = list(range(groups.bit_length() - 1))
    head_bits = bits[len(group_bits) :]
    far_bits = bits[2:]

    def spread(bits):
        masks = [
            sum(((m >> at) & 1) << bit for at, bit in enumerate(bits))
            for m in range(1 << len(bits))
        ]
        here = sum((((me >> bit) & 1) << at) for at, bit in enumerate(bits))
        return masks, here

    def pick(pieces, index):
        value = pieces[0]
        for at in range(1, len(pieces)):
            value = jnp.where(index == at, pieces[at], value)
        return value

    def hop(value, mask):
        return lax.ppermute(value, "ctx", [(i, i ^ mask) for i in range(ctx)])

    def deal(value, bits, axis):
        masks, here = spread(bits)
        pieces = jnp.split(value, len(masks), axis=axis)
        return [pick(pieces, here ^ m) for m in range(len(masks))]

    def send_dealt(dealt, bits):
        masks, _ = spread(bits)
        return [dealt[0]] + [hop(dealt[m], masks[m]) for m in range(1, len(masks))]

    def total(pieces):
        return sum(piece.astype(F32) for piece in pieces).astype(BF16)

    def send_all(value, bits):
        masks, _ = spread(bits)
        return [value] + [hop(value, masks[m]) for m in range(1, len(masks))]

    def arrange(pieces, bits, axis):
        _, here = spread(bits)
        return jnp.concatenate(
            [pick(pieces, here ^ at) for at in range(len(pieces))], axis=axis
        )

    def fence(*values):
        return lax.optimization_barrier(values)

    over_cols = (((1,), (1,)), ((), ()))
    over_rows = (((0,), (0,)), ((), ()))
    across = (((0,), (1,)), ((), ()))

    def dot(left, right, dims=(((1,), (0,)), ((), ()))):
        return lax.dot_general(left, right, dims, preferred_element_type=F32)

    input_tokens = tokens.astype(F32)
    attention_standardized, attention_inverse_deviation, attention_normed_input = layer_normalize(
        input_tokens, attention_norm_gain
    )
    first = attention_normed_input.astype(BF16)
    planes = [qkv_weight[:, c] for c in range(3)]
    proj = [dot(plane, first, across).reshape(heads_here, HD, tok_rows) for plane in planes]
    positions = me * tok_rows + jnp.arange(tok_rows, dtype=jnp.int32)
    cosine, sine = rope_tables_t(positions, HD)
    ids = jnp.broadcast_to(seq_ids.astype(BF16)[None, None, :], (heads_here, PAD, tok_rows))
    packed = jnp.concatenate(
        [
            rotate_t(proj[0], cosine, sine).astype(BF16),
            rotate_t(proj[1], cosine, sine).astype(BF16),
            proj[2].astype(BF16),
            ids,
        ],
        axis=1,
    )
    own = to_heads(for_heads(packed))
    if groups > 1:
        oth = jnp.stack([to_group(own[HD:], groups - r) for r in range(1, groups)])
    else:
        oth = own[None, HD:]
    id_own = own[3 * HD]
    id_all = jnp.concatenate([id_own[None], oth[: groups - 1, 2 * HD]], axis=0)
    marks = jnp.arange(SEQS + 1, dtype=F32)
    below = jnp.sum((id_all.astype(F32)[:, None, :] < marks[None, :, None]).astype(jnp.int32), -1)
    first_key = jnp.zeros((groups, count), jnp.int32)
    end_key = jnp.zeros((groups, count), jnp.int32)
    for s in range(SEQS):
        hit = (id_own == s)[None, :]
        first_key = jnp.where(hit, below[:, s : s + 1], first_key)
        end_key = jnp.where(hit, below[:, s + 1 : s + 2], end_key)
    rows = jnp.concatenate([first_key, end_key], axis=0)
    qb, _ = blocks_of(count)
    lo = first_key[:, ::qb].T.reshape(-1)
    hi = end_key[:, qb - 1 :: qb].T.reshape(-1)

    place = me % groups
    parts = after(first, own).reshape(groups, part, width)
    held = [lax.dynamic_index_in_dim(parts, place, 0, keepdims=False)]
    for r in range(1, groups):
        held.append(
            to_group(
                lax.dynamic_index_in_dim(parts, (place + r) % groups, 0, keepdims=False), r
            )
        )
    held = jnp.stack(held)
    held = jnp.concatenate(
        [
            lax.dynamic_index_in_dim(held, (place - c) % groups, 0, keepdims=False)
            for c in range(groups)
        ],
        axis=0,
    )
    first_all = lax.all_gather(
        held,
        "ctx",
        axis=0,
        tiled=True,
        axis_index_groups=[[h * groups + g for h in range(heads_here)] for g in range(groups)],
    )

    att_head, lse = attention_forward(lo, hi, own, oth, rows, groups)
    attended = to_tokens(for_tokens(att_head)).reshape(local_cols, tok_rows)
    attn_part = dot(attended, out_weight, over_rows)
    residual_middle = input_tokens + tp_sum(attn_part)
    feedforward_standardized, feedforward_inverse_deviation, feedforward_normed_input = (
        layer_normalize(residual_middle, feedforward_norm_gain)
    )
    second, first_all = lax.optimization_barrier(
        (feedforward_normed_input.astype(BF16), first_all)
    )
    in_act = mlp_in_weight[:, 0]
    in_gate = mlp_in_weight[:, 1]
    act_in = dot(second, in_act)
    gate = dot(second, in_gate)
    hidden = (gelu_value(act_in) * gate).astype(BF16)
    upstream = grad_out.astype(F32)
    grad_hidden = dot(grad_out, mlp_out_weight, over_cols)
    grad_act = (grad_hidden * gate * gelu_slope(act_in)).astype(BF16)
    grad_gate = (grad_hidden * gelu_value(act_in)).astype(BF16)
    second_part = dot(grad_act, in_act, over_cols) + dot(grad_gate, in_gate, over_cols)
    second_part, second_w, act_w, gate_w, hidden_w = fence(
        second_part.astype(BF16), second, grad_act, grad_gate, hidden
    )
    feedforward_norm_gradient = tp_sum(second_part)
    grad_w_in = jnp.concatenate(
        [dot(act_w, second_w, over_rows), dot(gate_w, second_w, over_rows)], axis=0
    ).astype(BF16)
    grad_w_out = dot(hidden_w, grad_out, over_rows).astype(BF16)
    w_core = deal(grad_w_out, bits[:1], 0)
    feedforward_norm_gradient, grad_w_in, *w_core = fence(
        feedforward_norm_gradient, grad_w_in, *w_core
    )
    sum_in = lax.psum(grad_w_in, "ctx")
    w_core = send_dealt(w_core, bits[:1])
    feedforward_normed_gradient, feedforward_gain_gradient = layer_normalize_backward(
        feedforward_norm_gradient,
        feedforward_standardized,
        feedforward_inverse_deviation,
        feedforward_norm_gain,
    )
    grad_mid = upstream + feedforward_normed_gradient
    grad_mid_b = grad_mid.astype(BF16)
    grad_att = dot(out_weight, grad_mid_b, over_cols).astype(BF16)
    chunks = for_heads(grad_att.reshape(heads_here, HD, tok_rows))
    chunks, w_kept, w_came, late_mid, late_hidden = fence(chunks, *w_core, grad_mid_b, hidden_w)
    do_head = to_heads(chunks)

    w_y = deal(total([w_kept, w_came]), bits[1:2], 1)
    w_y = send_dealt(w_y, bits[1:2])
    grad_w_attn = dot(attended, late_mid).astype(BF16)
    u_core = send_dealt(deal(grad_w_attn, bits[:1], 0), bits[:1])
    ffn_part = dot(late_hidden, mlp_out_weight).astype(BF16)
    do_head, ffn_part, *held_back = fence(do_head, ffn_part, *w_y, *u_core)
    w_y, u_core = held_back[: len(w_y)], held_back[len(w_y) :]

    output_sum = tp_sum(ffn_part)
    w_far = deal(total(w_y), far_bits, 1)
    u_y = deal(total(u_core), bits[1:2], 1)
    do_head, *sends = fence(do_head, *w_far, *u_y)
    w_far = send_dealt(sends[: len(w_far)], far_bits)
    u_y = send_dealt(sends[len(w_far) :], bits[1:2])
    dq, dkv, dkv_oth = attention_backward(
        lo, hi, own, oth, rows, att_head, do_head, lse, groups
    )
    dq, dkv, dkv_oth, output_sum, *held_back = fence(
        dq, dkv, dkv_oth, output_sum, *w_far, *u_y
    )
    w_far, u_y = held_back[: len(w_far)], held_back[len(w_far) :]
    for r in range(1, groups):
        dkv = dkv + to_group(dkv_oth[r - 1], r).astype(F32)
    spots = (
        jnp.arange(ctx, dtype=jnp.int32)[:, None] * tok_rows
        + place * part
        + jnp.arange(part, dtype=jnp.int32)[None, :]
    ).reshape(-1)
    cosine_head, sine_head = rope_tables_t(spots, HD)
    grads = jnp.concatenate(
        [
            unrotate_t(dq[None], cosine_head, sine_head)[0].astype(BF16),
            unrotate_t(dkv[None, :HD], cosine_head, sine_head)[0].astype(BF16),
            dkv[HD:].astype(BF16),
        ],
        axis=0,
    )
    chunks = for_tokens(grads)
    chunks, grads_w = fence(chunks, grads)
    grad_proj = to_tokens(chunks)

    share = dot(grads_w, first_all).astype(BF16)
    share = send_dealt(deal(share, group_bits, 1), group_bits)
    w = total(w_far)
    u_far = send_dealt(deal(total(u_y), far_bits, 1), far_bits)
    output = (residual_middle + output_sum).astype(BF16)
    share = total(share)[None]
    grad_proj, w, share, output = fence(grad_proj, w, share, output)

    first_part = sum(
        dot(grad_proj[:, c * HD : (c + 1) * HD].reshape(local_cols, tok_rows), planes[c], across)
        for c in range(3)
    ).astype(BF16)
    first_part, w, share, *u_far = fence(first_part, w, share, *u_far)
    attention_norm_gradient = tp_sum(first_part)
    u = total(u_far)
    high_bits = [bit for bit in head_bits if bit in far_bits]
    low_bits = [bit for bit in head_bits if bit not in far_bits]
    joint = group_bits == bits[:1] and low_bits == bits[1:2] and high_bits == far_bits
    if joint:
        cut = share.shape[2] // (1 << len(far_bits))
        tall, lanes = (w.shape[0], u.shape[0], HD * 3), share.shape[2]
        bundle = jnp.concatenate(
            [w, u] + [share[0, :, j * cut : (j + 1) * cut] for j in range(lanes // cut)], axis=0
        )
        attention_norm_gradient, *bundle = fence(
            attention_norm_gradient, *send_all(bundle, far_bits)
        )
        _, here = spread(far_bits)
        bundle = [pick(bundle, here ^ at) for at in range(len(bundle))]
        ends = (tall[0], tall[0] + tall[1])
        bundle = jnp.concatenate(
            [
                jnp.concatenate([piece[: ends[0]] for piece in bundle], axis=1),
                jnp.concatenate([piece[ends[0] : ends[1]] for piece in bundle], axis=1),
            ]
            + [
                jnp.concatenate(
                    [
                        piece[ends[1] + j * tall[2] : ends[1] + (j + 1) * tall[2]]
                        for j in range(lanes // cut)
                    ],
                    axis=1,
                )
                for piece in bundle
            ],
            axis=0,
        )
        bundle = send_all(bundle, bits[1:2])
    else:
        share = arrange(send_all(share, high_bits), high_bits, 0)
        share = arrange(send_all(share, low_bits), low_bits, 0)
        share = arrange(send_all(share, group_bits), group_bits, 2)
        w = arrange(send_all(w, far_bits), far_bits, 1)
        w = arrange(send_all(w, bits[1:2]), bits[1:2], 1)
        w = arrange(send_all(w, bits[:1]), bits[:1], 0)
        u = arrange(send_all(u, far_bits), far_bits, 1)
        u = arrange(send_all(u, bits[1:2]), bits[1:2], 1)
        u = arrange(send_all(u, bits[:1]), bits[:1], 0)
    attention_normed_gradient, attention_gain_gradient = layer_normalize_backward(
        attention_norm_gradient,
        attention_standardized,
        attention_inverse_deviation,
        attention_norm_gain,
    )
    grad_tokens = grad_mid + attention_normed_gradient
    gains = jnp.stack([attention_gain_gradient, feedforward_gain_gradient])
    gains = sum(send_all(gains, bits[:1]))
    gains = sum(send_all(gains, bits[1:2]))
    masks, here = spread(far_bits)
    gains = send_all(gains, far_bits)
    if joint:
        grad_tokens, *held_back = fence(grad_tokens, *gains, *bundle)
        gains, bundle = held_back[: len(gains)], held_back[len(gains) :]
        _, side = spread(bits[1:2])
        bundle = jnp.stack([pick(bundle, side ^ at) for at in range(2)])
        bundle = send_all(bundle, bits[:1])
        _, side = spread(bits[:1])
        bundle = jnp.stack([pick(bundle, side ^ at) for at in range(2)])
        w = bundle[:, :, : ends[0]].transpose(0, 2, 1, 3).reshape(hidden_here, width)
        u = bundle[:, :, ends[0] : ends[1]].transpose(0, 2, 1, 3).reshape(local_cols, width)
        share = bundle[:, :, ends[1] :].reshape(2, 2, len(masks), tall[2], lanes)
        share = share.transpose(1, 2, 3, 0, 4)
    gains = sum(pick(gains, here ^ at) for at in range(len(masks)))
    sum_in = after(sum_in, bundle if joint else share, w, u, grad_tokens, gains)
    sum_qkv = (
        share.reshape(1 << len(low_bits), 1 << len(high_bits), 3, HD, width)
        .transpose(4, 2, 1, 0, 3)
        .reshape(width, 3, local_cols)
    )
    return (
        output,
        grad_tokens,
        gains[0],
        sum_qkv.astype(F32),
        u.astype(F32),
        gains[1],
        sum_in.reshape(2, hidden_here, width).transpose(2, 0, 1).astype(F32),
        w.astype(F32),
    )


def solution(mesh):
    return jax.shard_map(
        functools.partial(layer, ctx=mesh.shape["ctx"], tp=mesh.shape["tp"]),
        mesh=mesh,
        in_specs=(
            P("ctx", None),
            P("ctx"),
            P(),
            P(None, None, "tp"),
            P("tp", None),
            P(),
            P(None, None, "tp"),
            P("tp", None),
            P("ctx", None),
        ),
        out_specs=(
            P("ctx", None),
            P("ctx", None),
            P(),
            P(None, None, "tp"),
            P("tp", None),
            P(),
            P(None, None, "tp"),
            P("tp", None),
        ),
        check_vma=False,
    )
```

```python
import functools
import math

import jax
import jax.numpy as jnp
from jax import lax
from jax.experimental import pallas as pl
from jax.experimental.pallas import tpu as pltpu
from jax.sharding import PartitionSpec as P

HD = 64
EPS = 1e-05
BASE = 160000.0
MASKED = -1e30
ROOT_HALF = 0.7071067811865476
INV_ROOT_TWO_PI = 0.3989422804014327
SEQS = 4
F32 = jnp.float32
BF16 = jnp.bfloat16
PAD = 16


def layer_normalize(values_in, norm_gain_vector):
    token_average = jnp.mean(values_in, axis=-1, keepdims=True)
    centered_input = values_in - token_average
    inverse_deviation = lax.rsqrt(
        jnp.mean(centered_input * centered_input, axis=-1, keepdims=True) + EPS
    )
    standardized_input = centered_input * inverse_deviation
    return (standardized_input, inverse_deviation, standardized_input * norm_gain_vector)


def layer_normalize_backward(
    output_gradient, standardized_input, inverse_deviation, norm_gain_vector
):
    normalized_gradient = output_gradient * norm_gain_vector
    correction_term = jnp.mean(
        normalized_gradient, axis=-1, keepdims=True
    ) + standardized_input * jnp.mean(
        normalized_gradient * standardized_input, axis=-1, keepdims=True
    )
    return (
        inverse_deviation * (normalized_gradient - correction_term),
        jnp.sum(output_gradient * standardized_input, axis=0),
    )


def gelu_value(v):
    return v * 0.5 * (1.0 + lax.erf(v * ROOT_HALF))


def gelu_slope(v):
    return 0.5 * (1.0 + lax.erf(v * ROOT_HALF)) + v * jnp.exp(-0.5 * v * v) * INV_ROOT_TWO_PI


def rope_tables_t(positions, head_size):
    half = head_size // 2
    inverse = BASE ** (-(jnp.arange(half, dtype=F32) * (2.0 / head_size)))
    angle = inverse[:, None] * positions.astype(F32)[None, :]
    return (jnp.cos(angle), jnp.sin(angle))


def rotate_t(field, cosine, sine):
    half = field.shape[1] // 2
    one, two = field[:, :half], field[:, half:]
    return jnp.concatenate([one * cosine - two * sine, two * cosine + one * sine], axis=1)


def unrotate_t(grad, cosine, sine):
    half = grad.shape[1] // 2
    one, two = grad[:, :half], grad[:, half:]
    return jnp.concatenate([one * cosine + two * sine, two * cosine - one * sine], axis=1)


def fill_natural(kvn, own, oth, groups, count, chunk):
    for r in range(groups):
        for c in range(count // chunk):
            at = slice(c * chunk, (c + 1) * chunk)
            if r == 0:
                piece = own[HD : 3 * HD, at]
            else:
                piece = oth[r - 1, 0 : 2 * HD, at]
            kvn[r * count + c * chunk : r * count + (c + 1) * chunk, :] = (
                piece.astype(F32).T.astype(BF16)
            )


def forward_kernel(lo, hi, q_ref, own, oth, rows, out, lse, kvn, *, groups, count, kb):
    i = pl.program_id(0)

    @pl.when(i == 0)
    def _():
        fill_natural(kvn, own, oth, groups, count, min(count, 256))

    qb = q_ref.shape[1]
    q = (q_ref[...].astype(F32) * (1.0 / math.sqrt(HD))).astype(BF16)
    q = jnp.concatenate([q, jnp.zeros_like(q)], axis=0)
    spot = lax.broadcasted_iota(jnp.int32, (kb, qb), 0)
    carry = (
        jnp.full((1, qb), MASKED, F32),
        jnp.zeros((1, qb), F32),
        jnp.zeros((HD, qb), F32),
    )
    for r in range(groups):
        first = rows[r : r + 1, :]
        end = rows[groups + r : groups + r + 1, :]

        def step(j, carry, r=r, first=first, end=end):
            top, den, acc = carry
            k0 = pl.multiple_of(j * kb, kb)
            s = jnp.dot(kvn[pl.ds(r * count + k0, kb), :], q, preferred_element_type=F32)
            s = jnp.where((spot >= first - k0) & (spot < end - k0), s, MASKED)
            new = jnp.maximum(top, jnp.max(s, axis=0, keepdims=True))
            p = jnp.exp(s - new)
            fade = jnp.exp(top - new)
            den = den * fade + jnp.sum(p, axis=0, keepdims=True)
            if r == 0:
                v = own[2 * HD : 3 * HD, pl.ds(k0, kb)]
            else:
                v = oth[r - 1, HD : 2 * HD, pl.ds(k0, kb)]
            acc = acc * fade + jnp.dot(v, p.astype(BF16), preferred_element_type=F32)
            return (new, den, acc)

        carry = lax.fori_loop(
            lo[i * groups + r] // kb, (hi[i * groups + r] + kb - 1) // kb, step, carry
        )
    top, den, acc = carry
    out[...] = (acc / den).astype(BF16)
    lse[...] = top + jnp.log(den)


def backward_kernel(
    lo, hi, q_ref, own, oth, rows, out, do_ref, lse, dq, dkv, dkv_oth, kvn, acc,
    *, groups, count, kb
):
    i = pl.program_id(0)

    @pl.when(i == 0)
    def _():
        fill_natural(kvn, own, oth, groups, count, min(count, 256))
        acc[...] = jnp.zeros_like(acc)

    qb = q_ref.shape[1]
    scale = 1.0 / math.sqrt(HD)
    qf = q_ref[...].astype(F32) * scale
    q = qf.astype(BF16)
    do = do_ref[...]
    dof = do.astype(F32)
    delta = jnp.sum(dof * out[...].astype(F32), axis=0, keepdims=True)
    none = jnp.zeros_like(q)
    q_pad = jnp.concatenate([q, none], axis=0)
    do_pad = jnp.concatenate([none, do], axis=0)
    q_nat = jnp.concatenate([qf, jnp.zeros_like(qf)], axis=0).T.astype(BF16)
    do_nat = jnp.concatenate([jnp.zeros_like(dof), dof], axis=0).T.astype(BF16)
    spot = lax.broadcasted_iota(jnp.int32, (kb, qb), 0)
    level = lse[...]
    grad = jnp.zeros((HD, qb), F32)
    for r in range(groups):
        first = rows[r : r + 1, :]
        end = rows[groups + r : groups + r + 1, :]

        def step(j, grad, r=r, first=first, end=end):
            k0 = pl.multiple_of(j * kb, kb)
            at = pl.ds(r * count + k0, kb)
            kv = kvn[at, :]
            s = jnp.dot(kv, q_pad, preferred_element_type=F32)
            dp = jnp.dot(kv, do_pad, preferred_element_type=F32)
            p = jnp.where((spot >= first - k0) & (spot < end - k0), jnp.exp(s - level), 0.0)
            ds = (p * (dp - delta)).astype(BF16)
            acc[at, :] += jnp.dot(ds, q_nat, preferred_element_type=F32) + jnp.dot(
                p.astype(BF16), do_nat, preferred_element_type=F32
            )
            if r == 0:
                k = own[HD : 2 * HD, pl.ds(k0, kb)]
            else:
                k = oth[r - 1, 0:HD, pl.ds(k0, kb)]
            return grad + jnp.dot(k, ds, preferred_element_type=F32)

        grad = lax.fori_loop(
            lo[i * groups + r] // kb, (hi[i * groups + r] + kb - 1) // kb, step, grad
        )
    dq[...] = grad * scale

    @pl.when(i == pl.num_programs(0) - 1)
    def _():
        chunk = min(count, 256)
        for r in range(groups):
            for c in range(count // chunk):
                at = slice(c * chunk, (c + 1) * chunk)
                piece = acc[r * count + c * chunk : r * count + (c + 1) * chunk, :].T
                if r == 0:
                    dkv[:, at] = piece
                else:
                    dkv_oth[r - 1, :, at] = piece.astype(BF16)


def place_kernel(where, near, near_y, over, over_y, *outs, spans, far):
    c = pl.program_id(0)

    def put(same, other):
        for y in range(2):
            for j in range(far):
                m = where[2] ^ j

                def write(source, y=y, j=j, m=m):
                    base = 0
                    for out, rows in zip(outs, spans):
                        if len(out.shape) == 2:
                            lanes = source.shape[2]
                            at = (y * far + j) * lanes
                            out[:, at : at + lanes] = source[m, base : base + rows, :].astype(F32)
                        base += rows

                @pl.when(where[1] == y)
                def _():
                    write(same)

                @pl.when(where[1] != y)
                def _():
                    write(other)

        base = 0
        for out, rows in zip(outs, spans):
            if len(out.shape) == 3:
                lanes = same.shape[2]

                def turn(low, high, out=out, base=base):
                    for j in range(far):
                        m = where[2] ^ j
                        for b in range(far):
                            for part in range(3):
                                at = base + (b * 3 + part) * HD
                                pair = jnp.concatenate(
                                    [
                                        low[m, at : at + HD, :].astype(F32),
                                        high[m, at : at + HD, :].astype(F32),
                                    ],
                                    axis=0,
                                )
                                out[
                                    part,
                                    b * lanes : (b + 1) * lanes,
                                    j * 2 * HD : (j + 1) * 2 * HD,
                                ] = pair.T

                @pl.when(where[1] == 0)
                def _():
                    turn(same, other)

                @pl.when(where[1] == 1)
                def _():
                    turn(other, same)
            base += rows

    @pl.when(where[0] == c)
    def _():
        put(near, near_y)

    @pl.when(where[0] != c)
    def _():
        put(over, over_y)


def place_sums(where, stacks, spans, shapes):
    far = stacks[0].shape[0]
    specs = [
        pl.BlockSpec((shape[0] // 2, shape[1]), lambda c, *_: (c, 0))
        if len(shape) == 2
        else pl.BlockSpec((shape[0], shape[1] // 2, shape[2]), lambda c, *_: (0, c, 0))
        for shape in shapes
    ]
    return pl.pallas_call(
        functools.partial(place_kernel, spans=spans, far=far),
        grid_spec=pltpu.PrefetchScalarGridSpec(
            num_scalar_prefetch=1,
            grid=(2,),
            in_specs=[whole(stack.shape) for stack in stacks],
            out_specs=specs,
        ),
        out_shape=[jax.ShapeDtypeStruct(shape, F32) for shape in shapes],
        name="place_sums",
    )(where, *stacks)


def blocks_of(count):
    return math.gcd(count, 256), math.gcd(count, 512)


def whole(shape):
    return pl.BlockSpec(shape, lambda i, *_: (0,) * len(shape))


def attention_forward(lo, hi, own, oth, rows, groups):
    count = own.shape[1]
    qb, kb = blocks_of(count)
    col = lambda height: pl.BlockSpec((height, qb), lambda i, *_: (0, i))
    return pl.pallas_call(
        functools.partial(forward_kernel, groups=groups, count=count, kb=kb),
        grid_spec=pltpu.PrefetchScalarGridSpec(
            num_scalar_prefetch=2,
            grid=(count // qb,),
            in_specs=[col(HD), whole(own.shape), whole(oth.shape), col(rows.shape[0])],
            out_specs=[col(HD), col(1)],
            scratch_shapes=[pltpu.VMEM((groups * count, 2 * HD), BF16)],
        ),
        out_shape=[
            jax.ShapeDtypeStruct((HD, count), BF16),
            jax.ShapeDtypeStruct((1, count), F32),
        ],
        name="attention_forward",
    )(lo, hi, own, own, oth, rows)


def attention_backward(lo, hi, own, oth, rows, out, do, lse, groups):
    count = own.shape[1]
    qb, kb = blocks_of(count)
    col = lambda height: pl.BlockSpec((height, qb), lambda i, *_: (0, i))
    others = (max(groups - 1, 1), 2 * HD, count)
    return pl.pallas_call(
        functools.partial(backward_kernel, groups=groups, count=count, kb=kb),
        grid_spec=pltpu.PrefetchScalarGridSpec(
            num_scalar_prefetch=2,
            grid=(count // qb,),
            in_specs=[
                col(HD), whole(own.shape), whole(oth.shape), col(rows.shape[0]),
                col(HD), col(HD), col(1),
            ],
            out_specs=[col(HD), whole((2 * HD, count)), whole(others)],
            scratch_shapes=[
                pltpu.VMEM((groups * count, 2 * HD), BF16),
                pltpu.VMEM((groups * count, 2 * HD), F32),
            ],
        ),
        out_shape=[
            jax.ShapeDtypeStruct((HD, count), F32),
            jax.ShapeDtypeStruct((2 * HD, count), F32),
            jax.ShapeDtypeStruct(others, BF16),
        ],
        name="attention_backward",
    )(lo, hi, own, own, oth, rows, out, do, lse)


def layer(
    tokens,
    seq_ids,
    attention_norm_gain,
    qkv_weight,
    out_weight,
    feedforward_norm_gain,
    mlp_in_weight,
    mlp_out_weight,
    grad_out,
    *,
    ctx,
    tp,
):
    tok_rows, width = tokens.shape
    local_cols = qkv_weight.shape[2]
    heads_here = local_cols // HD
    hidden_here = mlp_in_weight.shape[2]
    groups = ctx // heads_here
    part = tok_rows // groups
    count = ctx * part
    me = lax.axis_index("ctx")

    def tp_sum(value):
        value = value.astype(BF16)
        if tp == 2:
            other = lax.ppermute(value, "tp", [(0, 1), (1, 0)])
            return value.astype(F32) + other.astype(F32)
        return lax.psum(value, "tp").astype(F32)

    def to_group(value, r):
        pairs = [(i, i // groups * groups + (i + r) % groups) for i in range(ctx)]
        return lax.ppermute(value, "ctx", pairs)

    def for_heads(value):
        rows = value.shape[1]
        value = value.reshape(heads_here, rows, groups, part).transpose(0, 2, 1, 3)
        return value.reshape(ctx, rows, part)

    def to_heads(chunks):
        value = lax.all_to_all(chunks, "ctx", 0, 0)
        return value.transpose(1, 0, 2).reshape(chunks.shape[1], count)

    def for_tokens(value):
        return value.reshape(value.shape[0], ctx, part).transpose(1, 0, 2)

    def to_tokens(chunks):
        rows = chunks.shape[1]
        value = lax.all_to_all(chunks, "ctx", 0, 0)
        value = value.reshape(heads_here, groups, rows, part).transpose(0, 2, 1, 3)
        return value.reshape(heads_here, rows, tok_rows)

    def after(value, *needed):
        return lax.optimization_barrier((value,) + needed)[0]

    bits = list(range(ctx.bit_length() - 1))
    group_bits = list(range(groups.bit_length() - 1))
    head_bits = bits[len(group_bits) :]
    far_bits = bits[2:]

    def spread(bits):
        masks = [
            sum(((m >> at) & 1) << bit for at, bit in enumerate(bits))
            for m in range(1 << len(bits))
        ]
        here = sum((((me >> bit) & 1) << at) for at, bit in enumerate(bits))
        return masks, here

    def pick(pieces, index):
        value = pieces[0]
        for at in range(1, len(pieces)):
            value = jnp.where(index == at, pieces[at], value)
        return value

    def hop(value, mask):
        return lax.ppermute(value, "ctx", [(i, i ^ mask) for i in range(ctx)])

    def deal(value, bits, axis):
        masks, here = spread(bits)
        pieces = jnp.split(value, len(masks), axis=axis)
        return [pick(pieces, here ^ m) for m in range(len(masks))]

    def send_dealt(dealt, bits):
        masks, _ = spread(bits)
        return [dealt[0]] + [hop(dealt[m], masks[m]) for m in range(1, len(masks))]

    def total(pieces):
        return sum(piece.astype(F32) for piece in pieces).astype(BF16)

    def send_all(value, bits):
        masks, _ = spread(bits)
        return [value] + [hop(value, masks[m]) for m in range(1, len(masks))]

    def arrange(pieces, bits, axis):
        _, here = spread(bits)
        return jnp.concatenate(
            [pick(pieces, here ^ at) for at in range(len(pieces))], axis=axis
        )

    def fence(*values):
        return lax.optimization_barrier(values)

    over_cols = (((1,), (1,)), ((), ()))
    over_rows = (((0,), (0,)), ((), ()))
    across = (((0,), (1,)), ((), ()))

    def dot(left, right, dims=(((1,), (0,)), ((), ()))):
        return lax.dot_general(left, right, dims, preferred_element_type=F32)

    input_tokens = tokens.astype(F32)
    attention_standardized, attention_inverse_deviation, attention_normed_input = layer_normalize(
        input_tokens, attention_norm_gain
    )
    first = attention_normed_input.astype(BF16)
    planes = [qkv_weight[:, c] for c in range(3)]
    proj = [dot(plane, first, across).reshape(heads_here, HD, tok_rows) for plane in planes]
    positions = me * tok_rows + jnp.arange(tok_rows, dtype=jnp.int32)
    cosine, sine = rope_tables_t(positions, HD)
    ids = jnp.broadcast_to(seq_ids.astype(BF16)[None, None, :], (heads_here, PAD, tok_rows))
    packed = jnp.concatenate(
        [
            rotate_t(proj[0], cosine, sine).astype(BF16),
            rotate_t(proj[1], cosine, sine).astype(BF16),
            proj[2].astype(BF16),
            ids,
        ],
        axis=1,
    )
    own = to_heads(for_heads(packed))
    if groups > 1:
        oth = jnp.stack([to_group(own[HD:], groups - r) for r in range(1, groups)])
    else:
        oth = own[None, HD:]
    id_own = own[3 * HD]
    id_all = jnp.concatenate([id_own[None], oth[: groups - 1, 2 * HD]], axis=0)
    marks = jnp.arange(SEQS + 1, dtype=F32)
    below = jnp.sum((id_all.astype(F32)[:, None, :] < marks[None, :, None]).astype(jnp.int32), -1)
    first_key = jnp.zeros((groups, count), jnp.int32)
    end_key = jnp.zeros((groups, count), jnp.int32)
    for s in range(SEQS):
        hit = (id_own == s)[None, :]
        first_key = jnp.where(hit, below[:, s : s + 1], first_key)
        end_key = jnp.where(hit, below[:, s + 1 : s + 2], end_key)
    rows = jnp.concatenate([first_key, end_key], axis=0)
    qb, _ = blocks_of(count)
    lo = first_key[:, ::qb].T.reshape(-1)
    hi = end_key[:, qb - 1 :: qb].T.reshape(-1)

    place = me % groups
    parts = after(first, own).reshape(groups, part, width)
    held = [lax.dynamic_index_in_dim(parts, place, 0, keepdims=False)]
    for r in range(1, groups):
        held.append(
            to_group(
                lax.dynamic_index_in_dim(parts, (place + r) % groups, 0, keepdims=False), r
            )
        )
    held = jnp.stack(held)
    held = jnp.concatenate(
        [
            lax.dynamic_index_in_dim(held, (place - c) % groups, 0, keepdims=False)
            for c in range(groups)
        ],
        axis=0,
    )
    first_all = lax.all_gather(
        held,
        "ctx",
        axis=0,
        tiled=True,
        axis_index_groups=[[h * groups + g for h in range(heads_here)] for g in range(groups)],
    )

    att_head, lse = attention_forward(lo, hi, own, oth, rows, groups)
    attended = to_tokens(for_tokens(att_head)).reshape(local_cols, tok_rows)
    attn_part = dot(attended, out_weight, over_rows)
    residual_middle = input_tokens + tp_sum(attn_part)
    feedforward_standardized, feedforward_inverse_deviation, feedforward_normed_input = (
        layer_normalize(residual_middle, feedforward_norm_gain)
    )
    second, first_all = lax.optimization_barrier(
        (feedforward_normed_input.astype(BF16), first_all)
    )
    in_act = mlp_in_weight[:, 0]
    in_gate = mlp_in_weight[:, 1]
    act_in = dot(second, in_act)
    gate = dot(second, in_gate)
    hidden = (gelu_value(act_in) * gate).astype(BF16)
    upstream = grad_out.astype(F32)
    grad_hidden = dot(grad_out, mlp_out_weight, over_cols)
    grad_act = (grad_hidden * gate * gelu_slope(act_in)).astype(BF16)
    grad_gate = (grad_hidden * gelu_value(act_in)).astype(BF16)
    second_part = dot(grad_act, in_act, over_cols) + dot(grad_gate, in_gate, over_cols)
    second_part, second_w, act_w, gate_w, hidden_w = fence(
        second_part.astype(BF16), second, grad_act, grad_gate, hidden
    )
    feedforward_norm_gradient = tp_sum(second_part)
    grad_w_in = jnp.concatenate(
        [dot(act_w, second_w, over_rows), dot(gate_w, second_w, over_rows)], axis=0
    ).astype(BF16)
    grad_w_out = dot(hidden_w, grad_out, over_rows).astype(BF16)
    w_core = deal(grad_w_out, bits[:1], 0)
    feedforward_norm_gradient, grad_w_in, *w_core = fence(
        feedforward_norm_gradient, grad_w_in, *w_core
    )
    sum_in = lax.psum(grad_w_in, "ctx")
    w_core = send_dealt(w_core, bits[:1])
    feedforward_normed_gradient, feedforward_gain_gradient = layer_normalize_backward(
        feedforward_norm_gradient,
        feedforward_standardized,
        feedforward_inverse_deviation,
        feedforward_norm_gain,
    )
    grad_mid = upstream + feedforward_normed_gradient
    grad_mid_b = grad_mid.astype(BF16)
    grad_att = dot(out_weight, grad_mid_b, over_cols).astype(BF16)
    chunks = for_heads(grad_att.reshape(heads_here, HD, tok_rows))
    chunks, w_kept, w_came, late_mid, late_hidden = fence(chunks, *w_core, grad_mid_b, hidden_w)
    do_head = to_heads(chunks)

    w_y = deal(total([w_kept, w_came]), bits[1:2], 1)
    w_y = send_dealt(w_y, bits[1:2])
    grad_w_attn = dot(attended, late_mid).astype(BF16)
    u_core = send_dealt(deal(grad_w_attn, bits[:1], 0), bits[:1])
    ffn_part = dot(late_hidden, mlp_out_weight).astype(BF16)
    do_head, ffn_part, *held_back = fence(do_head, ffn_part, *w_y, *u_core)
    w_y, u_core = held_back[: len(w_y)], held_back[len(w_y) :]

    output_sum = tp_sum(ffn_part)
    w_far = deal(total(w_y), far_bits, 1)
    u_y = deal(total(u_core), bits[1:2], 1)
    do_head, *sends = fence(do_head, *w_far, *u_y)
    w_far = send_dealt(sends[: len(w_far)], far_bits)
    u_y = send_dealt(sends[len(w_far) :], bits[1:2])
    dq, dkv, dkv_oth = attention_backward(
        lo, hi, own, oth, rows, att_head, do_head, lse, groups
    )
    dq, dkv, dkv_oth, output_sum, *held_back = fence(
        dq, dkv, dkv_oth, output_sum, *w_far, *u_y
    )
    w_far, u_y = held_back[: len(w_far)], held_back[len(w_far) :]
    for r in range(1, groups):
        dkv = dkv + to_group(dkv_oth[r - 1], r).astype(F32)
    spots = (
        jnp.arange(ctx, dtype=jnp.int32)[:, None] * tok_rows
        + place * part
        + jnp.arange(part, dtype=jnp.int32)[None, :]
    ).reshape(-1)
    cosine_head, sine_head = rope_tables_t(spots, HD)
    grads = jnp.concatenate(
        [
            unrotate_t(dq[None], cosine_head, sine_head)[0].astype(BF16),
            unrotate_t(dkv[None, :HD], cosine_head, sine_head)[0].astype(BF16),
            dkv[HD:].astype(BF16),
        ],
        axis=0,
    )
    chunks = for_tokens(grads)
    chunks, grads_w = fence(chunks, grads)
    grad_proj = to_tokens(chunks)

    share = dot(grads_w, first_all).astype(BF16)
    share = send_dealt(deal(share, group_bits, 1), group_bits)
    high_bits = [bit for bit in head_bits if bit in far_bits]
    low_bits = [bit for bit in head_bits if bit not in far_bits]
    joint = group_bits == bits[:1] and low_bits == bits[1:2] and high_bits == far_bits
    w = total(w_far)
    if joint:
        w_stack = send_all(after(w, chunks), far_bits)
    u_far = send_dealt(deal(total(u_y), far_bits, 1), far_bits)
    output = (residual_middle + output_sum).astype(BF16)
    share = total(share)[None]
    grad_proj, share, output = fence(grad_proj, share, output)

    first_part = sum(
        dot(grad_proj[:, c * HD : (c + 1) * HD].reshape(local_cols, tok_rows), planes[c], across)
        for c in range(3)
    ).astype(BF16)
    first_part, share, *u_far = fence(first_part, share, *u_far)
    attention_norm_gradient = tp_sum(first_part)
    u = total(u_far)
    if joint:
        cut = share.shape[2] // (1 << len(far_bits))
        u_stack = jnp.concatenate(
            [u] + [share[0, :, at : at + cut] for at in range(0, share.shape[2], cut)], axis=0
        )
        u_stack = send_all(u_stack, far_bits)
        w_stack = jnp.stack(w_stack)
        w_y, w_over = hop(w_stack, 2), hop(w_stack, 1)
        attention_norm_gradient, w_y, w_over = fence(attention_norm_gradient, w_y, w_over)
        w_stacks = [w_stack, w_y, w_over, hop(w_y, 1)]
        u_stack = jnp.stack(u_stack)
        u_y, u_over = hop(u_stack, 2), hop(u_stack, 1)
    else:
        share = arrange(send_all(share, high_bits), high_bits, 0)
        share = arrange(send_all(share, low_bits), low_bits, 0)
        share = arrange(send_all(share, group_bits), group_bits, 2)
        w = arrange(send_all(w, far_bits), far_bits, 1)
        w = arrange(send_all(w, bits[1:2]), bits[1:2], 1)
        w = arrange(send_all(w, bits[:1]), bits[:1], 0)
        u = arrange(send_all(u, far_bits), far_bits, 1)
        u = arrange(send_all(u, bits[1:2]), bits[1:2], 1)
        u = arrange(send_all(u, bits[:1]), bits[:1], 0)
    attention_normed_gradient, attention_gain_gradient = layer_normalize_backward(
        attention_norm_gradient,
        attention_standardized,
        attention_inverse_deviation,
        attention_norm_gain,
    )
    grad_tokens = grad_mid + attention_normed_gradient
    gains = jnp.stack([attention_gain_gradient, feedforward_gain_gradient])
    gains = sum(send_all(gains, bits[:1]))
    gains = sum(send_all(gains, bits[1:2]))
    masks, here = spread(far_bits)
    gains = send_all(gains, far_bits)
    gains = sum(pick(gains, here ^ at) for at in range(len(masks)))
    if joint:
        here = jnp.stack([me & 1, (me >> 1) & 1, me >> 2]).astype(jnp.int32)
        (w,) = place_sums(here, w_stacks, [w.shape[0]], [(hidden_here, width)])
        gains, grad_tokens, w, u_y, u_over = fence(gains, grad_tokens, w, u_y, u_over)
        u, sum_qkv = place_sums(
            here,
            [u_stack, u_y, u_over, hop(u_y, 1)],
            [u.shape[0], u_stack.shape[1] - u.shape[0]],
            [(local_cols, width), (3, width, local_cols)],
        )
        sum_qkv = sum_qkv.transpose(1, 0, 2)
    else:
        sum_qkv = (
            share.reshape(1 << len(low_bits), 1 << len(high_bits), 3, HD, width)
            .transpose(4, 2, 1, 0, 3)
            .reshape(width, 3, local_cols)
        )
    sum_in = after(sum_in, sum_qkv, w, u, grad_tokens, gains)
    return (
        output,
        grad_tokens,
        gains[0],
        sum_qkv.astype(F32),
        u.astype(F32),
        gains[1],
        sum_in.reshape(2, hidden_here, width).transpose(2, 0, 1).astype(F32),
        w.astype(F32),
    )


def solution(mesh):
    return jax.shard_map(
        functools.partial(layer, ctx=mesh.shape["ctx"], tp=mesh.shape["tp"]),
        mesh=mesh,
        in_specs=(
            P("ctx", None),
            P("ctx"),
            P(),
            P(None, None, "tp"),
            P("tp", None),
            P(),
            P(None, None, "tp"),
            P("tp", None),
            P("ctx", None),
        ),
        out_specs=(
            P("ctx", None),
            P("ctx", None),
            P(),
            P(None, None, "tp"),
            P("tp", None),
            P(),
            P(None, None, "tp"),
            P("tp", None),
        ),
        check_vma=False,
    )
```

```python
import functools
import math

import jax
import jax.numpy as jnp
from jax import lax
from jax.experimental import pallas as pl
from jax.experimental.pallas import tpu as pltpu
from jax.sharding import PartitionSpec as P

HD = 64
EPS = 1e-05
BASE = 160000.0
MASKED = -1e30
ROOT_HALF = 0.7071067811865476
INV_ROOT_TWO_PI = 0.3989422804014327
SEQS = 4
F32 = jnp.float32
BF16 = jnp.bfloat16
PAD = 16


def layer_normalize(values_in, norm_gain_vector):
    token_average = jnp.mean(values_in, axis=-1, keepdims=True)
    centered_input = values_in - token_average
    inverse_deviation = lax.rsqrt(
        jnp.mean(centered_input * centered_input, axis=-1, keepdims=True) + EPS
    )
    standardized_input = centered_input * inverse_deviation
    return (standardized_input, inverse_deviation, standardized_input * norm_gain_vector)


def layer_normalize_backward(
    output_gradient, standardized_input, inverse_deviation, norm_gain_vector
):
    normalized_gradient = output_gradient * norm_gain_vector
    correction_term = jnp.mean(
        normalized_gradient, axis=-1, keepdims=True
    ) + standardized_input * jnp.mean(
        normalized_gradient * standardized_input, axis=-1, keepdims=True
    )
    return (
        inverse_deviation * (normalized_gradient - correction_term),
        jnp.sum(output_gradient * standardized_input, axis=0),
    )


def gelu_value(v):
    return v * 0.5 * (1.0 + lax.erf(v * ROOT_HALF))


def gelu_slope(v):
    return 0.5 * (1.0 + lax.erf(v * ROOT_HALF)) + v * jnp.exp(-0.5 * v * v) * INV_ROOT_TWO_PI


def rope_tables_t(positions, head_size):
    half = head_size // 2
    inverse = BASE ** (-(jnp.arange(half, dtype=F32) * (2.0 / head_size)))
    angle = inverse[:, None] * positions.astype(F32)[None, :]
    return (jnp.cos(angle), jnp.sin(angle))


def rotate_t(field, cosine, sine):
    half = field.shape[1] // 2
    one, two = field[:, :half], field[:, half:]
    return jnp.concatenate([one * cosine - two * sine, two * cosine + one * sine], axis=1)


def unrotate_t(grad, cosine, sine):
    half = grad.shape[1] // 2
    one, two = grad[:, :half], grad[:, half:]
    return jnp.concatenate([one * cosine + two * sine, two * cosine - one * sine], axis=1)


def fill_natural(kvn, own, oth, groups, count, chunk):
    for r in range(groups):
        for c in range(count // chunk):
            at = slice(c * chunk, (c + 1) * chunk)
            if r == 0:
                piece = own[HD : 3 * HD, at]
            else:
                piece = oth[r - 1, 0 : 2 * HD, at]
            kvn[r * count + c * chunk : r * count + (c + 1) * chunk, :] = (
                piece.astype(F32).T.astype(BF16)
            )


def forward_kernel(lo, hi, q_ref, own, oth, rows, out, lse, kvn, *, groups, count, kb):
    i = pl.program_id(0)

    @pl.when(i == 0)
    def _():
        fill_natural(kvn, own, oth, groups, count, min(count, 256))

    qb = q_ref.shape[1]
    q = (q_ref[...].astype(F32) * (1.0 / math.sqrt(HD))).astype(BF16)
    q = jnp.concatenate([q, jnp.zeros_like(q)], axis=0)
    spot = lax.broadcasted_iota(jnp.int32, (kb, qb), 0)
    carry = (
        jnp.full((1, qb), MASKED, F32),
        jnp.zeros((1, qb), F32),
        jnp.zeros((HD, qb), F32),
    )
    for r in range(groups):
        first = rows[r : r + 1, :]
        end = rows[groups + r : groups + r + 1, :]

        def step(j, carry, r=r, first=first, end=end):
            top, den, acc = carry
            k0 = pl.multiple_of(j * kb, kb)
            s = jnp.dot(kvn[pl.ds(r * count + k0, kb), :], q, preferred_element_type=F32)
            s = jnp.where((spot >= first - k0) & (spot < end - k0), s, MASKED)
            new = jnp.maximum(top, jnp.max(s, axis=0, keepdims=True))
            p = jnp.exp(s - new)
            fade = jnp.exp(top - new)
            den = den * fade + jnp.sum(p, axis=0, keepdims=True)
            if r == 0:
                v = own[2 * HD : 3 * HD, pl.ds(k0, kb)]
            else:
                v = oth[r - 1, HD : 2 * HD, pl.ds(k0, kb)]
            acc = acc * fade + jnp.dot(v, p.astype(BF16), preferred_element_type=F32)
            return (new, den, acc)

        carry = lax.fori_loop(
            lo[i * groups + r] // kb, (hi[i * groups + r] + kb - 1) // kb, step, carry
        )
    top, den, acc = carry
    out[...] = (acc / den).astype(BF16)
    lse[...] = top + jnp.log(den)


def backward_kernel(
    lo, hi, q_ref, own, oth, rows, out, do_ref, lse, dq, dkv, dkv_oth, kvn, acc,
    *, groups, count, kb
):
    i = pl.program_id(0)

    @pl.when(i == 0)
    def _():
        fill_natural(kvn, own, oth, groups, count, min(count, 256))
        acc[...] = jnp.zeros_like(acc)

    qb = q_ref.shape[1]
    scale = 1.0 / math.sqrt(HD)
    qf = q_ref[...].astype(F32) * scale
    q = qf.astype(BF16)
    do = do_ref[...]
    dof = do.astype(F32)
    delta = jnp.sum(dof * out[...].astype(F32), axis=0, keepdims=True)
    none = jnp.zeros_like(q)
    q_pad = jnp.concatenate([q, none], axis=0)
    do_pad = jnp.concatenate([none, do], axis=0)
    q_nat = jnp.concatenate([qf, jnp.zeros_like(qf)], axis=0).T.astype(BF16)
    do_nat = jnp.concatenate([jnp.zeros_like(dof), dof], axis=0).T.astype(BF16)
    spot = lax.broadcasted_iota(jnp.int32, (kb, qb), 0)
    level = lse[...]
    grad = jnp.zeros((HD, qb), F32)
    for r in range(groups):
        first = rows[r : r + 1, :]
        end = rows[groups + r : groups + r + 1, :]

        def step(j, grad, r=r, first=first, end=end):
            k0 = pl.multiple_of(j * kb, kb)
            at = pl.ds(r * count + k0, kb)
            kv = kvn[at, :]
            s = jnp.dot(kv, q_pad, preferred_element_type=F32)
            dp = jnp.dot(kv, do_pad, preferred_element_type=F32)
            p = jnp.where((spot >= first - k0) & (spot < end - k0), jnp.exp(s - level), 0.0)
            ds = (p * (dp - delta)).astype(BF16)
            acc[at, :] += jnp.dot(ds, q_nat, preferred_element_type=F32) + jnp.dot(
                p.astype(BF16), do_nat, preferred_element_type=F32
            )
            if r == 0:
                k = own[HD : 2 * HD, pl.ds(k0, kb)]
            else:
                k = oth[r - 1, 0:HD, pl.ds(k0, kb)]
            return grad + jnp.dot(k, ds, preferred_element_type=F32)

        grad = lax.fori_loop(
            lo[i * groups + r] // kb, (hi[i * groups + r] + kb - 1) // kb, step, grad
        )
    dq[...] = grad * scale

    @pl.when(i == pl.num_programs(0) - 1)
    def _():
        chunk = min(count, 256)
        for r in range(groups):
            for c in range(count // chunk):
                at = slice(c * chunk, (c + 1) * chunk)
                piece = acc[r * count + c * chunk : r * count + (c + 1) * chunk, :].T
                if r == 0:
                    dkv[:, at] = piece
                else:
                    dkv_oth[r - 1, :, at] = piece.astype(BF16)


def slot_of(m):
    return (m & 1) * 2 + m // 2


def place_kernel(where, near, near_y, over, over_y, *outs, spans, far):
    c = pl.program_id(0)

    def put(same, other):
        for y in range(2):
            for j in range(far):
                m = slot_of(where[2] ^ j)

                def write(source, y=y, j=j, m=m):
                    base = 0
                    for out, rows in zip(outs, spans):
                        if len(out.shape) == 2:
                            lanes = source.shape[2]
                            at = (y * far + ((j & 1) << 1 | j >> 1)) * lanes
                            out[:, at : at + lanes] = source[m, base : base + rows, :].astype(F32)
                        base += rows

                @pl.when(where[1] == y)
                def _():
                    write(same)

                @pl.when(where[1] != y)
                def _():
                    write(other)

        base = 0
        for out, rows in zip(outs, spans):
            if len(out.shape) == 3:
                lanes = same.shape[2]

                def turn(low, high, out=out, base=base):
                    for j in range(far):
                        m = slot_of(where[2] ^ j)
                        for b in range(far):
                            for part in range(3):
                                at = base + (b * 3 + part) * HD
                                pair = jnp.concatenate(
                                    [
                                        low[m, at : at + HD, :].astype(F32),
                                        high[m, at : at + HD, :].astype(F32),
                                    ],
                                    axis=0,
                                )
                                out[
                                    part,
                                    b * lanes : (b + 1) * lanes,
                                    j * 2 * HD : (j + 1) * 2 * HD,
                                ] = pair.T

                @pl.when(where[1] == 0)
                def _():
                    turn(same, other)

                @pl.when(where[1] == 1)
                def _():
                    turn(other, same)
            base += rows

    @pl.when(where[0] == c)
    def _():
        put(near, near_y)

    @pl.when(where[0] != c)
    def _():
        put(over, over_y)


def place_sums(where, stacks, spans, shapes):
    far = stacks[0].shape[0]
    specs = [
        pl.BlockSpec((shape[0] // 2, shape[1]), lambda c, *_: (c, 0))
        if len(shape) == 2
        else pl.BlockSpec((shape[0], shape[1] // 2, shape[2]), lambda c, *_: (0, c, 0))
        for shape in shapes
    ]
    return pl.pallas_call(
        functools.partial(place_kernel, spans=spans, far=far),
        grid_spec=pltpu.PrefetchScalarGridSpec(
            num_scalar_prefetch=1,
            grid=(2,),
            in_specs=[whole(stack.shape) for stack in stacks],
            out_specs=specs,
        ),
        out_shape=[jax.ShapeDtypeStruct(shape, F32) for shape in shapes],
        name="place_sums",
    )(where, *stacks)


def blocks_of(count):
    return math.gcd(count, 256), math.gcd(count, 512)


def whole(shape):
    return pl.BlockSpec(shape, lambda i, *_: (0,) * len(shape))


def attention_forward(lo, hi, own, oth, rows, groups):
    count = own.shape[1]
    qb, kb = blocks_of(count)
    col = lambda height: pl.BlockSpec((height, qb), lambda i, *_: (0, i))
    return pl.pallas_call(
        functools.partial(forward_kernel, groups=groups, count=count, kb=kb),
        grid_spec=pltpu.PrefetchScalarGridSpec(
            num_scalar_prefetch=2,
            grid=(count // qb,),
            in_specs=[col(HD), whole(own.shape), whole(oth.shape), col(rows.shape[0])],
            out_specs=[col(HD), col(1)],
            scratch_shapes=[pltpu.VMEM((groups * count, 2 * HD), BF16)],
        ),
        out_shape=[
            jax.ShapeDtypeStruct((HD, count), BF16),
            jax.ShapeDtypeStruct((1, count), F32),
        ],
        name="attention_forward",
    )(lo, hi, own, own, oth, rows)


def attention_backward(lo, hi, own, oth, rows, out, do, lse, groups):
    count = own.shape[1]
    qb, kb = blocks_of(count)
    col = lambda height: pl.BlockSpec((height, qb), lambda i, *_: (0, i))
    others = (max(groups - 1, 1), 2 * HD, count)
    return pl.pallas_call(
        functools.partial(backward_kernel, groups=groups, count=count, kb=kb),
        grid_spec=pltpu.PrefetchScalarGridSpec(
            num_scalar_prefetch=2,
            grid=(count // qb,),
            in_specs=[
                col(HD), whole(own.shape), whole(oth.shape), col(rows.shape[0]),
                col(HD), col(HD), col(1),
            ],
            out_specs=[col(HD), whole((2 * HD, count)), whole(others)],
            scratch_shapes=[
                pltpu.VMEM((groups * count, 2 * HD), BF16),
                pltpu.VMEM((groups * count, 2 * HD), F32),
            ],
        ),
        out_shape=[
            jax.ShapeDtypeStruct((HD, count), F32),
            jax.ShapeDtypeStruct((2 * HD, count), F32),
            jax.ShapeDtypeStruct(others, BF16),
        ],
        name="attention_backward",
    )(lo, hi, own, own, oth, rows, out, do, lse)


def layer(
    tokens,
    seq_ids,
    attention_norm_gain,
    qkv_weight,
    out_weight,
    feedforward_norm_gain,
    mlp_in_weight,
    mlp_out_weight,
    grad_out,
    *,
    ctx,
    tp,
):
    tok_rows, width = tokens.shape
    local_cols = qkv_weight.shape[2]
    heads_here = local_cols // HD
    hidden_here = mlp_in_weight.shape[2]
    groups = ctx // heads_here
    part = tok_rows // groups
    count = ctx * part
    me = lax.axis_index("ctx")

    def tp_sum(value):
        value = value.astype(BF16)
        if tp == 2:
            other = lax.ppermute(value, "tp", [(0, 1), (1, 0)])
            return value.astype(F32) + other.astype(F32)
        return lax.psum(value, "tp").astype(F32)

    def to_group(value, r):
        pairs = [(i, i // groups * groups + (i + r) % groups) for i in range(ctx)]
        return lax.ppermute(value, "ctx", pairs)

    def for_heads(value):
        rows = value.shape[1]
        value = value.reshape(heads_here, rows, groups, part).transpose(0, 2, 1, 3)
        return value.reshape(ctx, rows, part)

    def to_heads(chunks):
        value = lax.all_to_all(chunks, "ctx", 0, 0)
        return value.transpose(1, 0, 2).reshape(chunks.shape[1], count)

    def for_tokens(value):
        return value.reshape(value.shape[0], ctx, part).transpose(1, 0, 2)

    def to_tokens(chunks):
        rows = chunks.shape[1]
        value = lax.all_to_all(chunks, "ctx", 0, 0)
        value = value.reshape(heads_here, groups, rows, part).transpose(0, 2, 1, 3)
        return value.reshape(heads_here, rows, tok_rows)

    def after(value, *needed):
        return lax.optimization_barrier((value,) + needed)[0]

    bits = list(range(ctx.bit_length() - 1))
    group_bits = list(range(groups.bit_length() - 1))
    head_bits = bits[len(group_bits) :]
    far_bits = bits[2:]

    def spread(bits):
        masks = [
            sum(((m >> at) & 1) << bit for at, bit in enumerate(bits))
            for m in range(1 << len(bits))
        ]
        here = sum((((me >> bit) & 1) << at) for at, bit in enumerate(bits))
        return masks, here

    def pick(pieces, index):
        value = pieces[0]
        for at in range(1, len(pieces)):
            value = jnp.where(index == at, pieces[at], value)
        return value

    def hop(value, mask):
        return lax.ppermute(value, "ctx", [(i, i ^ mask) for i in range(ctx)])

    def deal(value, bits, axis):
        masks, here = spread(bits)
        pieces = jnp.split(value, len(masks), axis=axis)
        return [pick(pieces, here ^ m) for m in range(len(masks))]

    def send_dealt(dealt, bits):
        masks, _ = spread(bits)
        return [dealt[0]] + [hop(dealt[m], masks[m]) for m in range(1, len(masks))]

    def total(pieces):
        return sum(piece.astype(F32) for piece in pieces).astype(BF16)

    def send_all(value, bits):
        masks, _ = spread(bits)
        return [value] + [hop(value, masks[m]) for m in range(1, len(masks))]

    def arrange(pieces, bits, axis):
        _, here = spread(bits)
        return jnp.concatenate(
            [pick(pieces, here ^ at) for at in range(len(pieces))], axis=axis
        )

    def double(value, inner, outer):
        value = arrange(send_all(value, inner), inner, 1)
        return arrange(send_all(value, outer), outer, 1)

    def fence(*values):
        return lax.optimization_barrier(values)

    over_cols = (((1,), (1,)), ((), ()))
    over_rows = (((0,), (0,)), ((), ()))
    across = (((0,), (1,)), ((), ()))

    def dot(left, right, dims=(((1,), (0,)), ((), ()))):
        return lax.dot_general(left, right, dims, preferred_element_type=F32)

    input_tokens = tokens.astype(F32)
    attention_standardized, attention_inverse_deviation, attention_normed_input = layer_normalize(
        input_tokens, attention_norm_gain
    )
    first = attention_normed_input.astype(BF16)
    planes = [qkv_weight[:, c] for c in range(3)]
    proj = [dot(plane, first, across).reshape(heads_here, HD, tok_rows) for plane in planes]
    positions = me * tok_rows + jnp.arange(tok_rows, dtype=jnp.int32)
    cosine, sine = rope_tables_t(positions, HD)
    ids = jnp.broadcast_to(seq_ids.astype(BF16)[None, None, :], (heads_here, PAD, tok_rows))
    packed = jnp.concatenate(
        [
            rotate_t(proj[0], cosine, sine).astype(BF16),
            rotate_t(proj[1], cosine, sine).astype(BF16),
            proj[2].astype(BF16),
            ids,
        ],
        axis=1,
    )
    own = to_heads(for_heads(packed))
    if groups > 1:
        oth = jnp.stack([to_group(own[HD:], groups - r) for r in range(1, groups)])
    else:
        oth = own[None, HD:]
    id_own = own[3 * HD]
    id_all = jnp.concatenate([id_own[None], oth[: groups - 1, 2 * HD]], axis=0)
    marks = jnp.arange(SEQS + 1, dtype=F32)
    below = jnp.sum((id_all.astype(F32)[:, None, :] < marks[None, :, None]).astype(jnp.int32), -1)
    first_key = jnp.zeros((groups, count), jnp.int32)
    end_key = jnp.zeros((groups, count), jnp.int32)
    for s in range(SEQS):
        hit = (id_own == s)[None, :]
        first_key = jnp.where(hit, below[:, s : s + 1], first_key)
        end_key = jnp.where(hit, below[:, s + 1 : s + 2], end_key)
    rows = jnp.concatenate([first_key, end_key], axis=0)
    qb, _ = blocks_of(count)
    lo = first_key[:, ::qb].T.reshape(-1)
    hi = end_key[:, qb - 1 :: qb].T.reshape(-1)

    place = me % groups
    parts = first.reshape(groups, part, width)
    held = [lax.dynamic_index_in_dim(parts, place, 0, keepdims=False)]
    for r in range(1, groups):
        held.append(
            to_group(
                lax.dynamic_index_in_dim(parts, (place + r) % groups, 0, keepdims=False), r
            )
        )
    held = jnp.stack(held)
    held = jnp.concatenate(
        [
            lax.dynamic_index_in_dim(held, (place - c) % groups, 0, keepdims=False)
            for c in range(groups)
        ],
        axis=0,
    )
    first_all = lax.all_gather(
        held,
        "ctx",
        axis=0,
        tiled=True,
        axis_index_groups=[[h * groups + g for h in range(heads_here)] for g in range(groups)],
    )

    att_head, lse = attention_forward(lo, hi, own, oth, rows, groups)
    attended = to_tokens(for_tokens(att_head)).reshape(local_cols, tok_rows)
    attn_part = dot(attended, out_weight, over_rows)
    residual_middle = input_tokens + tp_sum(attn_part)
    feedforward_standardized, feedforward_inverse_deviation, feedforward_normed_input = (
        layer_normalize(residual_middle, feedforward_norm_gain)
    )
    second, first_all = lax.optimization_barrier(
        (feedforward_normed_input.astype(BF16), first_all)
    )
    in_act = mlp_in_weight[:, 0]
    in_gate = mlp_in_weight[:, 1]
    act_in = dot(second, in_act)
    gate = dot(second, in_gate)
    hidden = (gelu_value(act_in) * gate).astype(BF16)
    upstream = grad_out.astype(F32)
    grad_hidden = dot(grad_out, mlp_out_weight, over_cols)
    grad_act = (grad_hidden * gate * gelu_slope(act_in)).astype(BF16)
    grad_gate = (grad_hidden * gelu_value(act_in)).astype(BF16)
    second_part = dot(grad_act, in_act, over_cols) + dot(grad_gate, in_gate, over_cols)
    second_part, second_w, act_w, gate_w, hidden_w = fence(
        second_part.astype(BF16), second, grad_act, grad_gate, hidden
    )
    feedforward_norm_gradient = tp_sum(second_part)
    grad_w_out = dot(hidden_w, grad_out, over_rows).astype(BF16)
    w_core = send_dealt(deal(grad_w_out, bits[:1], 0), bits[:1])
    grad_w_act = dot(act_w, second_w, over_rows).astype(BF16)
    grad_w_gate = dot(gate_w, second_w, over_rows).astype(BF16)
    feedforward_norm_gradient, grad_w_act, grad_w_gate, *w_core = fence(
        feedforward_norm_gradient, grad_w_act, grad_w_gate, *w_core
    )
    sum_act, sum_gate = lax.psum((grad_w_act, grad_w_gate), "ctx")
    feedforward_normed_gradient, feedforward_gain_gradient = layer_normalize_backward(
        feedforward_norm_gradient,
        feedforward_standardized,
        feedforward_inverse_deviation,
        feedforward_norm_gain,
    )
    grad_mid = upstream + feedforward_normed_gradient
    grad_mid_b = grad_mid.astype(BF16)
    grad_att = dot(out_weight, grad_mid_b, over_cols).astype(BF16)
    chunks = for_heads(grad_att.reshape(heads_here, HD, tok_rows))
    chunks, w_kept, w_came, late_mid, late_hidden = fence(chunks, *w_core, grad_mid_b, hidden_w)
    do_head = to_heads(chunks)

    w_y = deal(total([w_kept, w_came]), bits[1:2], 1)
    w_y = send_dealt(w_y, bits[1:2])
    grad_w_attn = dot(attended, late_mid).astype(BF16)
    u_core = send_dealt(deal(grad_w_attn, bits[:1], 0), bits[:1])
    ffn_part = dot(late_hidden, mlp_out_weight).astype(BF16)
    do_head, ffn_part, *held_back = fence(do_head, ffn_part, *w_y, *u_core)
    w_y, u_core = held_back[: len(w_y)], held_back[len(w_y) :]

    output_sum = tp_sum(ffn_part)
    third, rest = bits[2:3], bits[3:]
    w_far = deal(total(w_y), third, 1)
    u_y = deal(total(u_core), bits[1:2], 1)
    do_head, *sends = fence(do_head, *w_far, *u_y)
    w_far = send_dealt(sends[: len(w_far)], third)
    u_y = send_dealt(sends[len(w_far) :], bits[1:2])
    dq, dkv, dkv_oth = attention_backward(
        lo, hi, own, oth, rows, att_head, do_head, lse, groups
    )
    dq, dkv, dkv_oth, output_sum, *held_back = fence(
        dq, dkv, dkv_oth, output_sum, *w_far, *u_y
    )
    w_far, u_y = held_back[: len(w_far)], held_back[len(w_far) :]
    for r in range(1, groups):
        dkv = dkv + to_group(dkv_oth[r - 1], r).astype(F32)
    spots = (
        jnp.arange(ctx, dtype=jnp.int32)[:, None] * tok_rows
        + place * part
        + jnp.arange(part, dtype=jnp.int32)[None, :]
    ).reshape(-1)
    cosine_head, sine_head = rope_tables_t(spots, HD)
    grads = jnp.concatenate(
        [
            unrotate_t(dq[None], cosine_head, sine_head)[0].astype(BF16),
            unrotate_t(dkv[None, :HD], cosine_head, sine_head)[0].astype(BF16),
            dkv[HD:].astype(BF16),
        ],
        axis=0,
    )
    chunks = for_tokens(grads)
    chunks, grads_w = fence(chunks, grads)
    grad_proj = to_tokens(chunks)

    _, *held_back = fence(chunks, *w_far, *u_y)
    w_far, u_y = held_back[: len(w_far)], held_back[len(w_far) :]
    w_rest = send_dealt(deal(total(w_far), rest, 1), rest)
    u_third = send_dealt(deal(total(u_y), third, 1), third)
    share = dot(grads_w, first_all).astype(BF16)
    share = send_dealt(deal(share, group_bits, 1), group_bits)
    low_bits = [bit for bit in head_bits if bit not in far_bits]
    high_bits = [bit for bit in head_bits if bit in far_bits]
    joint = group_bits == bits[:1] and low_bits == bits[1:2] and high_bits == far_bits == bits[2:4]
    output = (residual_middle + output_sum).astype(BF16)
    w = total(w_rest)
    w_back = send_all(w, rest)
    u_rest = send_dealt(deal(total(u_third), rest, 1), rest)
    share = total(share)[None]
    grad_proj, share, output, w, *u_rest = fence(grad_proj, share, output, w, *u_rest)

    first_part = sum(
        dot(grad_proj[:, c * HD : (c + 1) * HD].reshape(local_cols, tok_rows), planes[c], across)
        for c in range(3)
    ).astype(BF16)
    u = total(u_rest)
    u_stack = u
    if joint:
        cut = share.shape[2] // (1 << len(far_bits))
        u_stack = jnp.concatenate(
            [u] + [share[0, :, at : at + cut] for at in range(0, share.shape[2], cut)], axis=0
        )
    first_part, u_stack, *w_back = fence(first_part, u_stack, *w_back)
    attention_norm_gradient = tp_sum(first_part)
    if joint:
        w_stack = jnp.stack(w_back)
        w_stack = jnp.concatenate(send_all(w_stack, third))
        u_back = send_all(u_stack, rest)
        attention_norm_gradient, w_stack, *u_back = fence(
            attention_norm_gradient, w_stack, *u_back
        )
        w_y, w_over = hop(w_stack, 2), hop(w_stack, 1)
        u_stack = jnp.stack(u_back)
        u_stack = jnp.concatenate(send_all(u_stack, third))
        w_y, w_over, u_stack = fence(w_y, w_over, u_stack)
        w_stacks = [w_stack, w_y, w_over, hop(w_y, 1)]
        u_y, u_over = hop(u_stack, 2), hop(u_stack, 1)
    else:
        share = arrange(send_all(share, high_bits), high_bits, 0)
        share = arrange(send_all(share, low_bits), low_bits, 0)
        share = arrange(send_all(share, group_bits), group_bits, 2)
        w = double(w, rest, third)
        w = arrange(send_all(w, bits[1:2]), bits[1:2], 1)
        w = arrange(send_all(w, bits[:1]), bits[:1], 0)
        u = double(u, rest, third)
        u = arrange(send_all(u, bits[1:2]), bits[1:2], 1)
        u = arrange(send_all(u, bits[:1]), bits[:1], 0)
    attention_normed_gradient, attention_gain_gradient = layer_normalize_backward(
        attention_norm_gradient,
        attention_standardized,
        attention_inverse_deviation,
        attention_norm_gain,
    )
    grad_tokens = grad_mid + attention_normed_gradient
    gains = jnp.stack([attention_gain_gradient, feedforward_gain_gradient])
    gains = sum(send_all(gains, bits[:1]))
    gains = sum(send_all(gains, bits[1:2]))
    masks, here = spread(far_bits)
    gains = send_all(gains, far_bits)
    gains = sum(pick(gains, here ^ at) for at in range(len(masks)))
    if joint:
        here = jnp.stack([me & 1, (me >> 1) & 1, me >> 2]).astype(jnp.int32)
        (w,) = place_sums(here, w_stacks, [w.shape[0]], [(hidden_here, width)])
        gains, grad_tokens, w, u_y, u_over = fence(gains, grad_tokens, w, u_y, u_over)
        u, sum_qkv = place_sums(
            here,
            [u_stack, u_y, u_over, hop(u_y, 1)],
            [u.shape[0], u_stack.shape[1] - u.shape[0]],
            [(local_cols, width), (3, width, local_cols)],
        )
        sum_qkv = sum_qkv.transpose(1, 0, 2)
    else:
        sum_qkv = (
            share.reshape(1 << len(low_bits), 1 << len(high_bits), 3, HD, width)
            .transpose(4, 2, 1, 0, 3)
            .reshape(width, 3, local_cols)
        )
    sum_act, sum_gate, *_ = fence(sum_act, sum_gate, sum_qkv, w, u, grad_tokens, gains)
    return (
        output,
        grad_tokens,
        gains[0],
        sum_qkv.astype(F32),
        u.astype(F32),
        gains[1],
        jnp.stack([sum_act, sum_gate]).transpose(2, 0, 1).astype(F32),
        w.astype(F32),
    )


def solution(mesh):
    return jax.shard_map(
        functools.partial(layer, ctx=mesh.shape["ctx"], tp=mesh.shape["tp"]),
        mesh=mesh,
        in_specs=(
            P("ctx", None),
            P("ctx"),
            P(),
            P(None, None, "tp"),
            P("tp", None),
            P(),
            P(None, None, "tp"),
            P("tp", None),
            P("ctx", None),
        ),
        out_specs=(
            P("ctx", None),
            P("ctx", None),
            P(),
            P(None, None, "tp"),
            P("tp", None),
            P(),
            P(None, None, "tp"),
            P("tp", None),
        ),
        check_vma=False,
    )
```

```python
import functools
import math

import jax
import jax.numpy as jnp
from jax import lax
from jax.experimental import pallas as pl
from jax.experimental.pallas import tpu as pltpu
from jax.sharding import PartitionSpec as P

HD = 64
EPS = 1e-05
BASE = 160000.0
MASKED = -1e30
ROOT_HALF = 0.7071067811865476
INV_ROOT_TWO_PI = 0.3989422804014327
SEQS = 4
F32 = jnp.float32
BF16 = jnp.bfloat16
PAD = 16


def layer_normalize(values_in, norm_gain_vector):
    token_average = jnp.mean(values_in, axis=-1, keepdims=True)
    centered_input = values_in - token_average
    inverse_deviation = lax.rsqrt(
        jnp.mean(centered_input * centered_input, axis=-1, keepdims=True) + EPS
    )
    standardized_input = centered_input * inverse_deviation
    return (standardized_input, inverse_deviation, standardized_input * norm_gain_vector)


def layer_normalize_backward(
    output_gradient, standardized_input, inverse_deviation, norm_gain_vector
):
    normalized_gradient = output_gradient * norm_gain_vector
    correction_term = jnp.mean(
        normalized_gradient, axis=-1, keepdims=True
    ) + standardized_input * jnp.mean(
        normalized_gradient * standardized_input, axis=-1, keepdims=True
    )
    return (
        inverse_deviation * (normalized_gradient - correction_term),
        jnp.sum(output_gradient * standardized_input, axis=0),
    )


def gelu_value(v):
    return v * 0.5 * (1.0 + lax.erf(v * ROOT_HALF))


def gelu_slope(v):
    return 0.5 * (1.0 + lax.erf(v * ROOT_HALF)) + v * jnp.exp(-0.5 * v * v) * INV_ROOT_TWO_PI


def rope_tables_t(positions, head_size):
    half = head_size // 2
    inverse = BASE ** (-(jnp.arange(half, dtype=F32) * (2.0 / head_size)))
    angle = inverse[:, None] * positions.astype(F32)[None, :]
    return (jnp.cos(angle), jnp.sin(angle))


def rotate_t(field, cosine, sine):
    half = field.shape[1] // 2
    one, two = field[:, :half], field[:, half:]
    return jnp.concatenate([one * cosine - two * sine, two * cosine + one * sine], axis=1)


def unrotate_t(grad, cosine, sine):
    half = grad.shape[1] // 2
    one, two = grad[:, :half], grad[:, half:]
    return jnp.concatenate([one * cosine + two * sine, two * cosine - one * sine], axis=1)


def fill_natural(kvn, own, oth, groups, count, chunk):
    for r in range(groups):
        for c in range(count // chunk):
            at = slice(c * chunk, (c + 1) * chunk)
            if r == 0:
                piece = own[HD : 3 * HD, at]
            else:
                piece = oth[r - 1, 0 : 2 * HD, at]
            kvn[r * count + c * chunk : r * count + (c + 1) * chunk, :] = (
                piece.astype(F32).T.astype(BF16)
            )


def forward_kernel(lo, hi, q_ref, own, oth, rows, out, lse, kvn, *, groups, count, kb):
    i = pl.program_id(0)

    @pl.when(i == 0)
    def _():
        fill_natural(kvn, own, oth, groups, count, min(count, 256))

    qb = q_ref.shape[1]
    q = (q_ref[...].astype(F32) * (1.0 / math.sqrt(HD))).astype(BF16)
    q = jnp.concatenate([q, jnp.zeros_like(q)], axis=0)
    spot = lax.broadcasted_iota(jnp.int32, (kb, qb), 0)
    carry = (
        jnp.full((1, qb), MASKED, F32),
        jnp.zeros((1, qb), F32),
        jnp.zeros((HD, qb), F32),
    )
    for r in range(groups):
        first = rows[r : r + 1, :]
        end = rows[groups + r : groups + r + 1, :]

        def step(j, carry, r=r, first=first, end=end):
            top, den, acc = carry
            k0 = pl.multiple_of(j * kb, kb)
            s = jnp.dot(kvn[pl.ds(r * count + k0, kb), :], q, preferred_element_type=F32)
            s = jnp.where((spot >= first - k0) & (spot < end - k0), s, MASKED)
            new = jnp.maximum(top, jnp.max(s, axis=0, keepdims=True))
            p = jnp.exp(s - new)
            fade = jnp.exp(top - new)
            den = den * fade + jnp.sum(p, axis=0, keepdims=True)
            if r == 0:
                v = own[2 * HD : 3 * HD, pl.ds(k0, kb)]
            else:
                v = oth[r - 1, HD : 2 * HD, pl.ds(k0, kb)]
            acc = acc * fade + jnp.dot(v, p.astype(BF16), preferred_element_type=F32)
            return (new, den, acc)

        carry = lax.fori_loop(
            lo[i * groups + r] // kb, (hi[i * groups + r] + kb - 1) // kb, step, carry
        )
    top, den, acc = carry
    out[...] = (acc / den).astype(BF16)
    lse[...] = top + jnp.log(den)


def backward_kernel(
    lo, hi, q_ref, own, oth, rows, out, do_ref, lse, dq, dkv, dkv_oth, kvn, acc,
    *, groups, count, kb
):
    i = pl.program_id(0)

    @pl.when(i == 0)
    def _():
        fill_natural(kvn, own, oth, groups, count, min(count, 256))
        acc[...] = jnp.zeros_like(acc)

    qb = q_ref.shape[1]
    scale = 1.0 / math.sqrt(HD)
    qf = q_ref[...].astype(F32) * scale
    q = qf.astype(BF16)
    do = do_ref[...]
    dof = do.astype(F32)
    delta = jnp.sum(dof * out[...].astype(F32), axis=0, keepdims=True)
    none = jnp.zeros_like(q)
    q_pad = jnp.concatenate([q, none], axis=0)
    do_pad = jnp.concatenate([none, do], axis=0)
    q_nat = jnp.concatenate([qf, jnp.zeros_like(qf)], axis=0).T.astype(BF16)
    do_nat = jnp.concatenate([jnp.zeros_like(dof), dof], axis=0).T.astype(BF16)
    spot = lax.broadcasted_iota(jnp.int32, (kb, qb), 0)
    level = lse[...]
    grad = jnp.zeros((HD, qb), F32)
    for r in range(groups):
        first = rows[r : r + 1, :]
        end = rows[groups + r : groups + r + 1, :]

        def step(j, grad, r=r, first=first, end=end):
            k0 = pl.multiple_of(j * kb, kb)
            at = pl.ds(r * count + k0, kb)
            kv = kvn[at, :]
            s = jnp.dot(kv, q_pad, preferred_element_type=F32)
            dp = jnp.dot(kv, do_pad, preferred_element_type=F32)
            p = jnp.where((spot >= first - k0) & (spot < end - k0), jnp.exp(s - level), 0.0)
            ds = (p * (dp - delta)).astype(BF16)
            acc[at, :] += jnp.dot(ds, q_nat, preferred_element_type=F32) + jnp.dot(
                p.astype(BF16), do_nat, preferred_element_type=F32
            )
            if r == 0:
                k = own[HD : 2 * HD, pl.ds(k0, kb)]
            else:
                k = oth[r - 1, 0:HD, pl.ds(k0, kb)]
            return grad + jnp.dot(k, ds, preferred_element_type=F32)

        grad = lax.fori_loop(
            lo[i * groups + r] // kb, (hi[i * groups + r] + kb - 1) // kb, step, grad
        )
    dq[...] = grad * scale

    @pl.when(i == pl.num_programs(0) - 1)
    def _():
        chunk = min(count, 256)
        for r in range(groups):
            for c in range(count // chunk):
                at = slice(c * chunk, (c + 1) * chunk)
                piece = acc[r * count + c * chunk : r * count + (c + 1) * chunk, :].T
                if r == 0:
                    dkv[:, at] = piece
                else:
                    dkv_oth[r - 1, :, at] = piece.astype(BF16)


def blocks_of(count):
    return math.gcd(count, 256), math.gcd(count, 512)


def whole(shape):
    return pl.BlockSpec(shape, lambda i, *_: (0,) * len(shape))


def attention_forward(lo, hi, own, oth, rows, groups):
    count = own.shape[1]
    qb, kb = blocks_of(count)
    col = lambda height: pl.BlockSpec((height, qb), lambda i, *_: (0, i))
    return pl.pallas_call(
        functools.partial(forward_kernel, groups=groups, count=count, kb=kb),
        grid_spec=pltpu.PrefetchScalarGridSpec(
            num_scalar_prefetch=2,
            grid=(count // qb,),
            in_specs=[col(HD), whole(own.shape), whole(oth.shape), col(rows.shape[0])],
            out_specs=[col(HD), col(1)],
            scratch_shapes=[pltpu.VMEM((groups * count, 2 * HD), BF16)],
        ),
        out_shape=[
            jax.ShapeDtypeStruct((HD, count), BF16),
            jax.ShapeDtypeStruct((1, count), F32),
        ],
        name="attention_forward",
    )(lo, hi, own, own, oth, rows)


def attention_backward(lo, hi, own, oth, rows, out, do, lse, groups):
    count = own.shape[1]
    qb, kb = blocks_of(count)
    col = lambda height: pl.BlockSpec((height, qb), lambda i, *_: (0, i))
    others = (max(groups - 1, 1), 2 * HD, count)
    return pl.pallas_call(
        functools.partial(backward_kernel, groups=groups, count=count, kb=kb),
        grid_spec=pltpu.PrefetchScalarGridSpec(
            num_scalar_prefetch=2,
            grid=(count // qb,),
            in_specs=[
                col(HD), whole(own.shape), whole(oth.shape), col(rows.shape[0]),
                col(HD), col(HD), col(1),
            ],
            out_specs=[col(HD), whole((2 * HD, count)), whole(others)],
            scratch_shapes=[
                pltpu.VMEM((groups * count, 2 * HD), BF16),
                pltpu.VMEM((groups * count, 2 * HD), F32),
            ],
        ),
        out_shape=[
            jax.ShapeDtypeStruct((HD, count), F32),
            jax.ShapeDtypeStruct((2 * HD, count), F32),
            jax.ShapeDtypeStruct(others, BF16),
        ],
        name="attention_backward",
    )(lo, hi, own, own, oth, rows, out, do, lse)


def layer(
    tokens,
    seq_ids,
    attention_norm_gain,
    qkv_weight,
    out_weight,
    feedforward_norm_gain,
    mlp_in_weight,
    mlp_out_weight,
    grad_out,
    *,
    ctx,
    tp,
):
    tok_rows, width = tokens.shape
    local_cols = qkv_weight.shape[2]
    heads_here = local_cols // HD
    hidden_here = mlp_in_weight.shape[2]
    groups = ctx // heads_here
    part = tok_rows // groups
    count = ctx * part
    me = lax.axis_index("ctx")

    def tp_sum(value):
        value = value.astype(BF16)
        if tp == 2:
            other = lax.ppermute(value, "tp", [(0, 1), (1, 0)])
            return value.astype(F32) + other.astype(F32)
        return lax.psum(value, "tp").astype(F32)

    def to_group(value, r):
        pairs = [(i, i // groups * groups + (i + r) % groups) for i in range(ctx)]
        return lax.ppermute(value, "ctx", pairs)

    def for_heads(value):
        value = jnp.stack(
            [value[:, :, g * part : (g + 1) * part] for g in range(groups)], axis=1
        )
        return value.reshape(ctx, value.shape[2], part)

    def to_heads(chunks):
        value = lax.all_to_all(chunks, "ctx", 0, 0)
        return value.transpose(1, 0, 2).reshape(chunks.shape[1], count)

    def for_tokens(value):
        return value.reshape(value.shape[0], ctx, part).transpose(1, 0, 2)

    def to_tokens(chunks):
        value = lax.all_to_all(chunks, "ctx", 0, 0)
        value = value.reshape(heads_here, groups, chunks.shape[1], part)
        return jnp.concatenate([value[:, g] for g in range(groups)], axis=2)

    bits = list(range(ctx.bit_length() - 1))
    group_bits = list(range(groups.bit_length() - 1))
    head_bits = bits[len(group_bits) :]
    far_bits = bits[2:]

    def spread(bits):
        masks = [
            sum(((m >> at) & 1) << bit for at, bit in enumerate(bits))
            for m in range(1 << len(bits))
        ]
        here = sum((((me >> bit) & 1) << at) for at, bit in enumerate(bits))
        return masks, here

    def pick(pieces, index):
        value = pieces[0]
        for at in range(1, len(pieces)):
            value = jnp.where(index == at, pieces[at], value)
        return value

    def hop(value, mask):
        return lax.ppermute(value, "ctx", [(i, i ^ mask) for i in range(ctx)])

    def deal(value, bits, axis):
        masks, here = spread(bits)
        pieces = jnp.split(value, len(masks), axis=axis)
        return [pick(pieces, here ^ m) for m in range(len(masks))]

    def send_dealt(dealt, bits):
        masks, _ = spread(bits)
        return [dealt[0]] + [hop(dealt[m], masks[m]) for m in range(1, len(masks))]

    def total(pieces):
        return sum(piece.astype(F32) for piece in pieces).astype(BF16)

    def send_all(value, bits):
        masks, _ = spread(bits)
        return [value] + [hop(value, masks[m]) for m in range(1, len(masks))]

    def arrange(pieces, bits, axis):
        _, here = spread(bits)
        return jnp.concatenate(
            [pick(pieces, here ^ at) for at in range(len(pieces))], axis=axis
        )

    def halve(value, bit):
        return send_dealt(deal(value, [bit], 0), [bit])

    def grow(value, bit):
        return send_all(value, [bit])

    def grown(pieces, bit):
        return arrange(pieces, [bit], 0)

    def fence(*values):
        return lax.optimization_barrier(values)

    over_cols = (((1,), (1,)), ((), ()))
    over_rows = (((0,), (0,)), ((), ()))
    across = (((0,), (1,)), ((), ()))

    def dot(left, right, dims=(((1,), (0,)), ((), ()))):
        return lax.dot_general(left, right, dims, preferred_element_type=F32)

    input_tokens = tokens.astype(F32)
    attention_standardized, attention_inverse_deviation, attention_normed_input = layer_normalize(
        input_tokens, attention_norm_gain
    )
    first = attention_normed_input.astype(BF16)
    planes = [qkv_weight[:, c] for c in range(3)]
    proj = [dot(plane, first, across).reshape(heads_here, HD, tok_rows) for plane in planes]
    positions = me * tok_rows + jnp.arange(tok_rows, dtype=jnp.int32)
    cosine, sine = rope_tables_t(positions, HD)
    ids = jnp.broadcast_to(seq_ids.astype(BF16)[None, None, :], (heads_here, PAD, tok_rows))
    packed = jnp.concatenate(
        [
            rotate_t(proj[0], cosine, sine).astype(BF16),
            rotate_t(proj[1], cosine, sine).astype(BF16),
            proj[2].astype(BF16),
            ids,
        ],
        axis=1,
    )
    own = to_heads(for_heads(packed))
    if groups > 1:
        oth = jnp.stack([to_group(own[HD:], groups - r) for r in range(1, groups)])
    else:
        oth = own[None, HD:]
    id_own = own[3 * HD]
    id_all = jnp.concatenate([id_own[None], oth[: groups - 1, 2 * HD]], axis=0)
    marks = jnp.arange(SEQS + 1, dtype=F32)
    below = jnp.sum((id_all.astype(F32)[:, None, :] < marks[None, :, None]).astype(jnp.int32), -1)
    first_key = jnp.zeros((groups, count), jnp.int32)
    end_key = jnp.zeros((groups, count), jnp.int32)
    for s in range(SEQS):
        hit = (id_own == s)[None, :]
        first_key = jnp.where(hit, below[:, s : s + 1], first_key)
        end_key = jnp.where(hit, below[:, s + 1 : s + 2], end_key)
    rows = jnp.concatenate([first_key, end_key], axis=0)
    qb, _ = blocks_of(count)
    lo = first_key[:, ::qb].T.reshape(-1)
    hi = end_key[:, qb - 1 :: qb].T.reshape(-1)

    att_head, lse = attention_forward(lo, hi, own, oth, rows, groups)
    attended = to_tokens(for_tokens(att_head)).reshape(local_cols, tok_rows)
    attn_part = dot(attended, out_weight, over_rows)
    residual_middle = input_tokens + tp_sum(attn_part)
    feedforward_standardized, feedforward_inverse_deviation, feedforward_normed_input = (
        layer_normalize(residual_middle, feedforward_norm_gain)
    )
    second = feedforward_normed_input.astype(BF16)
    in_act = mlp_in_weight[:, 0]
    in_gate = mlp_in_weight[:, 1]
    act_in = dot(second, in_act)
    gate = dot(second, in_gate)
    hidden = (gelu_value(act_in) * gate).astype(BF16)
    upstream = grad_out.astype(F32)
    grad_hidden = dot(grad_out, mlp_out_weight, over_cols)
    grad_act = (grad_hidden * gate * gelu_slope(act_in)).astype(BF16)
    grad_gate = (grad_hidden * gelu_value(act_in)).astype(BF16)
    second_part = dot(grad_act, in_act, over_cols) + dot(grad_gate, in_gate, over_cols)
    second_part, second_w, act_w, gate_w, hidden_w = fence(
        second_part.astype(BF16), second, grad_act, grad_gate, hidden
    )
    feedforward_norm_gradient = tp_sum(second_part)
    grad_w = [
        dot(left, right, over_rows).astype(BF16)
        for left, right in ((hidden_w, grad_out), (act_w, second_w), (gate_w, second_w))
    ]
    feedforward_norm_gradient, *grad_w = fence(feedforward_norm_gradient, *grad_w)
    sum_w = lax.psum(tuple(grad_w), "ctx")
    feedforward_normed_gradient, feedforward_gain_gradient = layer_normalize_backward(
        feedforward_norm_gradient,
        feedforward_standardized,
        feedforward_inverse_deviation,
        feedforward_norm_gain,
    )
    grad_mid = upstream + feedforward_normed_gradient
    grad_mid_b = grad_mid.astype(BF16)
    grad_att = dot(out_weight, grad_mid_b, over_cols).astype(BF16)
    chunks = for_heads(grad_att.reshape(heads_here, HD, tok_rows))
    chunks, late_mid, late_hidden = fence(chunks, grad_mid_b, hidden_w)
    do_head = to_heads(chunks)

    wide = width // local_cols
    grad_w_attn = [
        dot(attended, late_mid[:, at * local_cols : (at + 1) * local_cols]).astype(BF16)
        for at in range(wide)
    ]
    ffn_part = dot(late_hidden, mlp_out_weight).astype(BF16)
    do_head, ffn_part, *grad_w_attn = fence(do_head, ffn_part, *grad_w_attn)

    output_sum = tp_sum(ffn_part)
    dq, dkv, dkv_oth = attention_backward(
        lo, hi, own, oth, rows, att_head, do_head, lse, groups
    )
    dq, dkv, dkv_oth, output_sum = fence(dq, dkv, dkv_oth, output_sum)
    for r in range(1, groups):
        dkv = dkv + to_group(dkv_oth[r - 1], r).astype(F32)
    place = me % groups
    spots = (
        jnp.arange(ctx, dtype=jnp.int32)[:, None] * tok_rows
        + place * part
        + jnp.arange(part, dtype=jnp.int32)[None, :]
    ).reshape(-1)
    cosine_head, sine_head = rope_tables_t(spots, HD)
    grads = jnp.concatenate(
        [
            unrotate_t(dq[None], cosine_head, sine_head)[0].astype(BF16),
            unrotate_t(dkv[None, :HD], cosine_head, sine_head)[0].astype(BF16),
            dkv[HD:].astype(BF16),
        ],
        axis=0,
    )
    chunks = for_tokens(grads)
    grad_proj = to_tokens(chunks)
    output = (residual_middle + output_sum).astype(BF16)
    grad_proj, output = fence(grad_proj, output)
    grad_planes = [
        grad_proj[:, c * HD : (c + 1) * HD].reshape(local_cols, tok_rows) for c in range(3)
    ]

    bundle = jnp.concatenate(
        [dot(first, plane, (((0,), (1,)), ((), ()))).astype(BF16) for plane in grad_planes]
        + grad_w_attn,
        axis=0,
    )
    first_send = deal(bundle, bits[:1], 0)
    grad_planes = fence(*grad_planes, *first_send)[:3]
    bundle = send_dealt(first_send, bits[:1])
    first_part = sum(
        dot(plane, weight, across) for plane, weight in zip(grad_planes, planes)
    ).astype(BF16)
    first_part, *bundle = fence(first_part, *bundle)
    one, two = jnp.split(total(bundle), 2)
    order_one = bits[1:]
    order_two = bits[2:3] + bits[1:2] + bits[3:]
    attention_norm_gradient = tp_sum(first_part)
    one, two = halve(one, order_one[0]), halve(two, order_two[0])
    attention_norm_gradient, *both = fence(attention_norm_gradient, *one, *two)
    one, two = total(both[:2]), total(both[2:])
    attention_normed_gradient, attention_gain_gradient = layer_normalize_backward(
        attention_norm_gradient,
        attention_standardized,
        attention_inverse_deviation,
        attention_norm_gain,
    )
    grad_tokens = grad_mid + attention_normed_gradient
    gains = jnp.stack([attention_gain_gradient, feedforward_gain_gradient])
    one, two = halve(one, order_one[1]), halve(two, order_two[1])
    gains = send_all(gains, bits[:1])
    grad_tokens, *both = fence(grad_tokens, *gains, *one, *two)
    gains = sum(both[: len(gains)])
    one, two = total(both[-4:-2]), total(both[-2:])
    gains = send_all(gains, bits[1:2])
    for bit_one, bit_two in zip(order_one[2:], order_two[2:]):
        one, two = halve(one, bit_one), halve(two, bit_two)
        both = fence(*gains, *one, *two)
        gains = list(both[: len(gains)])
        one, two = total(both[-4:-2]), total(both[-2:])
    gains = sum(gains)
    masks, here = spread(far_bits)
    gains = send_all(gains, far_bits)
    for bit_one, bit_two in zip(reversed(order_one), reversed(order_two)):
        one, two = grow(one, bit_one), grow(two, bit_two)
        both = fence(*gains, *one, *two)
        gains = list(both[: len(gains)])
        one, two = grown(both[-4:-2], bit_one), grown(both[-2:], bit_two)
    bundle = grown(grow(jnp.concatenate([one, two], axis=0), bits[0]), bits[0])
    gains = sum(pick(gains, here ^ at) for at in range(len(masks)))
    sum_qkv = bundle[: 3 * width].reshape(3, width, local_cols).transpose(1, 0, 2).astype(F32)
    sum_attn = jnp.concatenate(
        [
            bundle[3 * width + at * local_cols : 3 * width + (at + 1) * local_cols]
            for at in range(wide)
        ],
        axis=1,
    ).astype(F32)
    *sum_w, sum_qkv, sum_attn = fence(*sum_w, sum_qkv, sum_attn)
    return (
        output,
        grad_tokens,
        gains[0],
        sum_qkv,
        sum_attn,
        gains[1],
        jnp.stack(sum_w[1:]).transpose(2, 0, 1).astype(F32),
        sum_w[0].astype(F32),
    )


def solution(mesh):
    return jax.shard_map(
        functools.partial(layer, ctx=mesh.shape["ctx"], tp=mesh.shape["tp"]),
        mesh=mesh,
        in_specs=(
            P("ctx", None),
            P("ctx"),
            P(),
            P(None, None, "tp"),
            P("tp", None),
            P(),
            P(None, None, "tp"),
            P("tp", None),
            P("ctx", None),
        ),
        out_specs=(
            P("ctx", None),
            P("ctx", None),
            P(),
            P(None, None, "tp"),
            P("tp", None),
            P(),
            P(None, None, "tp"),
            P("tp", None),
        ),
        check_vma=False,
    )
```

```python
import functools
import math

import jax
import jax.numpy as jnp
from jax import lax
from jax.experimental import pallas as pl
from jax.experimental.pallas import tpu as pltpu
from jax.sharding import PartitionSpec as P

HD = 64
EPS = 1e-05
BASE = 160000.0
MASKED = -1e30
ROOT_HALF = 0.7071067811865476
INV_ROOT_TWO_PI = 0.3989422804014327
SEQS = 4
F32 = jnp.float32
BF16 = jnp.bfloat16
PAD = 16


def layer_normalize(values_in, norm_gain_vector):
    token_average = jnp.mean(values_in, axis=-1, keepdims=True)
    centered_input = values_in - token_average
    inverse_deviation = lax.rsqrt(
        jnp.mean(centered_input * centered_input, axis=-1, keepdims=True) + EPS
    )
    standardized_input = centered_input * inverse_deviation
    return (standardized_input, inverse_deviation, standardized_input * norm_gain_vector)


def layer_normalize_backward(
    output_gradient, standardized_input, inverse_deviation, norm_gain_vector
):
    normalized_gradient = output_gradient * norm_gain_vector
    correction_term = jnp.mean(
        normalized_gradient, axis=-1, keepdims=True
    ) + standardized_input * jnp.mean(
        normalized_gradient * standardized_input, axis=-1, keepdims=True
    )
    return (
        inverse_deviation * (normalized_gradient - correction_term),
        jnp.sum(output_gradient * standardized_input, axis=0),
    )


def gelu_value(v):
    return v * 0.5 * (1.0 + lax.erf(v * ROOT_HALF))


def gelu_slope(v):
    return 0.5 * (1.0 + lax.erf(v * ROOT_HALF)) + v * jnp.exp(-0.5 * v * v) * INV_ROOT_TWO_PI


def rope_tables_t(positions, head_size):
    half = head_size // 2
    inverse = BASE ** (-(jnp.arange(half, dtype=F32) * (2.0 / head_size)))
    angle = inverse[:, None] * positions.astype(F32)[None, :]
    return (jnp.cos(angle), jnp.sin(angle))


def rotate_t(field, cosine, sine):
    half = field.shape[1] // 2
    one, two = field[:, :half], field[:, half:]
    return jnp.concatenate([one * cosine - two * sine, two * cosine + one * sine], axis=1)


def unrotate_t(grad, cosine, sine):
    half = grad.shape[1] // 2
    one, two = grad[:, :half], grad[:, half:]
    return jnp.concatenate([one * cosine + two * sine, two * cosine - one * sine], axis=1)


def fill_natural(kvn, own, oth, groups, count, chunk):
    for r in range(groups):
        for c in range(count // chunk):
            at = slice(c * chunk, (c + 1) * chunk)
            if r == 0:
                piece = own[HD : 3 * HD, at]
            else:
                piece = oth[r - 1, 0 : 2 * HD, at]
            kvn[r * count + c * chunk : r * count + (c + 1) * chunk, :] = (
                piece.astype(F32).T.astype(BF16)
            )


def forward_kernel(lo, hi, q_ref, own, oth, rows, out, lse, kvn, *, groups, count, kb):
    i = pl.program_id(0)

    @pl.when(i == 0)
    def _():
        fill_natural(kvn, own, oth, groups, count, min(count, 256))

    qb = q_ref.shape[1]
    q = (q_ref[...].astype(F32) * (1.0 / math.sqrt(HD))).astype(BF16)
    q = jnp.concatenate([q, jnp.zeros_like(q)], axis=0)
    spot = lax.broadcasted_iota(jnp.int32, (kb, qb), 0)
    carry = (
        jnp.full((1, qb), MASKED, F32),
        jnp.zeros((1, qb), F32),
        jnp.zeros((HD, qb), F32),
    )
    for r in range(groups):
        first = rows[r : r + 1, :]
        end = rows[groups + r : groups + r + 1, :]

        def step(j, carry, r=r, first=first, end=end):
            top, den, acc = carry
            k0 = pl.multiple_of(j * kb, kb)
            s = jnp.dot(kvn[pl.ds(r * count + k0, kb), :], q, preferred_element_type=F32)
            s = jnp.where((spot >= first - k0) & (spot < end - k0), s, MASKED)
            new = jnp.maximum(top, jnp.max(s, axis=0, keepdims=True))
            p = jnp.exp(s - new)
            fade = jnp.exp(top - new)
            den = den * fade + jnp.sum(p, axis=0, keepdims=True)
            if r == 0:
                v = own[2 * HD : 3 * HD, pl.ds(k0, kb)]
            else:
                v = oth[r - 1, HD : 2 * HD, pl.ds(k0, kb)]
            acc = acc * fade + jnp.dot(v, p.astype(BF16), preferred_element_type=F32)
            return (new, den, acc)

        carry = lax.fori_loop(
            lo[i * groups + r] // kb, (hi[i * groups + r] + kb - 1) // kb, step, carry
        )
    top, den, acc = carry
    out[...] = (acc / den).astype(BF16)
    lse[...] = top + jnp.log(den)


def backward_kernel(
    lo, hi, q_ref, own, oth, rows, out, do_ref, lse, dq, dkv, dkv_oth, kvn, acc,
    *, groups, count, kb
):
    i = pl.program_id(0)

    @pl.when(i == 0)
    def _():
        fill_natural(kvn, own, oth, groups, count, min(count, 256))
        acc[...] = jnp.zeros_like(acc)

    qb = q_ref.shape[1]
    scale = 1.0 / math.sqrt(HD)
    qf = q_ref[...].astype(F32) * scale
    q = qf.astype(BF16)
    do = do_ref[...]
    dof = do.astype(F32)
    delta = jnp.sum(dof * out[...].astype(F32), axis=0, keepdims=True)
    none = jnp.zeros_like(q)
    q_pad = jnp.concatenate([q, none], axis=0)
    do_pad = jnp.concatenate([none, do], axis=0)
    q_nat = jnp.concatenate([qf, jnp.zeros_like(qf)], axis=0).T.astype(BF16)
    do_nat = jnp.concatenate([jnp.zeros_like(dof), dof], axis=0).T.astype(BF16)
    spot = lax.broadcasted_iota(jnp.int32, (kb, qb), 0)
    level = lse[...]
    grad = jnp.zeros((HD, qb), F32)
    for r in range(groups):
        first = rows[r : r + 1, :]
        end = rows[groups + r : groups + r + 1, :]

        def step(j, grad, r=r, first=first, end=end):
            k0 = pl.multiple_of(j * kb, kb)
            at = pl.ds(r * count + k0, kb)
            kv = kvn[at, :]
            s = jnp.dot(kv, q_pad, preferred_element_type=F32)
            dp = jnp.dot(kv, do_pad, preferred_element_type=F32)
            p = jnp.where((spot >= first - k0) & (spot < end - k0), jnp.exp(s - level), 0.0)
            ds = (p * (dp - delta)).astype(BF16)
            acc[at, :] += jnp.dot(ds, q_nat, preferred_element_type=F32) + jnp.dot(
                p.astype(BF16), do_nat, preferred_element_type=F32
            )
            if r == 0:
                k = own[HD : 2 * HD, pl.ds(k0, kb)]
            else:
                k = oth[r - 1, 0:HD, pl.ds(k0, kb)]
            return grad + jnp.dot(k, ds, preferred_element_type=F32)

        grad = lax.fori_loop(
            lo[i * groups + r] // kb, (hi[i * groups + r] + kb - 1) // kb, step, grad
        )
    dq[...] = grad * scale

    @pl.when(i == pl.num_programs(0) - 1)
    def _():
        chunk = min(count, 256)
        for r in range(groups):
            for c in range(count // chunk):
                at = slice(c * chunk, (c + 1) * chunk)
                piece = acc[r * count + c * chunk : r * count + (c + 1) * chunk, :].T
                if r == 0:
                    dkv[:, at] = piece
                else:
                    dkv_oth[r - 1, :, at] = piece.astype(BF16)


def project_kernel(
    tokens, gain, weight, cosine, sine, ids, packed, first, average, inverse, *, groups, heads
):
    c = pl.program_id(0)
    part = packed.shape[3]

    @pl.when(c == 0)
    def _():
        x = tokens[...].astype(F32)
        mean = jnp.mean(x, axis=-1, keepdims=True)
        centered = x - mean
        inv = lax.rsqrt(jnp.mean(centered * centered, axis=-1, keepdims=True) + EPS)
        average[...] = mean
        inverse[...] = inv
        first[...] = (centered * inv * gain[...]).astype(BF16)
        mark = jnp.broadcast_to(ids[...], (PAD, ids.shape[1])).astype(BF16)
        for h in range(heads):
            for g in range(groups):
                packed[h, g, 3 * HD : 3 * HD + PAD, :] = mark[:, g * part : (g + 1) * part]

    proj = jnp.dot(first[...], weight[0], preferred_element_type=F32).T

    def store(h, at, rows):
        rows = rows.astype(BF16)
        for g in range(groups):
            packed[h, g, pl.ds(pl.multiple_of(at, HD // 2), rows.shape[0]), :] = rows[
                :, g * part : (g + 1) * part
            ]

    half = HD // 2
    turn = c < 2
    cos = jnp.where(turn, cosine[...], 1.0)
    sin = jnp.where(turn, sine[...], 0.0)
    for h in range(heads):
        one = proj[h * HD : h * HD + half]
        two = proj[h * HD + half : (h + 1) * HD]
        store(h, c * HD, one * cos - two * sin)
        store(h, c * HD + half, two * cos + one * sin)


def project(tokens, gain, weight, cosine, sine, ids, groups):
    rows, width = tokens.shape
    cols = weight.shape[2]
    heads = cols // HD
    shape = (heads, groups, 3 * HD + PAD, rows // groups)
    return pl.pallas_call(
        functools.partial(project_kernel, groups=groups, heads=heads),
        grid=(3,),
        in_specs=[
            whole((rows, width)),
            whole((1, width)),
            pl.BlockSpec((1, width, cols), lambda c: (c, 0, 0)),
            whole(cosine.shape),
            whole(sine.shape),
            whole((1, rows)),
        ],
        out_specs=[whole(shape), whole((rows, width)), whole((rows, 1)), whole((rows, 1))],
        out_shape=[
            jax.ShapeDtypeStruct(shape, BF16),
            jax.ShapeDtypeStruct((rows, width), BF16),
            jax.ShapeDtypeStruct((rows, 1), F32),
            jax.ShapeDtypeStruct((rows, 1), F32),
        ],
        name="project",
    )(tokens, gain, weight, cosine, sine, ids)


def blocks_of(count):
    return math.gcd(count, 256), math.gcd(count, 512)


def whole(shape):
    return pl.BlockSpec(shape, lambda i, *_: (0,) * len(shape))


def attention_forward(lo, hi, own, oth, rows, groups):
    count = own.shape[1]
    qb, kb = blocks_of(count)
    col = lambda height: pl.BlockSpec((height, qb), lambda i, *_: (0, i))
    return pl.pallas_call(
        functools.partial(forward_kernel, groups=groups, count=count, kb=kb),
        grid_spec=pltpu.PrefetchScalarGridSpec(
            num_scalar_prefetch=2,
            grid=(count // qb,),
            in_specs=[col(HD), whole(own.shape), whole(oth.shape), col(rows.shape[0])],
            out_specs=[col(HD), col(1)],
            scratch_shapes=[pltpu.VMEM((groups * count, 2 * HD), BF16)],
        ),
        out_shape=[
            jax.ShapeDtypeStruct((HD, count), BF16),
            jax.ShapeDtypeStruct((1, count), F32),
        ],
        name="attention_forward",
    )(lo, hi, own, own, oth, rows)


def attention_backward(lo, hi, own, oth, rows, out, do, lse, groups):
    count = own.shape[1]
    qb, kb = blocks_of(count)
    col = lambda height: pl.BlockSpec((height, qb), lambda i, *_: (0, i))
    others = (max(groups - 1, 1), 2 * HD, count)
    return pl.pallas_call(
        functools.partial(backward_kernel, groups=groups, count=count, kb=kb),
        grid_spec=pltpu.PrefetchScalarGridSpec(
            num_scalar_prefetch=2,
            grid=(count // qb,),
            in_specs=[
                col(HD), whole(own.shape), whole(oth.shape), col(rows.shape[0]),
                col(HD), col(HD), col(1),
            ],
            out_specs=[col(HD), whole((2 * HD, count)), whole(others)],
            scratch_shapes=[
                pltpu.VMEM((groups * count, 2 * HD), BF16),
                pltpu.VMEM((groups * count, 2 * HD), F32),
            ],
        ),
        out_shape=[
            jax.ShapeDtypeStruct((HD, count), F32),
            jax.ShapeDtypeStruct((2 * HD, count), F32),
            jax.ShapeDtypeStruct(others, BF16),
        ],
        name="attention_backward",
    )(lo, hi, own, own, oth, rows, out, do, lse)


def layer(
    tokens,
    seq_ids,
    attention_norm_gain,
    qkv_weight,
    out_weight,
    feedforward_norm_gain,
    mlp_in_weight,
    mlp_out_weight,
    grad_out,
    *,
    ctx,
    tp,
):
    tok_rows, width = tokens.shape
    local_cols = qkv_weight.shape[2]
    heads_here = local_cols // HD
    hidden_here = mlp_in_weight.shape[2]
    groups = ctx // heads_here
    part = tok_rows // groups
    count = ctx * part
    me = lax.axis_index("ctx")

    def tp_sum(value):
        value = value.astype(BF16)
        if tp == 2:
            other = lax.ppermute(value, "tp", [(0, 1), (1, 0)])
            return value.astype(F32) + other.astype(F32)
        return lax.psum(value, "tp").astype(F32)

    def to_group(value, r):
        pairs = [(i, i // groups * groups + (i + r) % groups) for i in range(ctx)]
        return lax.ppermute(value, "ctx", pairs)

    def for_heads(value):
        value = jnp.stack(
            [value[:, :, g * part : (g + 1) * part] for g in range(groups)], axis=1
        )
        return value.reshape(ctx, value.shape[2], part)

    def to_heads(chunks):
        value = lax.all_to_all(chunks, "ctx", 0, 0)
        return value.transpose(1, 0, 2).reshape(chunks.shape[1], count)

    def for_tokens(value):
        return value.reshape(value.shape[0], ctx, part).transpose(1, 0, 2)

    def to_tokens(chunks):
        value = lax.all_to_all(chunks, "ctx", 0, 0)
        value = value.reshape(heads_here, groups, chunks.shape[1], part)
        return jnp.concatenate([value[:, g] for g in range(groups)], axis=2)

    bits = list(range(ctx.bit_length() - 1))
    group_bits = list(range(groups.bit_length() - 1))
    head_bits = bits[len(group_bits) :]
    far_bits = bits[2:]

    def spread(bits):
        masks = [
            sum(((m >> at) & 1) << bit for at, bit in enumerate(bits))
            for m in range(1 << len(bits))
        ]
        here = sum((((me >> bit) & 1) << at) for at, bit in enumerate(bits))
        return masks, here

    def pick(pieces, index):
        value = pieces[0]
        for at in range(1, len(pieces)):
            value = jnp.where(index == at, pieces[at], value)
        return value

    def hop(value, mask):
        return lax.ppermute(value, "ctx", [(i, i ^ mask) for i in range(ctx)])

    def deal(value, bits, axis):
        masks, here = spread(bits)
        pieces = jnp.split(value, len(masks), axis=axis)
        return [pick(pieces, here ^ m) for m in range(len(masks))]

    def send_dealt(dealt, bits):
        masks, _ = spread(bits)
        return [dealt[0]] + [hop(dealt[m], masks[m]) for m in range(1, len(masks))]

    def total(pieces):
        return sum(piece.astype(F32) for piece in pieces).astype(BF16)

    def send_all(value, bits):
        masks, _ = spread(bits)
        return [value] + [hop(value, masks[m]) for m in range(1, len(masks))]

    def arrange(pieces, bits, axis):
        _, here = spread(bits)
        return jnp.concatenate(
            [pick(pieces, here ^ at) for at in range(len(pieces))], axis=axis
        )

    def halve(value, bit):
        return send_dealt(deal(value, [bit], 0), [bit])

    def grow(value, bit):
        return send_all(value, [bit])

    def grown(pieces, bit):
        return arrange(pieces, [bit], 0)

    def fence(*values):
        return lax.optimization_barrier(values)

    over_cols = (((1,), (1,)), ((), ()))
    over_rows = (((0,), (0,)), ((), ()))
    across = (((0,), (1,)), ((), ()))

    def dot(left, right, dims=(((1,), (0,)), ((), ()))):
        return lax.dot_general(left, right, dims, preferred_element_type=F32)

    input_tokens = tokens.astype(F32)
    planes = [qkv_weight[:, c] for c in range(3)]
    positions = me * tok_rows + jnp.arange(tok_rows, dtype=jnp.int32)
    cosine, sine = rope_tables_t(positions, HD)
    packed, first, average, attention_inverse_deviation = project(
        tokens,
        attention_norm_gain[None],
        qkv_weight.transpose(1, 0, 2),
        cosine,
        sine,
        seq_ids.astype(F32)[None],
        groups,
    )
    own = to_heads(packed.reshape(ctx, 3 * HD + PAD, part))
    if groups > 1:
        oth = jnp.stack([to_group(own[HD:], groups - r) for r in range(1, groups)])
    else:
        oth = own[None, HD:]
    id_own = own[3 * HD]
    id_all = jnp.concatenate([id_own[None], oth[: groups - 1, 2 * HD]], axis=0)
    marks = jnp.arange(SEQS + 1, dtype=F32)
    below = jnp.sum((id_all.astype(F32)[:, None, :] < marks[None, :, None]).astype(jnp.int32), -1)
    first_key = jnp.zeros((groups, count), jnp.int32)
    end_key = jnp.zeros((groups, count), jnp.int32)
    for s in range(SEQS):
        hit = (id_own == s)[None, :]
        first_key = jnp.where(hit, below[:, s : s + 1], first_key)
        end_key = jnp.where(hit, below[:, s + 1 : s + 2], end_key)
    rows = jnp.concatenate([first_key, end_key], axis=0)
    qb, _ = blocks_of(count)
    lo = first_key[:, ::qb].T.reshape(-1)
    hi = end_key[:, qb - 1 :: qb].T.reshape(-1)

    att_head, lse = attention_forward(lo, hi, own, oth, rows, groups)
    attended = to_tokens(for_tokens(att_head)).reshape(local_cols, tok_rows)
    attn_part = dot(attended, out_weight, over_rows)
    residual_middle = input_tokens + tp_sum(attn_part)
    feedforward_standardized, feedforward_inverse_deviation, feedforward_normed_input = (
        layer_normalize(residual_middle, feedforward_norm_gain)
    )
    second = feedforward_normed_input.astype(BF16)
    in_act = mlp_in_weight[:, 0]
    in_gate = mlp_in_weight[:, 1]
    act_in = dot(second, in_act)
    gate = dot(second, in_gate)
    hidden = (gelu_value(act_in) * gate).astype(BF16)
    upstream = grad_out.astype(F32)
    grad_hidden = dot(grad_out, mlp_out_weight, over_cols)
    grad_act = (grad_hidden * gate * gelu_slope(act_in)).astype(BF16)
    grad_gate = (grad_hidden * gelu_value(act_in)).astype(BF16)
    second_part = dot(grad_act, in_act, over_cols) + dot(grad_gate, in_gate, over_cols)
    second_part, second_w, act_w, gate_w, hidden_w = fence(
        second_part.astype(BF16), second, grad_act, grad_gate, hidden
    )
    feedforward_norm_gradient = tp_sum(second_part)
    grad_w = [
        dot(left, right, over_rows).astype(BF16)
        for left, right in ((hidden_w, grad_out), (act_w, second_w), (gate_w, second_w))
    ]
    feedforward_norm_gradient, *grad_w = fence(feedforward_norm_gradient, *grad_w)
    sum_w = lax.psum(tuple(grad_w), "ctx")
    feedforward_normed_gradient, feedforward_gain_gradient = layer_normalize_backward(
        feedforward_norm_gradient,
        feedforward_standardized,
        feedforward_inverse_deviation,
        feedforward_norm_gain,
    )
    grad_mid = upstream + feedforward_normed_gradient
    grad_mid_b = grad_mid.astype(BF16)
    grad_att = dot(out_weight, grad_mid_b, over_cols).astype(BF16)
    chunks = for_heads(grad_att.reshape(heads_here, HD, tok_rows))
    chunks, late_mid, late_hidden = fence(chunks, grad_mid_b, hidden_w)
    do_head = to_heads(chunks)

    wide = width // local_cols
    grad_w_attn = [
        dot(attended, late_mid[:, at * local_cols : (at + 1) * local_cols]).astype(BF16)
        for at in range(wide)
    ]
    ffn_part = dot(late_hidden, mlp_out_weight).astype(BF16)
    do_head, ffn_part, *grad_w_attn = fence(do_head, ffn_part, *grad_w_attn)

    output_sum = tp_sum(ffn_part)
    dq, dkv, dkv_oth = attention_backward(
        lo, hi, own, oth, rows, att_head, do_head, lse, groups
    )
    dq, dkv, dkv_oth, output_sum = fence(dq, dkv, dkv_oth, output_sum)
    for r in range(1, groups):
        dkv = dkv + to_group(dkv_oth[r - 1], r).astype(F32)
    place = me % groups
    spots = (
        jnp.arange(ctx, dtype=jnp.int32)[:, None] * tok_rows
        + place * part
        + jnp.arange(part, dtype=jnp.int32)[None, :]
    ).reshape(-1)
    cosine_head, sine_head = rope_tables_t(spots, HD)
    grads = jnp.concatenate(
        [
            unrotate_t(dq[None], cosine_head, sine_head)[0].astype(BF16),
            unrotate_t(dkv[None, :HD], cosine_head, sine_head)[0].astype(BF16),
            dkv[HD:].astype(BF16),
        ],
        axis=0,
    )
    chunks = for_tokens(grads)
    grad_proj = to_tokens(chunks)
    output = (residual_middle + output_sum).astype(BF16)
    grad_proj, output = fence(grad_proj, output)
    grad_planes = [
        grad_proj[:, c * HD : (c + 1) * HD].reshape(local_cols, tok_rows) for c in range(3)
    ]

    bundle = jnp.concatenate(
        [dot(first, plane, (((0,), (1,)), ((), ()))).astype(BF16) for plane in grad_planes]
        + grad_w_attn,
        axis=0,
    )
    first_send = deal(bundle, bits[:1], 0)
    grad_planes = fence(*grad_planes, *first_send)[:3]
    bundle = send_dealt(first_send, bits[:1])
    first_part = sum(
        dot(plane, weight, across) for plane, weight in zip(grad_planes, planes)
    ).astype(BF16)
    first_part, *bundle = fence(first_part, *bundle)
    one, two = jnp.split(total(bundle), 2)
    order_one = bits[1:]
    order_two = bits[2:3] + bits[1:2] + bits[3:]
    attention_norm_gradient = tp_sum(first_part)
    one, two = halve(one, order_one[0]), halve(two, order_two[0])
    attention_norm_gradient, *both = fence(attention_norm_gradient, *one, *two)
    one, two = total(both[:2]), total(both[2:])
    attention_standardized = (input_tokens - average) * attention_inverse_deviation
    attention_normed_gradient, attention_gain_gradient = layer_normalize_backward(
        attention_norm_gradient,
        attention_standardized,
        attention_inverse_deviation,
        attention_norm_gain,
    )
    grad_tokens = grad_mid + attention_normed_gradient
    lanes = one.shape[1]
    gains = jnp.stack([attention_gain_gradient, feedforward_gain_gradient]).reshape(-1, lanes)
    many = gains.shape[0]
    gains = jnp.pad(gains, ((0, -many % 16), (0, 0))).astype(BF16)

    def riding(send, bit, gains):
        came = hop(jnp.concatenate([send, gains], axis=0), 1 << bit)
        return came[: send.shape[0]], total([gains, came[send.shape[0] :]])

    for bit_one, bit_two in zip(order_one[1:], order_two[1:]):
        kept, send = deal(one, [bit_one], 0)
        came, gains = riding(send, bit_one, gains)
        kept, came, gains, *two = fence(kept, came, gains, *halve(two, bit_two))
        one, two = total([kept, came]), total(two)
    for bit_one, bit_two in zip(reversed(order_one), reversed(order_two)):
        if bit_one == order_one[0]:
            came, gains = riding(one, bit_one, gains)
            sums = [
                sum_w[0].astype(F32),
                jnp.stack(sum_w[1:]).transpose(2, 0, 1).astype(F32),
            ]
            came, gains, grad_tokens, *both = fence(
                came, gains, grad_tokens, *sums, *grow(two, bit_two)
            )
            sums, two = both[:2], both[2:]
            one = [one, came]
        else:
            both = fence(*grow(one, bit_one), *grow(two, bit_two))
            one, two = both[:2], both[2:]
        one, two = grown(one, bit_one), grown(two, bit_two)
    kept = jnp.concatenate([one, two], axis=0)
    came, gains = riding(kept, bits[0], gains)
    bundle = grown([kept, came], bits[0])
    gains = gains[:many].astype(F32).reshape(2, width)
    sum_qkv = bundle[: 3 * width].reshape(3, width, local_cols).transpose(1, 0, 2).astype(F32)
    sum_attn = jnp.concatenate(
        [
            bundle[3 * width + at * local_cols : 3 * width + (at + 1) * local_cols]
            for at in range(wide)
        ],
        axis=1,
    ).astype(F32)
    return (
        output,
        grad_tokens,
        gains[0],
        sum_qkv,
        sum_attn,
        gains[1],
        sums[1],
        sums[0],
    )


def solution(mesh):
    return jax.shard_map(
        functools.partial(layer, ctx=mesh.shape["ctx"], tp=mesh.shape["tp"]),
        mesh=mesh,
        in_specs=(
            P("ctx", None),
            P("ctx"),
            P(),
            P(None, None, "tp"),
            P("tp", None),
            P(),
            P(None, None, "tp"),
            P("tp", None),
            P("ctx", None),
        ),
        out_specs=(
            P("ctx", None),
            P("ctx", None),
            P(),
            P(None, None, "tp"),
            P("tp", None),
            P(),
            P(None, None, "tp"),
            P("tp", None),
        ),
        check_vma=False,
    )
```

```python
import functools
import math

import jax
import jax.numpy as jnp
from jax import lax
from jax.experimental import pallas as pl
from jax.experimental.pallas import tpu as pltpu
from jax.sharding import PartitionSpec as P

HD = 64
EPS = 1e-05
BASE = 160000.0
MASKED = -1e30
ROOT_HALF = 0.7071067811865476
INV_ROOT_TWO_PI = 0.3989422804014327
SEQS = 4
F32 = jnp.float32
BF16 = jnp.bfloat16
PAD = 16


def layer_normalize(values_in, norm_gain_vector):
    token_average = jnp.mean(values_in, axis=-1, keepdims=True)
    centered_input = values_in - token_average
    inverse_deviation = lax.rsqrt(
        jnp.mean(centered_input * centered_input, axis=-1, keepdims=True) + EPS
    )
    standardized_input = centered_input * inverse_deviation
    return (standardized_input, inverse_deviation, standardized_input * norm_gain_vector)


def layer_normalize_backward(
    output_gradient, standardized_input, inverse_deviation, norm_gain_vector
):
    normalized_gradient = output_gradient * norm_gain_vector
    correction_term = jnp.mean(
        normalized_gradient, axis=-1, keepdims=True
    ) + standardized_input * jnp.mean(
        normalized_gradient * standardized_input, axis=-1, keepdims=True
    )
    return (
        inverse_deviation * (normalized_gradient - correction_term),
        jnp.sum(output_gradient * standardized_input, axis=0),
    )


def gelu_value(v):
    return v * 0.5 * (1.0 + lax.erf(v * ROOT_HALF))


def gelu_slope(v):
    return 0.5 * (1.0 + lax.erf(v * ROOT_HALF)) + v * jnp.exp(-0.5 * v * v) * INV_ROOT_TWO_PI


def rope_tables_t(positions, head_size):
    half = head_size // 2
    inverse = BASE ** (-(jnp.arange(half, dtype=F32) * (2.0 / head_size)))
    angle = inverse[:, None] * positions.astype(F32)[None, :]
    return (jnp.cos(angle), jnp.sin(angle))


def rotate_t(field, cosine, sine):
    half = field.shape[1] // 2
    one, two = field[:, :half], field[:, half:]
    return jnp.concatenate([one * cosine - two * sine, two * cosine + one * sine], axis=1)


def unrotate_t(grad, cosine, sine):
    half = grad.shape[1] // 2
    one, two = grad[:, :half], grad[:, half:]
    return jnp.concatenate([one * cosine + two * sine, two * cosine - one * sine], axis=1)


def fill_natural(kvn, own, oth, groups, count, chunk):
    for r in range(groups):
        for c in range(count // chunk):
            at = slice(c * chunk, (c + 1) * chunk)
            if r == 0:
                piece = own[HD : 3 * HD, at]
            else:
                piece = oth[r - 1, 0 : 2 * HD, at]
            kvn[r * count + c * chunk : r * count + (c + 1) * chunk, :] = (
                piece.astype(F32).T.astype(BF16)
            )


def forward_kernel(lo, hi, q_ref, own, oth, rows, out, lse, kvn, *, groups, count, kb):
    i = pl.program_id(0)

    @pl.when(i == 0)
    def _():
        fill_natural(kvn, own, oth, groups, count, min(count, 256))

    qb = q_ref.shape[1]
    q = (q_ref[...].astype(F32) * (1.0 / math.sqrt(HD))).astype(BF16)
    q = jnp.concatenate([q, jnp.zeros_like(q)], axis=0)
    spot = lax.broadcasted_iota(jnp.int32, (kb, qb), 0)
    carry = (
        jnp.full((1, qb), MASKED, F32),
        jnp.zeros((1, qb), F32),
        jnp.zeros((HD, qb), F32),
    )
    for r in range(groups):
        first = rows[r : r + 1, :]
        end = rows[groups + r : groups + r + 1, :]

        def step(j, carry, r=r, first=first, end=end):
            top, den, acc = carry
            k0 = pl.multiple_of(j * kb, kb)
            s = jnp.dot(kvn[pl.ds(r * count + k0, kb), :], q, preferred_element_type=F32)
            s = jnp.where((spot >= first - k0) & (spot < end - k0), s, MASKED)
            new = jnp.maximum(top, jnp.max(s, axis=0, keepdims=True))
            p = jnp.exp(s - new)
            fade = jnp.exp(top - new)
            den = den * fade + jnp.sum(p, axis=0, keepdims=True)
            if r == 0:
                v = own[2 * HD : 3 * HD, pl.ds(k0, kb)]
            else:
                v = oth[r - 1, HD : 2 * HD, pl.ds(k0, kb)]
            acc = acc * fade + jnp.dot(v, p.astype(BF16), preferred_element_type=F32)
            return (new, den, acc)

        carry = lax.fori_loop(
            lo[i * groups + r] // kb, (hi[i * groups + r] + kb - 1) // kb, step, carry
        )
    top, den, acc = carry
    out[...] = (acc / den).astype(BF16)
    lse[...] = top + jnp.log(den)


def backward_kernel(
    lo, hi, q_ref, own, oth, rows, out, do_ref, lse, dq, dkv, dkv_oth, kvn, acc,
    *, groups, count, kb
):
    i = pl.program_id(0)

    @pl.when(i == 0)
    def _():
        fill_natural(kvn, own, oth, groups, count, min(count, 256))
        acc[...] = jnp.zeros_like(acc)

    qb = q_ref.shape[1]
    scale = 1.0 / math.sqrt(HD)
    qf = q_ref[...].astype(F32) * scale
    q = qf.astype(BF16)
    do = do_ref[...]
    dof = do.astype(F32)
    delta = jnp.sum(dof * out[...].astype(F32), axis=0, keepdims=True)
    none = jnp.zeros_like(q)
    q_pad = jnp.concatenate([q, none], axis=0)
    do_pad = jnp.concatenate([none, do], axis=0)
    q_nat = jnp.concatenate([qf, jnp.zeros_like(qf)], axis=0).T.astype(BF16)
    do_nat = jnp.concatenate([jnp.zeros_like(dof), dof], axis=0).T.astype(BF16)
    spot = lax.broadcasted_iota(jnp.int32, (kb, qb), 0)
    level = lse[...]
    grad = jnp.zeros((HD, qb), F32)
    for r in range(groups):
        first = rows[r : r + 1, :]
        end = rows[groups + r : groups + r + 1, :]

        def step(j, grad, r=r, first=first, end=end):
            k0 = pl.multiple_of(j * kb, kb)
            at = pl.ds(r * count + k0, kb)
            kv = kvn[at, :]
            s = jnp.dot(kv, q_pad, preferred_element_type=F32)
            dp = jnp.dot(kv, do_pad, preferred_element_type=F32)
            p = jnp.where((spot >= first - k0) & (spot < end - k0), jnp.exp(s - level), 0.0)
            ds = (p * (dp - delta)).astype(BF16)
            acc[at, :] += jnp.dot(ds, q_nat, preferred_element_type=F32) + jnp.dot(
                p.astype(BF16), do_nat, preferred_element_type=F32
            )
            if r == 0:
                k = own[HD : 2 * HD, pl.ds(k0, kb)]
            else:
                k = oth[r - 1, 0:HD, pl.ds(k0, kb)]
            return grad + jnp.dot(k, ds, preferred_element_type=F32)

        grad = lax.fori_loop(
            lo[i * groups + r] // kb, (hi[i * groups + r] + kb - 1) // kb, step, grad
        )
    dq[...] = grad * scale

    @pl.when(i == pl.num_programs(0) - 1)
    def _():
        chunk = min(count, 256)
        for r in range(groups):
            for c in range(count // chunk):
                at = slice(c * chunk, (c + 1) * chunk)
                piece = acc[r * count + c * chunk : r * count + (c + 1) * chunk, :].T
                if r == 0:
                    dkv[:, at] = piece
                else:
                    dkv_oth[r - 1, :, at] = piece.astype(BF16)


def project_kernel(
    tokens, gain, weight, cosine, sine, ids, packed, first, average, inverse, *, groups, heads
):
    c = pl.program_id(0)
    part = packed.shape[3]

    @pl.when(c == 0)
    def _():
        x = tokens[...].astype(F32)
        mean = jnp.mean(x, axis=-1, keepdims=True)
        centered = x - mean
        inv = lax.rsqrt(jnp.mean(centered * centered, axis=-1, keepdims=True) + EPS)
        average[...] = mean
        inverse[...] = inv
        first[...] = (centered * inv * gain[...]).astype(BF16)
        mark = jnp.broadcast_to(ids[...].astype(F32), (PAD, ids.shape[1])).astype(BF16)
        for h in range(heads):
            for g in range(groups):
                packed[h, g, 3 * HD : 3 * HD + PAD, :] = mark[:, g * part : (g + 1) * part]

    proj = jnp.dot(first[...], weight[0], preferred_element_type=F32).T

    def store(h, at, rows):
        rows = rows.astype(BF16)
        for g in range(groups):
            packed[h, g, pl.ds(pl.multiple_of(at, HD // 2), rows.shape[0]), :] = rows[
                :, g * part : (g + 1) * part
            ]

    half = HD // 2
    turn = c < 2
    cos = jnp.where(turn, cosine[...], 1.0)
    sin = jnp.where(turn, sine[...], 0.0)
    for h in range(heads):
        one = proj[h * HD : h * HD + half]
        two = proj[h * HD + half : (h + 1) * HD]
        store(h, c * HD, one * cos - two * sin)
        store(h, c * HD + half, two * cos + one * sin)


def project(tokens, gain, weight, cosine, sine, ids, groups):
    rows, width = tokens.shape
    cols = weight.shape[2]
    heads = cols // HD
    shape = (heads, groups, 3 * HD + PAD, rows // groups)
    return pl.pallas_call(
        functools.partial(project_kernel, groups=groups, heads=heads),
        grid=(3,),
        in_specs=[
            whole((rows, width)),
            whole((1, width)),
            pl.BlockSpec((1, width, cols), lambda c: (c, 0, 0)),
            whole(cosine.shape),
            whole(sine.shape),
            whole((1, rows)),
        ],
        out_specs=[whole(shape), whole((rows, width)), whole((rows, 1)), whole((rows, 1))],
        out_shape=[
            jax.ShapeDtypeStruct(shape, BF16),
            jax.ShapeDtypeStruct((rows, width), BF16),
            jax.ShapeDtypeStruct((rows, 1), F32),
            jax.ShapeDtypeStruct((rows, 1), F32),
        ],
        name="project",
    )(tokens, gain, weight, cosine, sine, ids)


def blocks_of(count):
    return math.gcd(count, 256), math.gcd(count, 512)


def whole(shape):
    return pl.BlockSpec(shape, lambda i, *_: (0,) * len(shape))


def attention_forward(lo, hi, own, oth, rows, groups):
    count = own.shape[1]
    qb, kb = blocks_of(count)
    col = lambda height: pl.BlockSpec((height, qb), lambda i, *_: (0, i))
    return pl.pallas_call(
        functools.partial(forward_kernel, groups=groups, count=count, kb=kb),
        grid_spec=pltpu.PrefetchScalarGridSpec(
            num_scalar_prefetch=2,
            grid=(count // qb,),
            in_specs=[col(HD), whole(own.shape), whole(oth.shape), col(rows.shape[0])],
            out_specs=[col(HD), col(1)],
            scratch_shapes=[pltpu.VMEM((groups * count, 2 * HD), BF16)],
        ),
        out_shape=[
            jax.ShapeDtypeStruct((HD, count), BF16),
            jax.ShapeDtypeStruct((1, count), F32),
        ],
        name="attention_forward",
    )(lo, hi, own, own, oth, rows)


def attention_backward(lo, hi, own, oth, rows, out, do, lse, groups):
    count = own.shape[1]
    qb, kb = blocks_of(count)
    col = lambda height: pl.BlockSpec((height, qb), lambda i, *_: (0, i))
    others = (max(groups - 1, 1), 2 * HD, count)
    return pl.pallas_call(
        functools.partial(backward_kernel, groups=groups, count=count, kb=kb),
        grid_spec=pltpu.PrefetchScalarGridSpec(
            num_scalar_prefetch=2,
            grid=(count // qb,),
            in_specs=[
                col(HD), whole(own.shape), whole(oth.shape), col(rows.shape[0]),
                col(HD), col(HD), col(1),
            ],
            out_specs=[col(HD), whole((2 * HD, count)), whole(others)],
            scratch_shapes=[
                pltpu.VMEM((groups * count, 2 * HD), BF16),
                pltpu.VMEM((groups * count, 2 * HD), F32),
            ],
        ),
        out_shape=[
            jax.ShapeDtypeStruct((HD, count), F32),
            jax.ShapeDtypeStruct((2 * HD, count), F32),
            jax.ShapeDtypeStruct(others, BF16),
        ],
        name="attention_backward",
    )(lo, hi, own, own, oth, rows, out, do, lse)


def layer(
    tokens,
    seq_ids,
    attention_norm_gain,
    qkv_weight,
    out_weight,
    feedforward_norm_gain,
    mlp_in_weight,
    mlp_out_weight,
    grad_out,
    *,
    ctx,
    tp,
):
    tok_rows, width = tokens.shape
    local_cols = qkv_weight.shape[2]
    heads_here = local_cols // HD
    hidden_here = mlp_in_weight.shape[2]
    groups = ctx // heads_here
    part = tok_rows // groups
    count = ctx * part
    me = lax.axis_index("ctx")

    def tp_sum(value):
        value = value.astype(BF16)
        if tp == 2:
            other = lax.ppermute(value, "tp", [(0, 1), (1, 0)])
            return value.astype(F32) + other.astype(F32)
        return lax.psum(value, "tp").astype(F32)

    def to_group(value, r):
        pairs = [(i, i // groups * groups + (i + r) % groups) for i in range(ctx)]
        return lax.ppermute(value, "ctx", pairs)

    def for_heads(value):
        value = jnp.stack(
            [value[:, :, g * part : (g + 1) * part] for g in range(groups)], axis=1
        )
        return value.reshape(ctx, value.shape[2], part)

    def to_heads(chunks):
        value = lax.all_to_all(chunks, "ctx", 0, 0)
        return value.transpose(1, 0, 2).reshape(chunks.shape[1], count)

    def for_tokens(value):
        return value.reshape(value.shape[0], ctx, part).transpose(1, 0, 2)

    def to_tokens(chunks):
        value = lax.all_to_all(chunks, "ctx", 0, 0)
        value = value.reshape(heads_here, groups, chunks.shape[1], part)
        return jnp.concatenate([value[:, g] for g in range(groups)], axis=2)

    bits = list(range(ctx.bit_length() - 1))
    group_bits = list(range(groups.bit_length() - 1))
    head_bits = bits[len(group_bits) :]
    far_bits = bits[2:]

    def spread(bits):
        masks = [
            sum(((m >> at) & 1) << bit for at, bit in enumerate(bits))
            for m in range(1 << len(bits))
        ]
        here = sum((((me >> bit) & 1) << at) for at, bit in enumerate(bits))
        return masks, here

    def pick(pieces, index):
        value = pieces[0]
        for at in range(1, len(pieces)):
            value = jnp.where(index == at, pieces[at], value)
        return value

    def hop(value, mask):
        return lax.ppermute(value, "ctx", [(i, i ^ mask) for i in range(ctx)])

    def deal(value, bits, axis):
        masks, here = spread(bits)
        pieces = jnp.split(value, len(masks), axis=axis)
        return [pick(pieces, here ^ m) for m in range(len(masks))]

    def send_dealt(dealt, bits):
        masks, _ = spread(bits)
        return [dealt[0]] + [hop(dealt[m], masks[m]) for m in range(1, len(masks))]

    def total(pieces):
        return sum(piece.astype(F32) for piece in pieces).astype(BF16)

    def send_all(value, bits):
        masks, _ = spread(bits)
        return [value] + [hop(value, masks[m]) for m in range(1, len(masks))]

    def arrange(pieces, bits, axis):
        _, here = spread(bits)
        return jnp.concatenate(
            [pick(pieces, here ^ at) for at in range(len(pieces))], axis=axis
        )

    def halve(value, bit):
        return send_dealt(deal(value, [bit], 0), [bit])

    def grow(value, bit):
        return send_all(value, [bit])

    def grown(pieces, bit):
        return arrange(pieces, [bit], 0)

    def fence(*values):
        return lax.optimization_barrier(values)

    over_cols = (((1,), (1,)), ((), ()))
    over_rows = (((0,), (0,)), ((), ()))
    across = (((0,), (1,)), ((), ()))

    def dot(left, right, dims=(((1,), (0,)), ((), ()))):
        return lax.dot_general(left, right, dims, preferred_element_type=F32)

    input_tokens = tokens.astype(F32)
    planes = [qkv_weight[:, c] for c in range(3)]
    positions = me * tok_rows + jnp.arange(tok_rows, dtype=jnp.int32)
    cosine, sine = rope_tables_t(positions, HD)
    packed, first, average, attention_inverse_deviation = project(
        tokens,
        attention_norm_gain[None],
        qkv_weight.transpose(1, 0, 2),
        cosine,
        sine,
        seq_ids[None],
        groups,
    )
    own = to_heads(packed.reshape(ctx, 3 * HD + PAD, part))
    if groups > 1:
        oth = jnp.stack([to_group(own[HD:], groups - r) for r in range(1, groups)])
    else:
        oth = own[None, HD:]
    id_own = own[3 * HD]
    id_all = jnp.concatenate([id_own[None], oth[: groups - 1, 2 * HD]], axis=0)
    marks = jnp.arange(SEQS + 1, dtype=F32)
    below = jnp.sum((id_all.astype(F32)[:, None, :] < marks[None, :, None]).astype(jnp.int32), -1)
    first_key = jnp.zeros((groups, count), jnp.int32)
    end_key = jnp.zeros((groups, count), jnp.int32)
    for s in range(SEQS):
        hit = (id_own == s)[None, :]
        first_key = jnp.where(hit, below[:, s : s + 1], first_key)
        end_key = jnp.where(hit, below[:, s + 1 : s + 2], end_key)
    rows = jnp.concatenate([first_key, end_key], axis=0)
    qb, _ = blocks_of(count)
    lo = first_key[:, ::qb].T.reshape(-1)
    hi = end_key[:, qb - 1 :: qb].T.reshape(-1)

    att_head, lse = attention_forward(lo, hi, own, oth, rows, groups)
    attended = to_tokens(for_tokens(att_head)).reshape(local_cols, tok_rows)
    attn_part = dot(attended, out_weight, over_rows)
    residual_middle = input_tokens + tp_sum(attn_part)
    feedforward_standardized, feedforward_inverse_deviation, feedforward_normed_input = (
        layer_normalize(residual_middle, feedforward_norm_gain)
    )
    second = feedforward_normed_input.astype(BF16)
    in_act = mlp_in_weight[:, 0]
    in_gate = mlp_in_weight[:, 1]
    act_in = dot(second, in_act)
    gate = dot(second, in_gate)
    hidden = (gelu_value(act_in) * gate).astype(BF16)
    upstream = grad_out.astype(F32)
    grad_hidden = dot(grad_out, mlp_out_weight, over_cols)
    grad_act = (grad_hidden * gate * gelu_slope(act_in)).astype(BF16)
    grad_gate = (grad_hidden * gelu_value(act_in)).astype(BF16)
    second_part = dot(grad_act, in_act, over_cols) + dot(grad_gate, in_gate, over_cols)
    second_part, second_w, act_w, gate_w, hidden_w = fence(
        second_part.astype(BF16), second, grad_act, grad_gate, hidden
    )
    feedforward_norm_gradient = tp_sum(second_part)
    grad_w = [
        dot(left, right, over_rows).astype(BF16)
        for left, right in ((hidden_w, grad_out), (act_w, second_w), (gate_w, second_w))
    ]
    feedforward_norm_gradient, *grad_w = fence(feedforward_norm_gradient, *grad_w)
    sum_w = lax.psum(tuple(grad_w), "ctx")
    feedforward_normed_gradient, feedforward_gain_gradient = layer_normalize_backward(
        feedforward_norm_gradient,
        feedforward_standardized,
        feedforward_inverse_deviation,
        feedforward_norm_gain,
    )
    grad_mid = upstream + feedforward_normed_gradient
    grad_mid_b = grad_mid.astype(BF16)
    grad_att = dot(out_weight, grad_mid_b, over_cols).astype(BF16)
    chunks = for_heads(grad_att.reshape(heads_here, HD, tok_rows))
    chunks, late_mid, late_hidden = fence(chunks, grad_mid_b, hidden_w)
    do_head = to_heads(chunks)

    wide = width // local_cols
    grad_w_attn = [
        dot(attended, late_mid[:, at * local_cols : (at + 1) * local_cols]).astype(BF16)
        for at in range(wide)
    ]
    ffn_part = dot(late_hidden, mlp_out_weight).astype(BF16)
    do_head, ffn_part, *grad_w_attn = fence(do_head, ffn_part, *grad_w_attn)

    output_sum = tp_sum(ffn_part)
    dq, dkv, dkv_oth = attention_backward(
        lo, hi, own, oth, rows, att_head, do_head, lse, groups
    )
    dq, dkv, dkv_oth, output_sum = fence(dq, dkv, dkv_oth, output_sum)
    for r in range(1, groups):
        dkv = dkv + to_group(dkv_oth[r - 1], r).astype(F32)
    place = me % groups
    spots = (
        jnp.arange(ctx, dtype=jnp.int32)[:, None] * tok_rows
        + place * part
        + jnp.arange(part, dtype=jnp.int32)[None, :]
    ).reshape(-1)
    cosine_head, sine_head = rope_tables_t(spots, HD)
    grads = jnp.concatenate(
        [
            unrotate_t(dq[None], cosine_head, sine_head)[0].astype(BF16),
            unrotate_t(dkv[None, :HD], cosine_head, sine_head)[0].astype(BF16),
            dkv[HD:].astype(BF16),
        ],
        axis=0,
    )
    chunks = for_tokens(grads)
    grad_proj = to_tokens(chunks)
    output = (residual_middle + output_sum).astype(BF16)
    grad_proj, output = fence(grad_proj, output)
    grad_planes = [
        grad_proj[:, c * HD : (c + 1) * HD].reshape(local_cols, tok_rows) for c in range(3)
    ]

    bundle = jnp.concatenate(
        [dot(first, plane, (((0,), (1,)), ((), ()))).astype(BF16) for plane in grad_planes]
        + grad_w_attn,
        axis=0,
    )
    first_send = deal(bundle, bits[:1], 0)
    *grad_planes, kept, send = fence(*grad_planes, *first_send)
    first_part = dot(grad_planes[0], planes[0], across) + dot(grad_planes[1], planes[1], across)
    first_part, *bundle = fence(first_part, *send_dealt([kept, send], bits[:1]))
    one, two = jnp.split(total(bundle), 2)
    order_one = bits[1:]
    order_two = bits[2:3] + bits[1:2] + bits[3:]
    one, two = deal(one, order_one[:1], 0), deal(two, order_two[:1], 0)
    last_plane, *both = fence(grad_planes[2], *one, *two)
    one, two = send_dealt(both[:2], order_one[:1]), send_dealt(both[2:], order_two[:1])
    first_part = (first_part + dot(last_plane, planes[2], across)).astype(BF16)
    attention_norm_gradient = tp_sum(first_part)
    one, two = total(one), total(two)
    for bit_one, bit_two in zip(order_one[1:-1], order_two[1:-1]):
        both = fence(*halve(one, bit_one), *halve(two, bit_two))
        one, two = total(both[:2]), total(both[2:])
    attention_standardized = (input_tokens - average) * attention_inverse_deviation
    attention_normed_gradient, attention_gain_gradient = layer_normalize_backward(
        attention_norm_gradient,
        attention_standardized,
        attention_inverse_deviation,
        attention_norm_gain,
    )
    grad_tokens = grad_mid + attention_normed_gradient
    lanes = one.shape[1]
    gains = jnp.stack([attention_gain_gradient, feedforward_gain_gradient]).reshape(-1, lanes)
    many = gains.shape[0]
    gains = jnp.pad(gains, ((0, -many % 16), (0, 0))).astype(BF16)

    def riding(send, bit, gains):
        came = hop(jnp.concatenate([send, gains], axis=0), 1 << bit)
        return came[: send.shape[0]], total([gains, came[send.shape[0] :]])

    both = jnp.concatenate([one, two], axis=0)
    came, gains = riding(both, order_one[-1], gains)
    both, came, gains, grad_tokens = fence(both, came, gains, grad_tokens)
    one, two = jnp.split(total([both, came]), 2)
    for bit_one, bit_two in zip(reversed(order_one[:-1]), reversed(order_two[:-1])):
        came, gains = riding(one, bit_one, gains)
        sums = []
        if bit_one == order_one[0]:
            sums = [
                sum_w[0].astype(F32),
                jnp.stack(sum_w[1:]).transpose(2, 0, 1).astype(F32),
            ]
        came, gains, *both = fence(came, gains, *grow(two, bit_two), *sums)
        one, two = grown([one, came], bit_one), grown(both[:2], bit_two)
    sums = both[2:]
    kept = jnp.concatenate([one, two], axis=0)
    came, gains = riding(kept, bits[0], gains)
    bundle = grown([kept, came], bits[0])
    gains = gains[:many].astype(F32).reshape(2, width)
    sum_qkv = bundle[: 3 * width].reshape(3, width, local_cols).transpose(1, 0, 2).astype(F32)
    sum_attn = jnp.concatenate(
        [
            bundle[3 * width + at * local_cols : 3 * width + (at + 1) * local_cols]
            for at in range(wide)
        ],
        axis=1,
    ).astype(F32)
    return (
        output,
        grad_tokens,
        gains[0],
        sum_qkv,
        sum_attn,
        gains[1],
        sums[1],
        sums[0],
    )


def solution(mesh):
    return jax.shard_map(
        functools.partial(layer, ctx=mesh.shape["ctx"], tp=mesh.shape["tp"]),
        mesh=mesh,
        in_specs=(
            P("ctx", None),
            P("ctx"),
            P(),
            P(None, None, "tp"),
            P("tp", None),
            P(),
            P(None, None, "tp"),
            P("tp", None),
            P("ctx", None),
        ),
        out_specs=(
            P("ctx", None),
            P("ctx", None),
            P(),
            P(None, None, "tp"),
            P("tp", None),
            P(),
            P(None, None, "tp"),
            P("tp", None),
        ),
        check_vma=False,
    )
```

```python
import functools
import math

import jax
import jax.numpy as jnp
from jax import lax
from jax.experimental import pallas as pl
from jax.experimental.pallas import tpu as pltpu
from jax.sharding import PartitionSpec as P

HD = 64
EPS = 1e-05
BASE = 160000.0
MASKED = -1e30
ROOT_HALF = 0.7071067811865476
INV_ROOT_TWO_PI = 0.3989422804014327
SEQS = 4
F32 = jnp.float32
BF16 = jnp.bfloat16
PAD = 16


def layer_normalize(values_in, norm_gain_vector):
    token_average = jnp.mean(values_in, axis=-1, keepdims=True)
    centered_input = values_in - token_average
    inverse_deviation = lax.rsqrt(
        jnp.mean(centered_input * centered_input, axis=-1, keepdims=True) + EPS
    )
    standardized_input = centered_input * inverse_deviation
    return (standardized_input, inverse_deviation, standardized_input * norm_gain_vector)


def layer_normalize_backward(
    output_gradient, standardized_input, inverse_deviation, norm_gain_vector
):
    normalized_gradient = output_gradient * norm_gain_vector
    correction_term = jnp.mean(
        normalized_gradient, axis=-1, keepdims=True
    ) + standardized_input * jnp.mean(
        normalized_gradient * standardized_input, axis=-1, keepdims=True
    )
    return (
        inverse_deviation * (normalized_gradient - correction_term),
        jnp.sum(output_gradient * standardized_input, axis=0),
    )


def gelu_value(v):
    return v * 0.5 * (1.0 + lax.erf(v * ROOT_HALF))


def gelu_slope(v):
    return 0.5 * (1.0 + lax.erf(v * ROOT_HALF)) + v * jnp.exp(-0.5 * v * v) * INV_ROOT_TWO_PI


def rope_tables_t(positions, head_size):
    half = head_size // 2
    inverse = BASE ** (-(jnp.arange(half, dtype=F32) * (2.0 / head_size)))
    angle = inverse[:, None] * positions.astype(F32)[None, :]
    return (jnp.cos(angle), jnp.sin(angle))


def rotate_t(field, cosine, sine):
    half = field.shape[1] // 2
    one, two = field[:, :half], field[:, half:]
    return jnp.concatenate([one * cosine - two * sine, two * cosine + one * sine], axis=1)


def unrotate_t(grad, cosine, sine):
    half = grad.shape[1] // 2
    one, two = grad[:, :half], grad[:, half:]
    return jnp.concatenate([one * cosine + two * sine, two * cosine - one * sine], axis=1)


def fill_natural(kvn, own, oth, groups, count, chunk):
    for r in range(groups):
        for c in range(count // chunk):
            at = slice(c * chunk, (c + 1) * chunk)
            if r == 0:
                piece = own[HD : 3 * HD, at]
            else:
                piece = oth[r - 1, 0 : 2 * HD, at]
            kvn[r * count + c * chunk : r * count + (c + 1) * chunk, :] = (
                piece.astype(F32).T.astype(BF16)
            )


def forward_kernel(lo, hi, q_ref, own, oth, rows, out, lse, kvn, *, groups, count, kb):
    i = pl.program_id(0)

    @pl.when(i == 0)
    def _():
        fill_natural(kvn, own, oth, groups, count, min(count, 256))

    qb = q_ref.shape[1]
    q = (q_ref[...].astype(F32) * (1.0 / math.sqrt(HD))).astype(BF16)
    q = jnp.concatenate([q, jnp.zeros_like(q)], axis=0)
    spot = lax.broadcasted_iota(jnp.int32, (kb, qb), 0)
    carry = (
        jnp.full((1, qb), MASKED, F32),
        jnp.zeros((1, qb), F32),
        jnp.zeros((HD, qb), F32),
    )
    for r in range(groups):
        first = rows[r : r + 1, :]
        end = rows[groups + r : groups + r + 1, :]

        def step(j, carry, r=r, first=first, end=end):
            top, den, acc = carry
            k0 = pl.multiple_of(j * kb, kb)
            s = jnp.dot(kvn[pl.ds(r * count + k0, kb), :], q, preferred_element_type=F32)
            s = jnp.where((spot >= first - k0) & (spot < end - k0), s, MASKED)
            new = jnp.maximum(top, jnp.max(s, axis=0, keepdims=True))
            p = jnp.exp(s - new)
            fade = jnp.exp(top - new)
            den = den * fade + jnp.sum(p, axis=0, keepdims=True)
            if r == 0:
                v = own[2 * HD : 3 * HD, pl.ds(k0, kb)]
            else:
                v = oth[r - 1, HD : 2 * HD, pl.ds(k0, kb)]
            acc = acc * fade + jnp.dot(v, p.astype(BF16), preferred_element_type=F32)
            return (new, den, acc)

        carry = lax.fori_loop(
            lo[i * groups + r] // kb, (hi[i * groups + r] + kb - 1) // kb, step, carry
        )
    top, den, acc = carry
    out[...] = (acc / den).astype(BF16)
    lse[...] = top + jnp.log(den)


def backward_kernel(
    lo, hi, q_ref, own, oth, rows, out, do_ref, lse, dq, dkv, dkv_oth, kvn, acc,
    *, groups, count, kb
):
    i = pl.program_id(0)

    @pl.when(i == 0)
    def _():
        fill_natural(kvn, own, oth, groups, count, min(count, 256))
        acc[...] = jnp.zeros_like(acc)

    qb = q_ref.shape[1]
    scale = 1.0 / math.sqrt(HD)
    qf = q_ref[...].astype(F32) * scale
    q = qf.astype(BF16)
    do = do_ref[...]
    dof = do.astype(F32)
    delta = jnp.sum(dof * out[...].astype(F32), axis=0, keepdims=True)
    none = jnp.zeros_like(q)
    q_pad = jnp.concatenate([q, none], axis=0)
    do_pad = jnp.concatenate([none, do], axis=0)
    q_nat = jnp.concatenate([qf, jnp.zeros_like(qf)], axis=0).T.astype(BF16)
    do_nat = jnp.concatenate([jnp.zeros_like(dof), dof], axis=0).T.astype(BF16)
    spot = lax.broadcasted_iota(jnp.int32, (kb, qb), 0)
    level = lse[...]
    grad = jnp.zeros((HD, qb), F32)
    for r in range(groups):
        first = rows[r : r + 1, :]
        end = rows[groups + r : groups + r + 1, :]

        def step(j, grad, r=r, first=first, end=end):
            k0 = pl.multiple_of(j * kb, kb)
            at = pl.ds(r * count + k0, kb)
            kv = kvn[at, :]
            s = jnp.dot(kv, q_pad, preferred_element_type=F32)
            dp = jnp.dot(kv, do_pad, preferred_element_type=F32)
            p = jnp.where((spot >= first - k0) & (spot < end - k0), jnp.exp(s - level), 0.0)
            ds = (p * (dp - delta)).astype(BF16)
            acc[at, :] += jnp.dot(ds, q_nat, preferred_element_type=F32) + jnp.dot(
                p.astype(BF16), do_nat, preferred_element_type=F32
            )
            if r == 0:
                k = own[HD : 2 * HD, pl.ds(k0, kb)]
            else:
                k = oth[r - 1, 0:HD, pl.ds(k0, kb)]
            return grad + jnp.dot(k, ds, preferred_element_type=F32)

        grad = lax.fori_loop(
            lo[i * groups + r] // kb, (hi[i * groups + r] + kb - 1) // kb, step, grad
        )
    dq[...] = grad * scale

    @pl.when(i == pl.num_programs(0) - 1)
    def _():
        chunk = min(count, 256)
        for r in range(groups):
            for c in range(count // chunk):
                at = slice(c * chunk, (c + 1) * chunk)
                piece = acc[r * count + c * chunk : r * count + (c + 1) * chunk, :].T
                if r == 0:
                    dkv[:, at] = piece
                else:
                    dkv_oth[r - 1, :, at] = piece.astype(BF16)


def project_kernel(
    tokens, gain, weight, cosine, sine, ids, packed, first, average, inverse, *, groups, heads
):
    c = pl.program_id(0)
    part = packed.shape[3]

    @pl.when(c == 0)
    def _():
        x = tokens[...].astype(F32)
        mean = jnp.mean(x, axis=-1, keepdims=True)
        centered = x - mean
        inv = lax.rsqrt(jnp.mean(centered * centered, axis=-1, keepdims=True) + EPS)
        average[...] = mean
        inverse[...] = inv
        first[...] = (centered * inv * gain[...]).astype(BF16)
        mark = jnp.broadcast_to(ids[...].astype(F32), (PAD, ids.shape[1])).astype(BF16)
        for h in range(heads):
            for g in range(groups):
                packed[h, g, 3 * HD : 3 * HD + PAD, :] = mark[:, g * part : (g + 1) * part]

    proj = jnp.dot(first[...], weight[0], preferred_element_type=F32).T

    def store(h, at, rows):
        rows = rows.astype(BF16)
        for g in range(groups):
            packed[h, g, pl.ds(pl.multiple_of(at, HD // 2), rows.shape[0]), :] = rows[
                :, g * part : (g + 1) * part
            ]

    half = HD // 2
    turn = c < 2
    cos = jnp.where(turn, cosine[...], 1.0)
    sin = jnp.where(turn, sine[...], 0.0)
    for h in range(heads):
        one = proj[h * HD : h * HD + half]
        two = proj[h * HD + half : (h + 1) * HD]
        store(h, c * HD, one * cos - two * sin)
        store(h, c * HD + half, two * cos + one * sin)


def project(tokens, gain, weight, cosine, sine, ids, groups):
    rows, width = tokens.shape
    cols = weight.shape[2]
    heads = cols // HD
    shape = (heads, groups, 3 * HD + PAD, rows // groups)
    return pl.pallas_call(
        functools.partial(project_kernel, groups=groups, heads=heads),
        grid=(3,),
        in_specs=[
            whole((rows, width)),
            whole((1, width)),
            pl.BlockSpec((1, width, cols), lambda c: (c, 0, 0)),
            whole(cosine.shape),
            whole(sine.shape),
            whole((1, rows)),
        ],
        out_specs=[whole(shape), whole((rows, width)), whole((rows, 1)), whole((rows, 1))],
        out_shape=[
            jax.ShapeDtypeStruct(shape, BF16),
            jax.ShapeDtypeStruct((rows, width), BF16),
            jax.ShapeDtypeStruct((rows, 1), F32),
            jax.ShapeDtypeStruct((rows, 1), F32),
        ],
        name="project",
    )(tokens, gain, weight, cosine, sine, ids)


def blocks_of(count):
    return math.gcd(count, 256), math.gcd(count, 512)


def whole(shape):
    return pl.BlockSpec(shape, lambda i, *_: (0,) * len(shape))


def attention_forward(lo, hi, own, oth, rows, groups):
    count = own.shape[1]
    qb, kb = blocks_of(count)
    col = lambda height: pl.BlockSpec((height, qb), lambda i, *_: (0, i))
    return pl.pallas_call(
        functools.partial(forward_kernel, groups=groups, count=count, kb=kb),
        grid_spec=pltpu.PrefetchScalarGridSpec(
            num_scalar_prefetch=2,
            grid=(count // qb,),
            in_specs=[col(HD), whole(own.shape), whole(oth.shape), col(rows.shape[0])],
            out_specs=[col(HD), col(1)],
            scratch_shapes=[pltpu.VMEM((groups * count, 2 * HD), BF16)],
        ),
        out_shape=[
            jax.ShapeDtypeStruct((HD, count), BF16),
            jax.ShapeDtypeStruct((1, count), F32),
        ],
        name="attention_forward",
    )(lo, hi, own, own, oth, rows)


def attention_backward(lo, hi, own, oth, rows, out, do, lse, groups):
    count = own.shape[1]
    qb, kb = blocks_of(count)
    col = lambda height: pl.BlockSpec((height, qb), lambda i, *_: (0, i))
    others = (max(groups - 1, 1), 2 * HD, count)
    return pl.pallas_call(
        functools.partial(backward_kernel, groups=groups, count=count, kb=kb),
        grid_spec=pltpu.PrefetchScalarGridSpec(
            num_scalar_prefetch=2,
            grid=(count // qb,),
            in_specs=[
                col(HD), whole(own.shape), whole(oth.shape), col(rows.shape[0]),
                col(HD), col(HD), col(1),
            ],
            out_specs=[col(HD), whole((2 * HD, count)), whole(others)],
            scratch_shapes=[
                pltpu.VMEM((groups * count, 2 * HD), BF16),
                pltpu.VMEM((groups * count, 2 * HD), F32),
            ],
        ),
        out_shape=[
            jax.ShapeDtypeStruct((HD, count), F32),
            jax.ShapeDtypeStruct((2 * HD, count), F32),
            jax.ShapeDtypeStruct(others, BF16),
        ],
        name="attention_backward",
    )(lo, hi, own, own, oth, rows, out, do, lse)


def layer(
    tokens,
    seq_ids,
    attention_norm_gain,
    qkv_weight,
    out_weight,
    feedforward_norm_gain,
    mlp_in_weight,
    mlp_out_weight,
    grad_out,
    *,
    ctx,
    tp,
):
    tok_rows, width = tokens.shape
    local_cols = qkv_weight.shape[2]
    heads_here = local_cols // HD
    hidden_here = mlp_in_weight.shape[2]
    groups = ctx // heads_here
    part = tok_rows // groups
    count = ctx * part
    me = lax.axis_index("ctx")

    def tp_sum(value):
        value = value.astype(BF16)
        if tp == 2:
            other = lax.ppermute(value, "tp", [(0, 1), (1, 0)])
            return value.astype(F32) + other.astype(F32)
        return lax.psum(value, "tp").astype(F32)

    def to_group(value, r):
        pairs = [(i, i // groups * groups + (i + r) % groups) for i in range(ctx)]
        return lax.ppermute(value, "ctx", pairs)

    def for_heads(value):
        value = jnp.stack(
            [value[:, :, g * part : (g + 1) * part] for g in range(groups)], axis=1
        )
        return value.reshape(ctx, value.shape[2], part)

    def to_heads(chunks):
        value = lax.all_to_all(chunks, "ctx", 0, 0)
        return value.transpose(1, 0, 2).reshape(chunks.shape[1], count)

    def for_tokens(value):
        return value.reshape(value.shape[0], ctx, part).transpose(1, 0, 2)

    def to_tokens(chunks):
        value = lax.all_to_all(chunks, "ctx", 0, 0)
        value = value.reshape(heads_here, groups, chunks.shape[1], part)
        return jnp.concatenate([value[:, g] for g in range(groups)], axis=2)

    bits = list(range(ctx.bit_length() - 1))
    group_bits = list(range(groups.bit_length() - 1))
    head_bits = bits[len(group_bits) :]
    far_bits = bits[2:]

    def spread(bits):
        masks = [
            sum(((m >> at) & 1) << bit for at, bit in enumerate(bits))
            for m in range(1 << len(bits))
        ]
        here = sum((((me >> bit) & 1) << at) for at, bit in enumerate(bits))
        return masks, here

    def pick(pieces, index):
        value = pieces[0]
        for at in range(1, len(pieces)):
            value = jnp.where(index == at, pieces[at], value)
        return value

    def hop(value, mask):
        return lax.ppermute(value, "ctx", [(i, i ^ mask) for i in range(ctx)])

    def deal(value, bits, axis):
        masks, here = spread(bits)
        pieces = jnp.split(value, len(masks), axis=axis)
        return [pick(pieces, here ^ m) for m in range(len(masks))]

    def send_dealt(dealt, bits):
        masks, _ = spread(bits)
        return [dealt[0]] + [hop(dealt[m], masks[m]) for m in range(1, len(masks))]

    def total(pieces):
        return sum(piece.astype(F32) for piece in pieces).astype(BF16)

    def send_all(value, bits):
        masks, _ = spread(bits)
        return [value] + [hop(value, masks[m]) for m in range(1, len(masks))]

    def arrange(pieces, bits, axis):
        _, here = spread(bits)
        return jnp.concatenate(
            [pick(pieces, here ^ at) for at in range(len(pieces))], axis=axis
        )

    def halve(value, bit):
        return send_dealt(deal(value, [bit], 0), [bit])

    def grow(value, bit):
        return send_all(value, [bit])

    def grown(pieces, bit):
        return arrange(pieces, [bit], 0)

    def fence(*values):
        return lax.optimization_barrier(values)

    over_cols = (((1,), (1,)), ((), ()))
    over_rows = (((0,), (0,)), ((), ()))
    across = (((0,), (1,)), ((), ()))

    def dot(left, right, dims=(((1,), (0,)), ((), ()))):
        return lax.dot_general(left, right, dims, preferred_element_type=F32)

    input_tokens = tokens.astype(F32)
    planes = [qkv_weight[:, c] for c in range(3)]
    positions = me * tok_rows + jnp.arange(tok_rows, dtype=jnp.int32)
    cosine, sine = rope_tables_t(positions, HD)
    packed, first, average, attention_inverse_deviation = project(
        tokens,
        attention_norm_gain[None],
        qkv_weight.transpose(1, 0, 2),
        cosine,
        sine,
        seq_ids[None],
        groups,
    )
    own = to_heads(packed.reshape(ctx, 3 * HD + PAD, part))
    if groups > 1:
        oth = jnp.stack([to_group(own[HD:], groups - r) for r in range(1, groups)])
    else:
        oth = own[None, HD:]
    id_own = own[3 * HD]
    id_all = jnp.concatenate([id_own[None], oth[: groups - 1, 2 * HD]], axis=0)
    marks = jnp.arange(SEQS + 1, dtype=F32)
    below = jnp.sum((id_all.astype(F32)[:, None, :] < marks[None, :, None]).astype(jnp.int32), -1)
    first_key = jnp.zeros((groups, count), jnp.int32)
    end_key = jnp.zeros((groups, count), jnp.int32)
    for s in range(SEQS):
        hit = (id_own == s)[None, :]
        first_key = jnp.where(hit, below[:, s : s + 1], first_key)
        end_key = jnp.where(hit, below[:, s + 1 : s + 2], end_key)
    rows = jnp.concatenate([first_key, end_key], axis=0)
    qb, _ = blocks_of(count)
    lo = first_key[:, ::qb].T.reshape(-1)
    hi = end_key[:, qb - 1 :: qb].T.reshape(-1)

    att_head, lse = attention_forward(lo, hi, own, oth, rows, groups)
    attended = to_tokens(for_tokens(att_head)).reshape(local_cols, tok_rows)
    attn_part = dot(attended, out_weight, over_rows)
    residual_middle = input_tokens + tp_sum(attn_part)
    feedforward_standardized, feedforward_inverse_deviation, feedforward_normed_input = (
        layer_normalize(residual_middle, feedforward_norm_gain)
    )
    second = feedforward_normed_input.astype(BF16)
    in_act = mlp_in_weight[:, 0]
    in_gate = mlp_in_weight[:, 1]
    act_in = dot(second, in_act)
    gate = dot(second, in_gate)
    hidden = (gelu_value(act_in) * gate).astype(BF16)
    upstream = grad_out.astype(F32)
    grad_hidden = dot(grad_out, mlp_out_weight, over_cols)
    grad_act = (grad_hidden * gate * gelu_slope(act_in)).astype(BF16)
    grad_gate = (grad_hidden * gelu_value(act_in)).astype(BF16)
    second_part = dot(grad_act, in_act, over_cols) + dot(grad_gate, in_gate, over_cols)
    second_part, second_w, act_w, gate_w, hidden_w = fence(
        second_part.astype(BF16), second, grad_act, grad_gate, hidden
    )
    feedforward_norm_gradient = tp_sum(second_part)
    grad_w = [
        dot(left, right, over_rows).astype(BF16)
        for left, right in ((hidden_w, grad_out), (act_w, second_w), (gate_w, second_w))
    ]
    feedforward_norm_gradient, *grad_w = fence(feedforward_norm_gradient, *grad_w)
    sum_w = lax.psum(tuple(grad_w), "ctx")
    feedforward_normed_gradient, feedforward_gain_gradient = layer_normalize_backward(
        feedforward_norm_gradient,
        feedforward_standardized,
        feedforward_inverse_deviation,
        feedforward_norm_gain,
    )
    grad_mid = upstream + feedforward_normed_gradient
    grad_mid_b = grad_mid.astype(BF16)
    grad_att = dot(out_weight, grad_mid_b, over_cols).astype(BF16)
    chunks = for_heads(grad_att.reshape(heads_here, HD, tok_rows))
    chunks, late_mid, late_hidden = fence(chunks, grad_mid_b, hidden_w)
    do_head = to_heads(chunks)

    wide = width // local_cols
    grad_w_attn = [
        dot(attended, late_mid[:, at * local_cols : (at + 1) * local_cols]).astype(BF16)
        for at in range(wide)
    ]
    ffn_part = dot(late_hidden, mlp_out_weight).astype(BF16)
    do_head, ffn_part, *grad_w_attn = fence(do_head, ffn_part, *grad_w_attn)

    output_sum = tp_sum(ffn_part)
    dq, dkv, dkv_oth = attention_backward(
        lo, hi, own, oth, rows, att_head, do_head, lse, groups
    )
    dq, dkv, dkv_oth, output_sum = fence(dq, dkv, dkv_oth, output_sum)
    for r in range(1, groups):
        dkv = dkv + to_group(dkv_oth[r - 1], r).astype(F32)
    place = me % groups
    spots = (
        jnp.arange(ctx, dtype=jnp.int32)[:, None] * tok_rows
        + place * part
        + jnp.arange(part, dtype=jnp.int32)[None, :]
    ).reshape(-1)
    cosine_head, sine_head = rope_tables_t(spots, HD)
    grads = jnp.concatenate(
        [
            unrotate_t(dq[None], cosine_head, sine_head)[0].astype(BF16),
            unrotate_t(dkv[None, :HD], cosine_head, sine_head)[0].astype(BF16),
            dkv[HD:].astype(BF16),
        ],
        axis=0,
    )
    chunks = for_tokens(grads)
    grad_proj = to_tokens(chunks)
    output = (residual_middle + output_sum).astype(BF16)
    grad_proj, output = fence(grad_proj, output)
    grad_planes = [
        grad_proj[:, c * HD : (c + 1) * HD].reshape(local_cols, tok_rows) for c in range(3)
    ]

    bundle = jnp.concatenate(
        [dot(first, plane, (((0,), (1,)), ((), ()))).astype(BF16) for plane in grad_planes]
        + grad_w_attn,
        axis=0,
    )
    first_send = deal(bundle, bits[:1], 0)
    *grad_planes, kept, send = fence(*grad_planes, *first_send)
    first_part = dot(grad_planes[0], planes[0], across) + dot(grad_planes[1], planes[1], across)
    first_part, *bundle = fence(first_part, *send_dealt([kept, send], bits[:1]))
    one, two = jnp.split(total(bundle), 2)
    order_one = bits[1:]
    order_two = bits[2:3] + bits[1:2] + bits[3:]
    one, two = deal(one, order_one[:1], 0), deal(two, order_two[:1], 0)
    last_plane, *both = fence(grad_planes[2], *one, *two)
    one, two = send_dealt(both[:2], order_one[:1]), send_dealt(both[2:], order_two[:1])
    first_part = (first_part + dot(last_plane, planes[2], across)).astype(BF16)
    attention_norm_gradient = tp_sum(first_part)
    one, two = total(one), total(two)
    for bit_one, bit_two in zip(order_one[1:-1], order_two[1:-1]):
        both = fence(*halve(one, bit_one), *halve(two, bit_two))
        one, two = total(both[:2]), total(both[2:])
    attention_standardized = (input_tokens - average) * attention_inverse_deviation
    attention_normed_gradient, attention_gain_gradient = layer_normalize_backward(
        attention_norm_gradient,
        attention_standardized,
        attention_inverse_deviation,
        attention_norm_gain,
    )
    grad_tokens = grad_mid + attention_normed_gradient
    lanes = one.shape[1]
    gains = jnp.stack([attention_gain_gradient, feedforward_gain_gradient]).reshape(-1, lanes)
    many = gains.shape[0]
    gains = jnp.pad(gains, ((0, -many % 16), (0, 0))).astype(BF16)

    def riding(send, bit, gains):
        came = hop(jnp.concatenate([send, gains], axis=0), 1 << bit)
        return came[: send.shape[0]], total([gains, came[send.shape[0] :]])

    both = jnp.concatenate([one, two], axis=0)
    came, gains = riding(both, order_one[-1], gains)
    both, came, gains, grad_tokens = fence(both, came, gains, grad_tokens)
    one, two = jnp.split(total([both, came]), 2)
    for bit_one, bit_two in zip(reversed(order_one[:-1]), reversed(order_two[:-1])):
        came, gains = riding(one, bit_one, gains)
        came, gains, *both = fence(came, gains, *grow(two, bit_two))
        one, two = grown([one, came], bit_one), grown(both, bit_two)
    kept = jnp.concatenate([one, two], axis=0)
    came, gains = riding(kept, bits[0], gains)
    bundle = grown([kept, came], bits[0])
    gains = gains[:many].astype(F32).reshape(2, width)
    sum_qkv = bundle[: 3 * width].reshape(3, width, local_cols).transpose(1, 0, 2).astype(F32)
    sum_attn = jnp.concatenate(
        [
            bundle[3 * width + at * local_cols : 3 * width + (at + 1) * local_cols]
            for at in range(wide)
        ],
        axis=1,
    ).astype(F32)
    *sum_w, sum_qkv, sum_attn = fence(*sum_w, sum_qkv, sum_attn)
    return (
        output,
        grad_tokens,
        gains[0],
        sum_qkv,
        sum_attn,
        gains[1],
        jnp.stack(sum_w[1:]).transpose(2, 0, 1).astype(F32),
        sum_w[0].astype(F32),
    )


def solution(mesh):
    return jax.shard_map(
        functools.partial(layer, ctx=mesh.shape["ctx"], tp=mesh.shape["tp"]),
        mesh=mesh,
        in_specs=(
            P("ctx", None),
            P("ctx"),
            P(),
            P(None, None, "tp"),
            P("tp", None),
            P(),
            P(None, None, "tp"),
            P("tp", None),
            P("ctx", None),
        ),
        out_specs=(
            P("ctx", None),
            P("ctx", None),
            P(),
            P(None, None, "tp"),
            P("tp", None),
            P(),
            P(None, None, "tp"),
            P("tp", None),
        ),
        check_vma=False,
    )
```
